32 devices in a mesh: sph: 8 (over z, core), fit: 4 (over y, x).
Axes of the slice: x: 2, y: 2, z: 4, core: 2. Of those that a mesh axis runs over, the one named last changes fastest.
Arguments:
- tiles: bfloat16 [1024, 163840], P('fit', 'sph'), may hold values from -0.1875 to 0.1875
- coefs: bfloat16 [16, 1024], P(None, 'fit'), may hold values from -6 to 6
- centres: float32 [3, 512], P(None, ('sph', 'fit'))
- radii: float32 [512], P(('sph', 'fit')), may hold values from 1 to 1.6
- neighbours: int32 [512, 16], P(('sph', 'fit')), may hold values from 0 to 511, as said below
- counts: int32 [512], P(('sph', 'fit')), may hold values from 1 to 16
Outputs:
- moments: float32 [512, 16, 49], P(('sph', 'fit'))
- fock: float32 [16, 1024], P(None, 'fit')
The draws below stay inside these ranges and needn't reach their ends.
Inputs may be any that keep to these rules, and one draw needn't show every extreme that they name: `neighbours`: every entry j of row i satisfies |j - i| <= 8; the first counts[i] entries of a row are distinct and differ from i, the rest equal i.
All inputs are finite; a program needn't handle non-finite values.
Results may differ from the reference program's by a relative error of at most 0.00086.
Values may be sent and summed in bfloat16 or wider, within the bound.
No kernel may reach another device: no remote copies, remote signals or barrier semaphores. Data moves between devices by JAX's collectives and lax.ppermute only.
A program may use at most 192 MiB of HBM per device.

```python
import math
import jax
import jax.numpy as jnp
from jax import lax

SPH_DEV = 16
REACH = 8
SLOTS = 16
DEGREE = 6
LM = 49
NTH = 16
NPHI = 20
NG = 320
NDENS = 16
AUX = 1024
NSPH = 512


def draw_centres(key, part):
    index = jnp.arange(NSPH).astype(jnp.float32)
    jitter = jax.random.uniform(key, (3, NSPH), jnp.float32, -0.1, 0.1)
    base = jnp.stack([0.5 * jnp.cos(0.9 * index), 0.5 * jnp.sin(0.9 * index), 0.3 * index])
    return base + jitter


def neighbour_plan(key):
    key = jax.random.fold_in(key, 7)
    first, second, third = jax.random.split(key, 3)
    cand = jnp.concatenate([jnp.arange(-REACH, 0), jnp.arange(1, REACH + 1)]).astype(jnp.int32)
    scores = jax.random.randint(first, (NSPH, SLOTS), 0, 1 << 20) * SLOTS + jnp.arange(SLOTS)[None, :]
    harmonic_order = jnp.argsort(scores, axis=1, stable=True)
    offsets = cand[harmonic_order]
    rows = jnp.arange(NSPH).astype(jnp.int32)[:, None]
    ids = rows + offsets
    outside = ((ids < 0) | (ids >= NSPH)).astype(jnp.int32)
    order_two = jnp.argsort(outside * SLOTS + jnp.arange(SLOTS)[None, :], axis=1, stable=True)
    ids = jnp.take_along_axis(ids, order_two, axis=1)
    inside = SLOTS - jnp.sum(outside, axis=1)
    blocks = NSPH // SPH_DEV
    harmonic_degree = jax.random.randint(second, (blocks,), 2, SLOTS + 1)
    harmonic_degree = harmonic_degree.at[0].set(SLOTS)
    per_sphere = jnp.repeat(harmonic_degree, SPH_DEV)
    wanted = jax.random.randint(third, (NSPH,), 1, SLOTS + 1)
    pick = jnp.where(jnp.arange(NSPH) % SPH_DEV == REACH, per_sphere, jnp.minimum(wanted, per_sphere))
    total = jnp.minimum(pick, inside).astype(jnp.int32)
    slots = jnp.arange(SLOTS)[None, :]
    ids = jnp.where(slots < total[:, None], ids, rows).astype(jnp.int32)
    return (ids, total)


def draw_neighbours(key, part):
    ids, total = neighbour_plan(key)
    return ids


def draw_counts(key, part):
    ids, total = neighbour_plan(key)
    return total


def shard_levels(stream_key, dims, pieces, low, high):
    loudness, own = 1.0, jax.random.fold_in(stream_key, 6)
    for dim, parts in pieces:
        draws = jnp.exp(jax.random.uniform(jax.random.fold_in(own, dim), (parts,), jnp.float32, low / len(pieces), high / len(pieces)))
        loudness = loudness * jnp.repeat(draws, dims[dim] // parts).reshape([-1 if axis == dim else 1 for axis in range(len(dims))])
    return loudness


def bell_draw(own_key, extent, width, most, pieces=(), held_as=jnp.bfloat16):
    factor_of = shard_levels(own_key, extent, pieces, -0.22, 0.18) if pieces else 1.0
    values = jax.random.normal(own_key, extent, jnp.float32) * width * factor_of
    return jnp.minimum(jnp.maximum(values, -most), most).astype(held_as)


def setup_inputs(seed: int = 0) -> dict:
    splits = jax.random.split(jax.random.key(seed), 7)
    return {
        "tiles": bell_draw(splits[0], (AUX, NSPH * NG), AUX ** -0.5, 0.1875, ((0, 4), (1, 8))),
        "coefs": bell_draw(splits[1], (NDENS, AUX), 1.0, 6.0, ((1, 4),)),
        "centres": draw_centres(jax.random.fold_in(splits[6], 71), 0),
        "radii": jnp.clip(jnp.exp(math.log(1.6) - 0.47000364 * jax.random.uniform(splits[3], (NSPH,), jnp.float32) ** shard_levels(splits[3], (NSPH,), ((0, 32),), -0.2, 0.2)), 1.0, 1.6),
        "neighbours": draw_neighbours(jax.random.fold_in(splits[6], 71), 0),
        "counts": draw_counts(jax.random.fold_in(splits[6], 71), 0),
    }


band = 0.1

def solid(coord_x, coord_y, coord_z):
    radius_squared = coord_x * coord_x + coord_y * coord_y + coord_z * coord_z
    cos_part = [jnp.ones_like(coord_x)]
    sin_part = [jnp.zeros_like(coord_x)]
    for harmonic_order in range(1, DEGREE + 1):
        cprev = cos_part[-1]
        sprev = sin_part[-1]
        cos_part.append(cprev * coord_x - sprev * coord_y)
        sin_part.append(cprev * coord_y + sprev * coord_x)
    result = [None] * (DEGREE + 1) ** 2
    for harmonic_order in range(DEGREE + 1):
        dfact = 1.0
        for odd in range(1, 2 * harmonic_order, 2):
            dfact = dfact * odd
        lower_term = None
        current = dfact * jnp.ones_like(coord_x)
        for harmonic_degree in range(harmonic_order, DEGREE + 1):
            if harmonic_degree > harmonic_order:
                next_term = (2 * harmonic_degree - 1) * coord_z * current
                if lower_term is not None:
                    next_term = next_term - (harmonic_degree + harmonic_order - 1) * radius_squared * lower_term
                lower_term = current
                current = next_term / (harmonic_degree - harmonic_order)
            scale = math.sqrt((2 * harmonic_degree + 1) / (4 * math.pi) * math.factorial(harmonic_degree - harmonic_order) / math.factorial(harmonic_degree + harmonic_order))
            if harmonic_order == 0:
                result[harmonic_degree * harmonic_degree + harmonic_degree] = scale * current
            else:
                result[harmonic_degree * harmonic_degree + harmonic_degree + harmonic_order] = math.sqrt(2.0) * scale * current * cos_part[harmonic_order]
                result[harmonic_degree * harmonic_degree + harmonic_degree - harmonic_order] = math.sqrt(2.0) * scale * current * sin_part[harmonic_order]
    return result

def grid_tables():
    polar_index = jnp.arange(NTH, dtype=jnp.float32)
    polar_nodes = -1.0 + (2.0 * polar_index + 1.0) / NTH
    angles = (jnp.arange(NPHI, dtype=jnp.float32) + 0.5) * (2.0 * math.pi / NPHI)
    cosines = jnp.repeat(polar_nodes, NPHI)
    sines = jnp.sqrt(1.0 - cosines * cosines)
    azimuth = jnp.tile(angles, NTH)
    dirs = jnp.stack([sines * jnp.cos(azimuth), sines * jnp.sin(azimuth), cosines])
    weights = jnp.full((NTH * NPHI,), 4.0 * math.pi / (NTH * NPHI), dtype=jnp.float32)
    ysurf = jnp.stack(solid(dirs[0], dirs[1], dirs[2]))
    levels = jnp.asarray([float(harmonic_degree) for harmonic_degree in range(DEGREE + 1) for harmonic_order in range(2 * harmonic_degree + 1)], dtype=jnp.float32)
    couple = 4.0 * math.pi / (2.0 * levels + 1.0)
    invert = (2.0 * levels + 1.0) / (4.0 * math.pi)
    return (dirs, weights, ysurf, couple, invert)

def block_basis(own, near, valid, dirs, couple):
    centre = own[:3]
    radius = own[3]
    offset = centre[:, :, None] - near[:3]
    near_rad = jnp.where(valid > 0, near[3], 1.0)
    vec = (offset[:, :, :, None] + radius[None, :, None, None] * dirs[:, None, None, :]) / near_rad[None, :, :, None]
    dist = jnp.sqrt(lax.optimization_barrier(jnp.sum(vec * vec, axis=0)))
    ramp = jnp.clip((1.0 - dist) / band, 0.0, 1.0)
    switch = ramp * ramp * (3.0 - 2.0 * ramp) * valid[:, :, None]
    harm = jnp.stack(solid(vec[0], vec[1], vec[2]), axis=2)
    basis = harm * couple[None, None, :, None] * switch[:, :, None, :]
    uncovered = jnp.maximum(0.0, 1.0 - lax.optimization_barrier(jnp.sum(switch, axis=1)))
    return (basis, uncovered)

def block_rhs(weighted, uncovered, potential):
    return -jnp.einsum('lp,sdp->sdl', weighted, uncovered[:, None, :] * potential, precision=lax.Precision.HIGHEST)

def block_sweep(basis, weighted, invert, rhs, near_moments):
    field = jnp.einsum('sklp,skdl->sdp', basis, near_moments, precision=lax.Precision.HIGHEST)
    proj = jnp.einsum('lp,sdp->sdl', weighted, field, precision=lax.Precision.HIGHEST)
    return invert[None, None, :] * (rhs + proj)

def block_charges(ysurf, weights, uncovered, moments):
    surface = jnp.einsum('lp,sdl->sdp', ysurf, moments, precision=lax.Precision.HIGHEST)
    return (surface * (weights[None, None, :] * uncovered[:, None, :])).astype(jnp.bfloat16)

def reference(tiles, coefs, centres, radii, neighbours, counts):
    dirs, weights, ysurf, couple, invert = grid_tables()
    weighted = ysurf * weights[None, :]
    geometry = jnp.concatenate([centres, radii[None, :]], axis=0)
    blocks = NSPH // SPH_DEV
    flat_phi = jnp.dot(coefs, tiles, preferred_element_type=jnp.float32)
    phi = jnp.transpose(flat_phi.reshape(NDENS, NSPH, NG), (1, 0, 2))
    nbr_b = neighbours.reshape(blocks, SPH_DEV, SLOTS)
    valid_b = (jnp.arange(SLOTS)[None, None, :] < counts.reshape(blocks, SPH_DEV, 1)).astype(jnp.float32)
    own_b = jnp.transpose(geometry.reshape(4, blocks, SPH_DEV), (1, 0, 2))
    phi_b = phi.reshape(blocks, SPH_DEV, NDENS, NG)

    def start(items):
        own, near_idx, valid, potential = items
        basis, uncovered = block_basis(own, geometry[:, near_idx], valid, dirs, couple)
        return (block_rhs(weighted, uncovered, potential), uncovered)
    rhs, uncovered = lax.map(start, (own_b, nbr_b, valid_b, phi_b))
    state = invert[None, None, None, :] * rhs
    for sweep in range(2):
        flat = state.reshape(NSPH, NDENS, LM)

        def relax(items):
            own, near_idx, valid, right = items
            basis, unused = block_basis(own, geometry[:, near_idx], valid, dirs, couple)
            return block_sweep(basis, weighted, invert, right, flat[near_idx])
        state = lax.map(relax, (own_b, nbr_b, valid_b, rhs))
    moments = state.reshape(NSPH, NDENS, LM)
    charges = block_charges(ysurf, weights, uncovered.reshape(NSPH, NG), moments)
    tiles3 = tiles.reshape(AUX, NSPH, NG)
    fock = lax.dot_general(charges, tiles3, (((0, 2), (1, 2)), ((), ())), preferred_element_type=jnp.float32)
    return (moments, fock)
```

```python
import functools
import math

import jax
import jax.numpy as jnp
import ml_dtypes
import numpy as np
from jax import lax
from jax.experimental import pallas as pl
from jax.experimental.pallas import tpu as pltpu
from jax.sharding import PartitionSpec as P

DEGREE = 6
LM = 49
NTH = 16
NPHI = 20
NG = 320
NDENS = 16
LP = 64
QUAD = 4
QN = QUAD * NG
BAND = 0.1
BF = jnp.bfloat16
F32 = jnp.float32


def gam(l, m):
    return (l + m - 1) * (l - 1 - m) / ((2 * l - 1) * (2 * l - 3))


def tables():
    c = -1.0 + (2.0 * np.arange(NTH) + 1.0) / NTH
    f = (np.arange(NPHI) + 0.5) * (2 * np.pi / NPHI)
    z = np.repeat(c, NPHI)
    s = np.sqrt(1 - z * z)
    az = np.tile(f, NTH)
    x, y = s * np.cos(az), s * np.sin(az)
    cos, sin = [np.ones_like(x)], [np.zeros_like(x)]
    for m in range(1, DEGREE + 1):
        cos.append(cos[m - 1] * x - sin[m - 1] * y)
        sin.append(cos[m - 1] * y + sin[m - 1] * x)
    ys, scale, invert = np.zeros((LM, NG)), np.zeros(LM), np.zeros(LM)
    for m in range(DEGREE + 1):
        q, lead = {m: np.ones_like(x)}, {m: 1.0}
        for odd in range(1, 2 * m, 2):
            lead[m] *= odd
        for l in range(m + 1, DEGREE + 1):
            q[l] = z * q[l - 1] - (gam(l, m) * q[l - 2] if l > m + 1 else 0.0)
            lead[l] = lead[l - 1] * (2 * l - 1) / (l - m)
        for l in range(m, DEGREE + 1):
            n = math.sqrt(
                (2 * l + 1) / (4 * math.pi) * math.factorial(l - m) / math.factorial(l + m)
            )
            n *= math.sqrt(2.0) if m else 1.0
            for sign, trig in ((1, cos[m]), (-1, sin[m])):
                if m == 0 and sign < 0:
                    continue
                i = l * l + l + sign * m
                ys[i] = n * lead[l] * q[l] * trig
                scale[i] = n * lead[l] * 4 * math.pi / (2 * l + 1)
                invert[i] = (2 * l + 1) / (4 * math.pi)
    return np.stack([x, y, z]), ys, scale, invert


def split(a):
    a = np.asarray(a, np.float32)
    hi = a.astype(ml_dtypes.bfloat16)
    return hi, (a - hi.astype(np.float32)).astype(ml_dtypes.bfloat16)


def halves(x):
    hi = x.astype(BF)
    return hi, (x - hi.astype(F32)).astype(BF)


def pair_weights():
    dirs, ys, _, _ = tables()
    w = np.zeros((2 * NG, 2 * LP))
    wy = ys.T * (4 * math.pi / NG)
    w[:NG, :LM] = wy
    w[NG:, LP : LP + LM] = wy
    d = np.zeros((8, 2 * NG), np.float32)
    d[:3, :NG] = dirs
    d[:3, NG:] = dirs
    return np.concatenate(split(w), 1), d


def quad_weights():
    _, ys, _, _ = tables()
    w = np.zeros((QN, QUAD * LP))
    for j in range(QUAD):
        w[j * NG : (j + 1) * NG, j * LP : j * LP + LM] = ys.T
    return split(w)


def lane_scales():
    _, _, scale, invert = tables()
    rows = np.zeros((8, 2 * LP), np.float32)
    for h in (0, LP):
        rows[0, h : h + LM] = scale * invert
        rows[1, h : h + LM] = invert
    return rows


def phi_kernel(chunk_ref, coef_ref, tile_ref, out_ref):
    out_ref[...] = jnp.dot(coef_ref[...], tile_ref[...], preferred_element_type=F32)


def phi_call(chunk, coefs, tiles, width):
    aux = tiles.shape[0]
    steps = 2
    wide = width // steps
    return pl.pallas_call(
        phi_kernel,
        grid_spec=pltpu.PrefetchScalarGridSpec(
            num_scalar_prefetch=1,
            grid=(steps,),
            in_specs=[
                pl.BlockSpec((NDENS, aux), lambda b, c: (0, 0)),
                pl.BlockSpec((aux, wide), lambda b, c: (0, c[0] * steps + b)),
            ],
            out_specs=pl.BlockSpec((NDENS, wide), lambda b, c: (0, b)),
        ),
        out_shape=jax.ShapeDtypeStruct((NDENS, width), F32),
        cost_estimate=pl.CostEstimate(
            flops=2 * NDENS * aux * width,
            bytes_accessed=2 * aux * width + 4 * NDENS * width,
            transcendentals=0,
        ),
        name="phi",
    )(chunk, coefs, tiles)


def pair_build(e, geo, mask, dir_ref, bh):
    lane = lax.broadcasted_iota(jnp.int32, (8, 128), 1)
    sub = lax.broadcasted_iota(jnp.int32, (8, 128), 0)
    own = jnp.broadcast_to(geo[pl.ds(e + 8, 1), :], (8, 128))
    mrow = jnp.broadcast_to(mask[pl.ds(e, 1), :], (8, 128))
    cols = []
    for g, start in ((0, e), (1, e + 9)):
        near = geo[pl.ds(start, 8), :]
        valid = jnp.sum(jnp.where(lane == sub + 8 * g, mrow, 0.0), axis=1, keepdims=True)
        on = valid > 0.0
        ir = 1.0 / jnp.where(on, near[:, 3:4], 1.0)
        off = jnp.where(on, own - near, 0.0)
        c = [off[:, 0:1] * ir, off[:, 1:2] * ir, off[:, 2:3] * ir, own[:, 3:4] * ir, valid]
        cols.append([jnp.broadcast_to(q, (8, 128)) for q in c])
    mid = [jnp.where(lane < 64, a, b) for a, b in zip(*cols)]
    sums = []
    for t in range(5):
        ox, oy, oz, q, valid = cols[0] if t < 2 else (mid if t == 2 else cols[1])
        ls = slice(128 * t, 128 * t + 128)
        x = ox + q * dir_ref[0:1, ls]
        y = oy + q * dir_ref[1:2, ls]
        z = oz + q * dir_ref[2:3, ls]
        r2 = x * x + y * y + z * z
        ramp = jnp.clip((1.0 - jnp.sqrt(r2)) * (1.0 / BAND), 0.0, 1.0)
        chi = ramp * ramp * (3.0 - 2.0 * ramp) * valid
        sums.append(jnp.sum(chi, axis=0, keepdims=True))
        cos, sin = [chi, chi * x], [None, chi * y]
        for m in range(2, DEGREE + 1):
            cos.append(cos[m - 1] * x - sin[m - 1] * y)
            sin.append(cos[m - 1] * y + sin[m - 1] * x)
        out = [None] * LM
        for m in range(DEGREE + 1):
            qm = {}
            for l in range(m, DEGREE + 1):
                if l == m + 1:
                    qm[l] = z
                elif l == m + 2:
                    qm[l] = z * z - gam(l, m) * r2
                elif l > m + 2:
                    qm[l] = z * qm[l - 1] - (gam(l, m) * r2) * qm[l - 2]
                for sign, trig in ((1, cos[m]), (-1, sin[m])):
                    if m == 0 and sign < 0:
                        continue
                    out[l * l + l + sign * m] = trig if l == m else trig * qm[l]
        out.append(jnp.zeros((8, 128), F32))
        for p in range(25):
            both = jnp.concatenate([out[2 * p], out[2 * p + 1]], axis=0)
            bh[16 * p : 16 * p + 16, ls] = both.astype(BF)
    return sums


def pair_finish(u, w_ref, t_ref, bh):
    r = jnp.dot(bh[...], w_ref[...], preferred_element_type=F32)
    tt = r[: LM * 8, : 2 * LP] + r[: LM * 8, 2 * LP :]
    a = jnp.swapaxes(tt.reshape(LM, 8, 2 * LP), 0, 1)
    a = jnp.concatenate([a, jnp.zeros((8, LP - LM, 2 * LP), F32)], 1).reshape(8 * LP, 2 * LP)
    hi, lo = halves(a)
    t_ref[u, :, : 2 * LP] = hi
    t_ref[u, :, 2 * LP :] = lo


def uncover(sums):
    low = lax.broadcasted_iota(jnp.int32, (1, 128), 1) < 64
    swap = lambda v: pltpu.roll(v, 64, 1)
    three = []
    for s in sums:
        r2, r3, r4 = swap(s[2]), swap(s[3]), swap(s[4])
        three.append([s[0] + jnp.where(low, r2, r3), s[1] + jnp.where(low, r3, r4), s[2] + r4])
    a, b = three
    b0, b1, b2 = swap(b[0]), swap(b[1]), swap(b[2])
    tiles = [a[0], a[1], jnp.where(low, a[2], b0), jnp.where(low, b0, b1), jnp.where(low, b1, b2)]
    return [jnp.maximum(0.0, 1.0 - t) for t in tiles]


def pair_kernel(
    first_ref, before_ref, own_ref, after_ref, nbr_ref, cnt_ref, dir_ref, w_ref,
    t_ref, unc_ref, geo, mask, *bhs
):
    spheres, slots = nbr_ref.shape
    reach = slots // 2
    step = pl.program_id(0)

    @pl.when(step == 0)
    def _():
        geo[...] = jnp.zeros_like(geo)
        geo[0:reach, 0:4] = before_ref[...]
        geo[reach : reach + spheres, 0:4] = own_ref[...]
        geo[reach + spheres :, 0:4] = after_ref[...]
        rel = nbr_ref[...] - first_ref[0]
        rel = rel - lax.broadcasted_iota(jnp.int32, (spheres, slots), 0)
        slot = lax.broadcasted_iota(jnp.int32, (spheres, slots), 1)
        listed = slot < jnp.broadcast_to(cnt_ref[...], (spheres, slots))
        lane = lax.broadcasted_iota(jnp.int32, (spheres, 128), 1)
        found = jnp.zeros((spheres, 128), F32)
        for c in range(slots):
            gap = c - reach if c < reach else c - reach + 1
            hit = jnp.where(listed & (rel == gap), 1.0, 0.0)
            hit = jnp.max(hit, axis=1, keepdims=True)
            found = jnp.where(lane == c, hit, found)
        mask[...] = found

    sums = []
    for u in range(QUAD):
        sums.append(pair_build(step * QUAD + u, geo, mask, dir_ref, bhs[u]))
        pair_finish(u, w_ref, t_ref, bhs[u])
    tiles = uncover(sums[:2]) + uncover(sums[2:])
    for t, v in enumerate(tiles):
        unc_ref[0, :, 128 * t : 128 * t + 128] = v


def pair_call(first, before, own, after, neighbours, counts):
    spheres, slots = neighbours.shape
    reach = slots // 2
    w, d = pair_weights()
    whole = lambda *shape: pl.BlockSpec(shape, lambda e, f: (0,) * len(shape))
    return pl.pallas_call(
        pair_kernel,
        grid_spec=pltpu.PrefetchScalarGridSpec(
            num_scalar_prefetch=1,
            grid=(spheres // QUAD,),
            in_specs=[
                whole(reach, 4),
                whole(spheres, 4),
                whole(reach, 4),
                whole(spheres, slots),
                whole(spheres, 1),
                whole(8, 2 * NG),
                whole(2 * NG, 4 * LP),
            ],
            out_specs=[
                pl.BlockSpec((QUAD, 8 * LP, 4 * LP), lambda e, f: (e, 0, 0)),
                pl.BlockSpec((1, 1, QN), lambda e, f: (e, 0, 0)),
            ],
            scratch_shapes=[
                pltpu.VMEM((spheres + 2 * reach, 128), F32),
                pltpu.VMEM((spheres, 128), F32),
            ]
            + [pltpu.VMEM((400, 2 * NG), BF)] * QUAD,
        ),
        out_shape=[
            jax.ShapeDtypeStruct((spheres, 8 * LP, 4 * LP), BF),
            jax.ShapeDtypeStruct((spheres // QUAD, 1, QN), F32),
        ],
        cost_estimate=pl.CostEstimate(
            flops=spheres * 2 * 400 * 640 * 256, bytes_accessed=spheres * 262144, transcendentals=0
        ),
        name="pairs",
    )(first, before, own, after, neighbours, counts, jnp.asarray(d), jnp.asarray(w))


def rhs_kernel(count, *refs):
    phis, (unc_ref, wh_ref, wl_ref, left_ref, right_ref) = refs[:count], refs[count:]
    quads = unc_ref.shape[0]
    rows = []
    for b in range(quads):
        ls = slice(b * QN, (b + 1) * QN)
        total = phis[0][:, ls]
        for p in phis[1:]:
            total = total + p[:, ls]
        rows.append(total * unc_ref[b])
    hi, lo = halves(jnp.concatenate(rows, 0))
    out = jnp.dot(hi, wh_ref[...], preferred_element_type=F32)
    out = out + jnp.dot(lo, wh_ref[...], preferred_element_type=F32)
    out = out + jnp.dot(hi, wl_ref[...], preferred_element_type=F32)
    out = out * (-4.0 * math.pi / NG)
    for b in range(quads):
        ref, at = (left_ref, b) if b < quads // 2 else (right_ref, b - quads // 2)
        ref[:, at * QUAD * LP : (at + 1) * QUAD * LP] = out[b * NDENS : (b + 1) * NDENS]


def rhs_call(phis, unc, wh, wl):
    half = unc.shape[0] // 2 * QUAD * LP
    return pl.pallas_call(
        functools.partial(rhs_kernel, len(phis)),
        out_shape=[jax.ShapeDtypeStruct((NDENS, half), F32)] * 2,
        cost_estimate=pl.CostEstimate(
            flops=6 * NDENS * unc.shape[0] * QN * 256, bytes_accessed=2700000, transcendentals=0
        ),
        name="rhs",
    )(*phis, unc, wh, wl)


def gather_field(t_ref, x, xs, e):
    low = lax.broadcasted_iota(jnp.int32, (NDENS, 128), 1) < LP
    parts = []
    for odd in (0, 1):
        i = e + odd
        below, above = (x, xs) if odd == 0 else (xs, x)
        lo_at = e * LP
        up_at = (e + 8) * LP if odd == 0 else (e + 10) * LP
        lhs = jnp.concatenate(
            [below[:, lo_at : lo_at + 8 * LP], above[:, up_at : up_at + 8 * LP]], 0
        )
        r = jnp.dot(lhs, t_ref[i], preferred_element_type=F32)
        n = NDENS
        a = r[0:n, : 2 * LP] + r[n : 2 * n, : 2 * LP] + r[0:n, 2 * LP :]
        b = r[2 * n : 3 * n, : 2 * LP] + r[3 * n :, : 2 * LP] + r[2 * n : 3 * n, 2 * LP :]
        parts.append((a, b))
    (a0, b0), (a1, b1) = parts
    return jnp.where(low, a0, b1) + pltpu.roll(jnp.where(low, a1, b0), LP, 1)


def sweep_kernel(
    spheres, before_ref, left_ref, right_ref, after_ref, t_ref, rl_ref, rr_ref, sc_ref,
    *rest
):
    x, xs = rest[-2:]
    half = left_ref.shape[1]
    at = 0
    for ref in (before_ref, left_ref, right_ref, after_ref):
        wide = ref.shape[1]
        for t in range(wide // 128):
            hi, lo = halves(ref[:, 128 * t : 128 * t + 128] * sc_ref[0:1, :])
            x[0:NDENS, at : at + 128] = hi
            x[NDENS:, at : at + 128] = lo
            at += 128
    total = at
    v = x[...].astype(F32)
    xs[...] = jnp.concatenate([v[:, LP:], v[:, :LP]], 1).astype(BF)
    for e in range(0, spheres, 2):
        got = gather_field(t_ref, x, xs, e)
        ls = slice(e * LP, e * LP + 128)
        if e * LP < half:
            src, ls_in = rl_ref, ls
        else:
            src, ls_in = rr_ref, slice(e * LP - half, e * LP - half + 128)
        new = src[:, ls_in] + got
        if len(rest) == 4:
            (rest[0] if e * LP < half else rest[1])[:, ls_in] = new
        else:
            rest[0][:, ls] = new * sc_ref[1:2, :]


def sweep_call(before, left, right, after, t, rl, rr, scales, last):
    spheres = t.shape[0]
    half = left.shape[1]
    if last:
        outs = [jax.ShapeDtypeStruct((NDENS, spheres * LP), F32)]
    else:
        outs = [jax.ShapeDtypeStruct((NDENS, half), F32)] * 2
    total = before.shape[1] + 2 * half + after.shape[1]
    return pl.pallas_call(
        functools.partial(sweep_kernel, spheres),
        out_shape=outs,
        scratch_shapes=[pltpu.VMEM((2 * NDENS, total), BF)] * 2,
        cost_estimate=pl.CostEstimate(
            flops=spheres * 2 * 64 * 512 * 256, bytes_accessed=spheres * 262144, transcendentals=0
        ),
        name="sweep",
    )(before, left, right, after, t, rl, rr, scales)


def charge_kernel(m_ref, unc_ref, yh_ref, yl_ref, out_ref):
    quads = unc_ref.shape[0]
    wide = QUAD * LP
    hi, lo = halves(jnp.concatenate([m_ref[:, b * wide : (b + 1) * wide] for b in range(quads)], 0))
    dims = (((1,), (1,)), ((), ()))
    out = lax.dot_general(hi, yh_ref[...], dims, preferred_element_type=F32)
    out = out + lax.dot_general(lo, yh_ref[...], dims, preferred_element_type=F32)
    out = out + lax.dot_general(hi, yl_ref[...], dims, preferred_element_type=F32)
    for b in range(quads):
        weight = unc_ref[b] * (4.0 * math.pi / NG)
        out_ref[:, b * QN : (b + 1) * QN] = (out[b * NDENS : (b + 1) * NDENS] * weight).astype(BF)


def charge_call(moments, unc, wh, wl):
    return pl.pallas_call(
        charge_kernel,
        out_shape=jax.ShapeDtypeStruct((NDENS, unc.shape[0] * QN), BF),
        cost_estimate=pl.CostEstimate(
            flops=6 * NDENS * unc.shape[0] * QN * 256, bytes_accessed=1500000, transcendentals=0
        ),
        name="charges",
    )(moments, unc, wh, wl)


def fock_kernel(count, steps, order_ref, tile_ref, *refs):
    charges, out_ref = refs[:count], refs[count]
    g = pl.program_id(0)

    @pl.when(g == 0)
    def _():
        out_ref[...] = jnp.zeros_like(out_ref)

    for k in range(count):

        @pl.when(g // steps == k)
        def _():
            out_ref[...] += lax.dot_general(
                charges[k][...], tile_ref[...], (((1,), (1,)), ((), ())),
                preferred_element_type=F32,
            )


def fock_call(order, tiles, charges):
    aux = tiles.shape[0]
    count = len(charges)
    width = charges[0].shape[1]
    steps = 2
    wide = width // steps

    def place(k):
        return pl.BlockSpec((NDENS, wide), lambda g, o: (0, jnp.clip(g - k * steps, 0, steps - 1)))

    return pl.pallas_call(
        functools.partial(fock_kernel, count, steps),
        grid_spec=pltpu.PrefetchScalarGridSpec(
            num_scalar_prefetch=1,
            grid=(count * steps,),
            in_specs=[
                pl.BlockSpec((aux, wide), lambda g, o: (0, o[g // steps] * steps + g % steps))
            ]
            + [place(k) for k in range(count)],
            out_specs=pl.BlockSpec((NDENS, aux), lambda g, o: (0, 0)),
        ),
        out_shape=jax.ShapeDtypeStruct((NDENS, aux), F32),
        cost_estimate=pl.CostEstimate(
            flops=2 * NDENS * aux * width * count,
            bytes_accessed=2 * aux * width * count,
            transcendentals=0,
        ),
        name="fock",
    )(order, tiles, *charges)


def trade(x, axis, k):
    count = lax.axis_size(axis)
    return lax.ppermute(x, axis, [(i, i ^ k) for i in range(count)])


def reach_out(last, initial):
    axes = ("sph", "fit")
    count = lax.axis_size("sph") * lax.axis_size("fit")
    up = [(i, i + 1) for i in range(count - 1)]
    down = [(i + 1, i) for i in range(count - 1)]
    return lax.ppermute(last, axes, up), lax.ppermute(initial, axes, down)


def body(tiles, coefs, centres, radii, neighbours, counts):
    spheres, slots = neighbours.shape
    reach = slots // 2
    fits = lax.axis_size("fit")
    sphs = lax.axis_size("sph")
    assert fits & (fits - 1) == 0 and sphs & (sphs - 1) == 0
    assert spheres % (2 * QUAD) == 0 and spheres // 2 == reach == 8
    fit = lax.axis_index("fit")
    first = (lax.axis_index("sph") * fits + fit) * spheres
    wh, wl = (jnp.asarray(a) for a in quad_weights())
    scales = jnp.asarray(lane_scales())

    own = jnp.concatenate([centres, radii[None, :]], axis=0).T
    before, after = reach_out(own[spheres - reach :], own[:reach])

    width = spheres * NG
    order = jnp.stack([fit ^ k for k in range(fits)]).astype(jnp.int32)
    partial = {}
    got = {}
    for k in list(range(fits - 1, 0, -1)) + [0]:
        partial[k] = phi_call(order[k : k + 1], coefs, tiles, width)
        if k:
            got[k] = trade(partial[k], "fit", k)

    t, unc = pair_call(
        first.reshape(1).astype(jnp.int32), before, own, after, neighbours, counts[:, None]
    )
    rl, rr = rhs_call([partial[0]] + [got[k] for k in range(1, fits)], unc, wh, wl)
    left, right = rl, rr
    for last in (False, True):
        below, above = reach_out(right, left)
        res = sweep_call(below, left, right, above, t, rl, rr, scales, last)
        if not last:
            left, right = res
    moments = res[0]
    charges = charge_call(moments, unc, wh, wl)
    all_charges = [charges] + [trade(charges, "fit", k) for k in range(1, fits)]
    fock = fock_call(order, tiles, all_charges)
    fock = fock + trade(fock, "sph", 1)
    bit = 2
    while bit < sphs:
        ks = [k for k in (bit, 2 * bit, 3 * bit) if k < sphs]
        fock = functools.reduce(jnp.add, [trade(fock, "sph", k) for k in ks], fock)
        bit *= 4
    shaped = moments.reshape(NDENS, spheres, LP)[:, :, :LM]
    return jnp.transpose(shaped, (1, 0, 2)), fock


def solution(mesh):
    placed = (
        P("fit", "sph"),
        P(None, "fit"),
        P(None, ("sph", "fit")),
        P(("sph", "fit")),
        P(("sph", "fit"), None),
        P(("sph", "fit")),
    )
    return jax.shard_map(
        body,
        mesh=mesh,
        in_specs=placed,
        out_specs=(P(("sph", "fit"), None, None), P(None, "fit")),
        check_vma=False,
    )
```

```python
import functools
import math

import jax
import jax.numpy as jnp
import ml_dtypes
import numpy as np
from jax import lax
from jax.experimental import pallas as pl
from jax.experimental.pallas import tpu as pltpu
from jax.sharding import PartitionSpec as P

DEGREE = 6
LM = 49
NTH = 16
NPHI = 20
NG = 320
NDENS = 16
LP = 64
QUAD = 4
QN = QUAD * NG
PN = 2 * NG
PIECE = 1280
VMEM_LIMIT = 60 << 20
BAND = 0.1
BF = jnp.bfloat16
F32 = jnp.float32


def gam(l, m):
    return (l + m - 1) * (l - 1 - m) / ((2 * l - 1) * (2 * l - 3))


def tables():
    c = -1.0 + (2.0 * np.arange(NTH) + 1.0) / NTH
    f = (np.arange(NPHI) + 0.5) * (2 * np.pi / NPHI)
    z = np.repeat(c, NPHI)
    s = np.sqrt(1 - z * z)
    az = np.tile(f, NTH)
    x, y = s * np.cos(az), s * np.sin(az)
    cos, sin = [np.ones_like(x)], [np.zeros_like(x)]
    for m in range(1, DEGREE + 1):
        cos.append(cos[m - 1] * x - sin[m - 1] * y)
        sin.append(cos[m - 1] * y + sin[m - 1] * x)
    ys, scale, invert = np.zeros((LM, NG)), np.zeros(LM), np.zeros(LM)
    for m in range(DEGREE + 1):
        q, lead = {m: np.ones_like(x)}, {m: 1.0}
        for odd in range(1, 2 * m, 2):
            lead[m] *= odd
        for l in range(m + 1, DEGREE + 1):
            q[l] = z * q[l - 1] - (gam(l, m) * q[l - 2] if l > m + 1 else 0.0)
            lead[l] = lead[l - 1] * (2 * l - 1) / (l - m)
        for l in range(m, DEGREE + 1):
            n = math.sqrt(
                (2 * l + 1) / (4 * math.pi) * math.factorial(l - m) / math.factorial(l + m)
            )
            n *= math.sqrt(2.0) if m else 1.0
            for sign, trig in ((1, cos[m]), (-1, sin[m])):
                if m == 0 and sign < 0:
                    continue
                i = l * l + l + sign * m
                ys[i] = n * lead[l] * q[l] * trig
                scale[i] = n * lead[l] * 4 * math.pi / (2 * l + 1)
                invert[i] = (2 * l + 1) / (4 * math.pi)
    return np.stack([x, y, z]), ys, scale, invert


def split(a):
    a = np.asarray(a, np.float32)
    hi = a.astype(ml_dtypes.bfloat16)
    return hi, (a - hi.astype(np.float32)).astype(ml_dtypes.bfloat16)


def halves(x):
    hi = x.astype(BF)
    return hi, (x - hi.astype(F32)).astype(BF)


def pair_weights():
    dirs, ys, _, _ = tables()
    w = np.zeros((2 * NG, 2 * LP))
    wy = ys.T * (4 * math.pi / NG)
    w[:NG, :LM] = wy
    w[NG:, LP : LP + LM] = wy
    d = np.zeros((8, 2 * NG), np.float32)
    d[:3, :NG] = dirs
    d[:3, NG:] = dirs
    return np.concatenate(split(w), 1), d


def even_weights():
    _, ys, _, _ = tables()
    w = np.zeros((PN, 2 * LP))
    w[:NG, :LM] = ys.T
    w[NG:, LP : LP + LM] = ys.T
    return np.concatenate(split(w), 1), np.concatenate(split(w.T), 1)


def lane_scales():
    _, _, scale, invert = tables()
    rows = np.zeros((8, 2 * LP), np.float32)
    for h in (0, LP):
        rows[0, h : h + LM] = scale * invert
        rows[1, h : h + LM] = invert
    return rows


def pieces(tile_ref, buf, sem, starts):
    copies = []
    for p, start in enumerate(starts):
        at = pl.ds(pl.multiple_of(start, 128), PIECE)
        copies.append(pltpu.make_async_copy(tile_ref.at[:, at], buf.at[p], sem.at[p]))
        copies[-1].start()
    return copies


def phi_kernel(count, width, chunk_ref, coef_ref, tile_ref, *rest):
    outs, (buf, sem) = rest[:count], rest[count:]
    per = width // PIECE
    starts = [chunk_ref[k] * width + p * PIECE for k in range(count) for p in range(per)]
    for i, copy in enumerate(pieces(tile_ref, buf, sem, starts)):
        copy.wait()
        ls = slice(i % per * PIECE, (i % per + 1) * PIECE)
        outs[i // per][:, ls] = jnp.dot(coef_ref[...], buf[i], preferred_element_type=F32)


def phi_call(chunks, coefs, tiles, width):
    aux = tiles.shape[0]
    count = chunks.shape[0]
    total = count * width // PIECE
    return pl.pallas_call(
        functools.partial(phi_kernel, count, width),
        in_specs=[
            pl.BlockSpec(memory_space=pltpu.SMEM),
            pl.BlockSpec(memory_space=pltpu.VMEM),
            pl.BlockSpec(memory_space=pl.ANY),
        ],
        out_specs=[pl.BlockSpec(memory_space=pltpu.VMEM)] * count,
        out_shape=[jax.ShapeDtypeStruct((NDENS, width), F32)] * count,
        scratch_shapes=[
            pltpu.VMEM((total, aux, PIECE), BF),
            pltpu.SemaphoreType.DMA((total,)),
        ],
        compiler_params=pltpu.CompilerParams(vmem_limit_bytes=VMEM_LIMIT),
        cost_estimate=pl.CostEstimate(
            flops=2 * NDENS * aux * width * count,
            bytes_accessed=(2 * aux + 4 * NDENS) * width * count,
            transcendentals=0,
        ),
        name="phi",
    )(chunks, coefs, tiles)


def pair_build(e, geo, mask, dir_ref, bh):
    lane = lax.broadcasted_iota(jnp.int32, (8, 128), 1)
    sub = lax.broadcasted_iota(jnp.int32, (8, 128), 0)
    own = jnp.broadcast_to(geo[pl.ds(e + 8, 1), :], (8, 128))
    mrow = jnp.broadcast_to(mask[pl.ds(e, 1), :], (8, 128))
    cols = []
    for g, start in ((0, e), (1, e + 9)):
        near = geo[pl.ds(start, 8), :]
        valid = jnp.sum(jnp.where(lane == sub + 8 * g, mrow, 0.0), axis=1, keepdims=True)
        on = valid > 0.0
        ir = 1.0 / jnp.where(on, near[:, 3:4], 1.0)
        off = jnp.where(on, own - near, 0.0)
        c = [off[:, 0:1] * ir, off[:, 1:2] * ir, off[:, 2:3] * ir, own[:, 3:4] * ir, valid]
        cols.append([jnp.broadcast_to(q, (8, 128)) for q in c])
    mid = [jnp.where(lane < 64, a, b) for a, b in zip(*cols)]
    sums = []
    for t in range(5):
        ox, oy, oz, q, valid = cols[0] if t < 2 else (mid if t == 2 else cols[1])
        ls = slice(128 * t, 128 * t + 128)
        x = ox + q * dir_ref[0:1, ls]
        y = oy + q * dir_ref[1:2, ls]
        z = oz + q * dir_ref[2:3, ls]
        r2 = x * x + y * y + z * z
        ramp = jnp.clip((1.0 - jnp.sqrt(r2)) * (1.0 / BAND), 0.0, 1.0)
        chi = ramp * ramp * (3.0 - 2.0 * ramp) * valid
        sums.append(jnp.sum(chi, axis=0, keepdims=True))
        cos, sin = [chi, chi * x], [None, chi * y]
        for m in range(2, DEGREE + 1):
            cos.append(cos[m - 1] * x - sin[m - 1] * y)
            sin.append(cos[m - 1] * y + sin[m - 1] * x)
        out = [None] * LM
        for m in range(DEGREE + 1):
            qm = {}
            for l in range(m, DEGREE + 1):
                if l == m + 1:
                    qm[l] = z
                elif l == m + 2:
                    qm[l] = z * z - gam(l, m) * r2
                elif l > m + 2:
                    qm[l] = z * qm[l - 1] - (gam(l, m) * r2) * qm[l - 2]
                for sign, trig in ((1, cos[m]), (-1, sin[m])):
                    if m == 0 and sign < 0:
                        continue
                    out[l * l + l + sign * m] = trig if l == m else trig * qm[l]
        out.append(jnp.zeros((8, 128), F32))
        for p in range(25):
            both = jnp.concatenate([out[2 * p], out[2 * p + 1]], axis=0)
            bh[16 * p : 16 * p + 16, ls] = both.astype(BF)
    return sums


def pair_finish(u, w_ref, t_ref, bh):
    r = jnp.dot(bh[...], w_ref[...], preferred_element_type=F32)
    tt = r[: LM * 8, : 2 * LP] + r[: LM * 8, 2 * LP :]
    a = jnp.swapaxes(tt.reshape(LM, 8, 2 * LP), 0, 1)
    a = jnp.concatenate([a, jnp.zeros((8, LP - LM, 2 * LP), F32)], 1).reshape(8 * LP, 2 * LP)
    hi, lo = halves(a)
    t_ref[u, :, : 2 * LP] = hi
    t_ref[u, :, 2 * LP :] = lo


def uncover(sums):
    low = lax.broadcasted_iota(jnp.int32, (1, 128), 1) < 64
    swap = lambda v: pltpu.roll(v, 64, 1)
    three = []
    for s in sums:
        r2, r3, r4 = swap(s[2]), swap(s[3]), swap(s[4])
        three.append([s[0] + jnp.where(low, r2, r3), s[1] + jnp.where(low, r3, r4), s[2] + r4])
    a, b = three
    b0, b1, b2 = swap(b[0]), swap(b[1]), swap(b[2])
    tiles = [a[0], a[1], jnp.where(low, a[2], b0), jnp.where(low, b0, b1), jnp.where(low, b1, b2)]
    return [jnp.maximum(0.0, 1.0 - t) for t in tiles]


def pair_kernel(
    first_ref, cnt_ref, before_ref, own_ref, after_ref, nbr_ref, dir_ref, w_ref,
    t_ref, unc_ref, geo, mask, *bhs
):
    spheres, slots = nbr_ref.shape
    reach = slots // 2
    step = pl.program_id(0)

    @pl.when(step == 0)
    def _():
        geo[...] = jnp.zeros_like(geo)
        geo[0:reach, 0:4] = before_ref[...]
        geo[reach : reach + spheres, 0:4] = own_ref[...]
        geo[reach + spheres :, 0:4] = after_ref[...]
        rel = nbr_ref[...] - first_ref[0]
        rel = rel - lax.broadcasted_iota(jnp.int32, (spheres, slots), 0)
        slot = lax.broadcasted_iota(jnp.int32, (spheres, slots), 1)
        row = lax.broadcasted_iota(jnp.int32, (spheres, slots), 0)
        many = jnp.zeros((spheres, slots), jnp.int32)
        for i in range(spheres):
            many = jnp.where(row == i, cnt_ref[i], many)
        listed = slot < many
        lane = lax.broadcasted_iota(jnp.int32, (spheres, 128), 1)
        found = jnp.zeros((spheres, 128), F32)
        for c in range(slots):
            gap = c - reach if c < reach else c - reach + 1
            hit = jnp.where(listed & (rel == gap), 1.0, 0.0)
            hit = jnp.max(hit, axis=1, keepdims=True)
            found = jnp.where(lane == c, hit, found)
        mask[...] = found

    sums = []
    for u in range(QUAD):
        sums.append(pair_build(step * QUAD + u, geo, mask, dir_ref, bhs[u]))
        pair_finish(u, w_ref, t_ref, bhs[u])
    tiles = uncover(sums[:2]) + uncover(sums[2:])
    for t, v in enumerate(tiles):
        unc_ref[0, :, 128 * t : 128 * t + 128] = v


def pair_call(first, before, own, after, neighbours, counts):
    spheres, slots = neighbours.shape
    reach = slots // 2
    w, d = pair_weights()
    whole = lambda *shape: pl.BlockSpec(shape, lambda e, f, c: (0,) * len(shape))
    return pl.pallas_call(
        pair_kernel,
        grid_spec=pltpu.PrefetchScalarGridSpec(
            num_scalar_prefetch=2,
            grid=(spheres // QUAD,),
            in_specs=[
                whole(reach, 4),
                whole(spheres, 4),
                whole(reach, 4),
                whole(spheres, slots),
                whole(8, 2 * NG),
                whole(2 * NG, 4 * LP),
            ],
            out_specs=[
                pl.BlockSpec((QUAD, 8 * LP, 4 * LP), lambda e, f, c: (e, 0, 0)),
                pl.BlockSpec((1, 1, QN), lambda e, f, c: (e, 0, 0)),
            ],
            scratch_shapes=[
                pltpu.VMEM((spheres + 2 * reach, 128), F32),
                pltpu.VMEM((spheres, 128), F32),
            ]
            + [pltpu.VMEM((400, 2 * NG), BF)] * QUAD,
        ),
        out_shape=[
            jax.ShapeDtypeStruct((spheres, 8 * LP, 4 * LP), BF),
            jax.ShapeDtypeStruct((spheres // QUAD, 1, QN), F32),
        ],
        cost_estimate=pl.CostEstimate(
            flops=spheres * 2 * 400 * 640 * 256, bytes_accessed=spheres * 262144, transcendentals=0
        ),
        name="pairs",
    )(first, counts, before, own, after, neighbours, jnp.asarray(d), jnp.asarray(w))


def rhs_kernel(count, *refs):
    phis, (unc_ref, w_ref, left_ref, right_ref) = refs[:count], refs[count:]
    pairs = 2 * unc_ref.shape[0]
    rows = []
    for b in range(pairs):
        ls = slice(b * PN, (b + 1) * PN)
        total = phis[0][:, ls]
        for p in phis[1:]:
            total = total + p[:, ls]
        rows.append(total * unc_ref[b // 2, :, b % 2 * PN : (b % 2 + 1) * PN])
    hi, lo = halves(jnp.concatenate(rows, 0))
    n = pairs * NDENS
    r = jnp.dot(jnp.concatenate([hi, lo], 0), w_ref[...], preferred_element_type=F32)
    out = r[:n, : 2 * LP] + r[:n, 2 * LP :] + r[n:, : 2 * LP]
    out = out * (-4.0 * math.pi / NG)
    for b in range(pairs):
        ref, at = (left_ref, b) if b < pairs // 2 else (right_ref, b - pairs // 2)
        ref[:, at * 2 * LP : (at + 1) * 2 * LP] = out[b * NDENS : (b + 1) * NDENS]


def rhs_call(phis, unc, w):
    half = unc.shape[0] // 2 * QUAD * LP
    return pl.pallas_call(
        functools.partial(rhs_kernel, len(phis)),
        out_shape=[jax.ShapeDtypeStruct((NDENS, half), F32)] * 2,
        cost_estimate=pl.CostEstimate(
            flops=6 * NDENS * unc.shape[0] * QN * 256, bytes_accessed=1700000, transcendentals=0
        ),
        name="rhs",
    )(*phis, unc, w)


def gather_field(ts, x, xs, e):
    low = lax.broadcasted_iota(jnp.int32, (NDENS, 128), 1) < LP
    parts = []
    for odd in (0, 1):
        i = e + odd
        below, above = (x, xs) if odd == 0 else (xs, x)
        lo_at = e * LP
        up_at = (e + 8) * LP if odd == 0 else (e + 10) * LP
        lhs = jnp.concatenate(
            [below[:, lo_at : lo_at + 8 * LP], above[:, up_at : up_at + 8 * LP]], 0
        )
        r = jnp.dot(lhs, ts[i], preferred_element_type=F32)
        n = NDENS
        a = r[0:n, : 2 * LP] + r[n : 2 * n, : 2 * LP] + r[0:n, 2 * LP :]
        b = r[2 * n : 3 * n, : 2 * LP] + r[3 * n :, : 2 * LP] + r[2 * n : 3 * n, 2 * LP :]
        parts.append((a, b))
    (a0, b0), (a1, b1) = parts
    return jnp.where(low, a0, b1) + pltpu.roll(jnp.where(low, a1, b0), LP, 1)


def sweep_kernel(spheres, last, before_ref, left_ref, right_ref, after_ref, t_ref, rl_ref,
                 rr_ref, sc_ref, *rest):
    x, xs, ts, sem = rest[-4:]
    copies = [pltpu.make_async_copy(t_ref.at[i], ts.at[i], sem.at[i]) for i in range(spheres)]
    for copy in copies:
        copy.start()
    half = left_ref.shape[1]
    at = 0
    for ref in (before_ref, left_ref, right_ref, after_ref):
        wide = ref.shape[1]
        for t in range(wide // 128):
            hi, lo = halves(ref[:, 128 * t : 128 * t + 128] * sc_ref[0:1, :])
            x[0:NDENS, at : at + 128] = hi
            x[NDENS:, at : at + 128] = lo
            at += 128
    v = x[...].astype(F32)
    xs[...] = jnp.concatenate([v[:, LP:], v[:, :LP]], 1).astype(BF)
    rows = []
    for e in range(0, spheres, 2):
        copies[e].wait()
        copies[e + 1].wait()
        got = gather_field(ts, x, xs, e)
        at = e * LP
        ref, at = (rl_ref, at) if at < half else (rr_ref, at - half)
        new = ref[:, at : at + 128] + got
        if last:
            new = new * sc_ref[1:2, :]
            rest[2][e] = new[:, :LM]
            rest[2][e + 1] = pltpu.roll(new, LP, 1)[:, :LM]
            rows.append(new)
        else:
            rest[0 if e * LP < half else 1][:, at : at + 128] = new
    if last:
        unc_ref, y_ref, _, out_ref = rest[:4]
        hi, lo = halves(jnp.concatenate(rows, 0))
        n = len(rows) * NDENS
        r = jnp.dot(jnp.concatenate([hi, lo], 0), y_ref[...], preferred_element_type=F32)
        out = r[:n, :PN] + r[:n, PN:] + r[n:, :PN]
        for b in range(len(rows)):
            weight = unc_ref[b // 2, :, b % 2 * PN : (b % 2 + 1) * PN] * (4.0 * math.pi / NG)
            out_ref[:, b * PN : (b + 1) * PN] = (out[b * NDENS : (b + 1) * NDENS] * weight).astype(BF)


def sweep_call(before, left, right, after, t, rl, rr, scales, last=None):
    spheres = t.shape[0]
    half = left.shape[1]
    if last is None:
        outs = [jax.ShapeDtypeStruct((NDENS, half), F32)] * 2
        more = ()
    else:
        outs = [
            jax.ShapeDtypeStruct((spheres, NDENS, LM), F32),
            jax.ShapeDtypeStruct((NDENS, spheres * NG), BF),
        ]
        more = last
    total = before.shape[1] + 2 * half + after.shape[1]
    vmem = pl.BlockSpec(memory_space=pltpu.VMEM)
    return pl.pallas_call(
        functools.partial(sweep_kernel, spheres, last is not None),
        in_specs=[vmem] * 4 + [pl.BlockSpec(memory_space=pl.ANY)] + [vmem] * (3 + len(more)),
        out_specs=[vmem] * 2,
        out_shape=outs,
        scratch_shapes=[pltpu.VMEM((2 * NDENS, total), BF)] * 2
        + [pltpu.VMEM(t.shape, BF), pltpu.SemaphoreType.DMA((spheres,))],
        compiler_params=pltpu.CompilerParams(vmem_limit_bytes=VMEM_LIMIT),
        cost_estimate=pl.CostEstimate(
            flops=spheres * 2 * 64 * 512 * 256, bytes_accessed=spheres * 262144, transcendentals=0
        ),
        name="sweep",
    )(before, left, right, after, t, rl, rr, scales, *more)


def fock_kernel(width, chunk_ref, charge_ref, tile_ref, *rest):
    out_ref, buf, sem = rest[-3:]
    total = rest[0][...] if len(rest) == 4 else None
    starts = [chunk_ref[0] * width + p * PIECE for p in range(width // PIECE)]
    for i, copy in enumerate(pieces(tile_ref, buf, sem, starts)):
        copy.wait()
        part = lax.dot_general(
            charge_ref[:, i * PIECE : (i + 1) * PIECE], buf[i], (((1,), (1,)), ((), ())),
            preferred_element_type=F32,
        )
        total = part if total is None else total + part
    out_ref[...] = total


def fock_call(chunk, charges, tiles, before=None):
    aux = tiles.shape[0]
    width = charges.shape[1]
    total = width // PIECE
    vmem = pl.BlockSpec(memory_space=pltpu.VMEM)
    more = [] if before is None else [before]
    return pl.pallas_call(
        functools.partial(fock_kernel, width),
        in_specs=[pl.BlockSpec(memory_space=pltpu.SMEM), vmem, pl.BlockSpec(memory_space=pl.ANY)]
        + [vmem] * len(more),
        out_specs=vmem,
        out_shape=jax.ShapeDtypeStruct((NDENS, aux), F32),
        scratch_shapes=[
            pltpu.VMEM((total, aux, PIECE), BF),
            pltpu.SemaphoreType.DMA((total,)),
        ],
        compiler_params=pltpu.CompilerParams(vmem_limit_bytes=VMEM_LIMIT),
        cost_estimate=pl.CostEstimate(
            flops=2 * NDENS * aux * width, bytes_accessed=2 * aux * width, transcendentals=0
        ),
        name="fock",
    )(chunk, charges, tiles, *more)


def trade(x, axis, k):
    count = lax.axis_size(axis)
    return lax.ppermute(x, axis, [(i, i ^ k) for i in range(count)])


def reach_out(last, initial):
    axes = ("sph", "fit")
    count = lax.axis_size("sph") * lax.axis_size("fit")
    up = [(i, (i + 1) % count) for i in range(count)]
    down = [((i + 1) % count, i) for i in range(count)]
    return lax.ppermute(last, axes, up), lax.ppermute(initial, axes, down)


def body(tiles, coefs, centres, radii, neighbours, counts):
    spheres, slots = neighbours.shape
    reach = slots // 2
    fits = lax.axis_size("fit")
    sphs = lax.axis_size("sph")
    assert fits & (fits - 1) == 0 and sphs & (sphs - 1) == 0
    assert spheres % (2 * QUAD) == 0 and spheres // 2 == reach == 8
    fit = lax.axis_index("fit")
    first = (lax.axis_index("sph") * fits + fit) * spheres
    w, wt = (jnp.asarray(a) for a in even_weights())
    scales = jnp.asarray(lane_scales())
    width = spheres * NG
    order = jnp.bitwise_xor(fit, jnp.arange(fits, dtype=jnp.int32))

    own = jnp.concatenate([centres, radii[None, :]], axis=0).T
    before, after = reach_out(own[spheres - reach :], own[:reach])

    sent = phi_call(order[1:], coefs, tiles, width)
    got = [trade(sent[k - 1], "fit", k) for k in range(1, fits)]
    mine = phi_call(order[:1], coefs, tiles, width)

    t, unc = pair_call(
        first.reshape(1).astype(jnp.int32), before, own, after, neighbours, counts
    )
    rl, rr = rhs_call([*mine, *got], unc, w)
    below, above = reach_out(rr, rl)
    left, right = sweep_call(below, rl, rr, above, t, rl, rr, scales)
    below, above = reach_out(right, left)
    moments, charges = sweep_call(below, left, right, above, t, rl, rr, scales, (unc, wt))
    others = [trade(charges, "fit", k) for k in range(1, fits)]
    fock = fock_call(order[:1], charges, tiles)
    for k in range(1, fits):
        fock = fock_call(order[k : k + 1], others[k - 1], tiles, fock)
    fock = fock + trade(fock, "sph", 1)
    bit = 2
    while bit < sphs:
        ks = [k for k in (bit, 2 * bit, 3 * bit) if k < sphs]
        fock = functools.reduce(jnp.add, [trade(fock, "sph", k) for k in ks], fock)
        bit *= 4
    return moments, fock


def solution(mesh):
    placed = (
        P("fit", "sph"),
        P(None, "fit"),
        P(None, ("sph", "fit")),
        P(("sph", "fit")),
        P(("sph", "fit"), None),
        P(("sph", "fit")),
    )
    return jax.shard_map(
        body,
        mesh=mesh,
        in_specs=placed,
        out_specs=(P(("sph", "fit"), None, None), P(None, "fit")),
        check_vma=False,
    )
```

```python
import functools
import math

import jax
import jax.numpy as jnp
import ml_dtypes
import numpy as np
from jax import lax
from jax.experimental import pallas as pl
from jax.experimental.pallas import tpu as pltpu
from jax.sharding import PartitionSpec as P

DEGREE = 6
LM = 49
NTH = 16
NPHI = 20
NG = 320
NDENS = 16
LP = 64
QUAD = 4
QN = QUAD * NG
PN = 2 * NG
PIECE = 2560
PARAMS = pltpu.CompilerParams(vmem_limit_bytes=16 << 20)
VMEM = pl.BlockSpec(memory_space=pltpu.VMEM)
SMEM = pl.BlockSpec(memory_space=pltpu.SMEM)
BAND = 0.1
BF = jnp.bfloat16
F32 = jnp.float32


def gam(l, m):
    return (l + m - 1) * (l - 1 - m) / ((2 * l - 1) * (2 * l - 3))


def tables():
    c = -1.0 + (2.0 * np.arange(NTH) + 1.0) / NTH
    f = (np.arange(NPHI) + 0.5) * (2 * np.pi / NPHI)
    z = np.repeat(c, NPHI)
    s = np.sqrt(1 - z * z)
    az = np.tile(f, NTH)
    x, y = s * np.cos(az), s * np.sin(az)
    cos, sin = [np.ones_like(x)], [np.zeros_like(x)]
    for m in range(1, DEGREE + 1):
        cos.append(cos[m - 1] * x - sin[m - 1] * y)
        sin.append(cos[m - 1] * y + sin[m - 1] * x)
    ys, scale, invert = np.zeros((LM, NG)), np.zeros(LM), np.zeros(LM)
    for m in range(DEGREE + 1):
        q, lead = {m: np.ones_like(x)}, {m: 1.0}
        for odd in range(1, 2 * m, 2):
            lead[m] *= odd
        for l in range(m + 1, DEGREE + 1):
            q[l] = z * q[l - 1] - (gam(l, m) * q[l - 2] if l > m + 1 else 0.0)
            lead[l] = lead[l - 1] * (2 * l - 1) / (l - m)
        for l in range(m, DEGREE + 1):
            n = math.sqrt(
                (2 * l + 1) / (4 * math.pi) * math.factorial(l - m) / math.factorial(l + m)
            )
            n *= math.sqrt(2.0) if m else 1.0
            for sign, trig in ((1, cos[m]), (-1, sin[m])):
                if m == 0 and sign < 0:
                    continue
                i = l * l + l + sign * m
                ys[i] = n * lead[l] * q[l] * trig
                scale[i] = n * lead[l] * 4 * math.pi / (2 * l + 1)
                invert[i] = (2 * l + 1) / (4 * math.pi)
    return np.stack([x, y, z]), ys, scale, invert


def split(a):
    a = np.asarray(a, np.float32)
    hi = a.astype(ml_dtypes.bfloat16)
    return hi, (a - hi.astype(np.float32)).astype(ml_dtypes.bfloat16)


def halves(x):
    hi = x.astype(BF)
    return hi, (x - hi.astype(F32)).astype(BF)


def pair_weights():
    dirs, ys, _, _ = tables()
    w = np.zeros((2 * NG, 2 * LP))
    wy = ys.T * (4 * math.pi / NG)
    w[:NG, :LM] = wy
    w[NG:, LP : LP + LM] = wy
    d = np.zeros((8, 2 * NG), np.float32)
    d[:3, :NG] = dirs
    d[:3, NG:] = dirs
    return np.concatenate(split(w), 1), d


def even_weights():
    _, ys, _, _ = tables()
    w = np.zeros((PN, 2 * LP))
    w[:NG, :LM] = ys.T
    w[NG:, LP : LP + LM] = ys.T
    return np.concatenate(split(w), 1), np.concatenate(split(w.T), 1)


def lane_scales():
    _, _, scale, invert = tables()
    rows = np.zeros((8, 2 * LP), np.float32)
    for h in (0, LP):
        rows[0, h : h + LM] = scale * invert
        rows[1, h : h + LM] = invert
    return rows


def chunk_piece(k, width, p):
    at = (lax.axis_index("fit") ^ k) * width + p * PIECE
    return pl.ds(pl.multiple_of(at, 128), PIECE)


def phi_kernel(width, coef_ref, far_ref, *rest):
    outs, (tile_ref, sem) = rest[:-2], rest[-2:]
    per = width // PIECE
    todo = [(k, p) for k in [*range(1, len(outs)), 0] for p in range(per)]
    copies = []
    for i, (k, p) in enumerate(todo):
        at = chunk_piece(k, width, p)
        copies.append(pltpu.make_async_copy(far_ref.at[:, at], tile_ref.at[:, at], sem.at[i]))
        copies[-1].start()
    for (k, p), copy in zip(todo, copies):
        copy.wait()
        outs[k][:, p * PIECE : (p + 1) * PIECE] = jnp.dot(
            coef_ref[...], tile_ref[:, chunk_piece(k, width, p)], preferred_element_type=F32
        )


def phi_call(coefs, tiles, width):
    aux, points = tiles.shape
    count = points // width
    return pl.pallas_call(
        functools.partial(phi_kernel, width),
        in_specs=[VMEM, pl.BlockSpec(memory_space=pltpu.HBM)],
        out_specs=[VMEM] * (count + 1),
        out_shape=[jax.ShapeDtypeStruct((NDENS, width), F32)] * count
        + [jax.ShapeDtypeStruct(tiles.shape, tiles.dtype)],
        scratch_shapes=[pltpu.SemaphoreType.DMA((points // PIECE,))],
        compiler_params=PARAMS,
        cost_estimate=pl.CostEstimate(
            flops=2 * NDENS * aux * points,
            bytes_accessed=(2 * aux + 4 * NDENS) * points,
            transcendentals=0,
        ),
        name="phi",
    )(coefs, pltpu.with_memory_space_constraint(tiles, pltpu.HBM))


def pair_build(e, geo, mask, dir_ref, bh):
    lane = lax.broadcasted_iota(jnp.int32, (8, 128), 1)
    sub = lax.broadcasted_iota(jnp.int32, (8, 128), 0)
    own = jnp.broadcast_to(geo[pl.ds(e + 8, 1), :], (8, 128))
    mrow = jnp.broadcast_to(mask[pl.ds(e, 1), :], (8, 128))
    cols = []
    for g, start in ((0, e), (1, e + 9)):
        near = geo[pl.ds(start, 8), :]
        valid = jnp.sum(jnp.where(lane == sub + 8 * g, mrow, 0.0), axis=1, keepdims=True)
        on = valid > 0.0
        ir = 1.0 / jnp.where(on, near[:, 3:4], 1.0)
        off = jnp.where(on, own - near, 0.0)
        c = [off[:, 0:1] * ir, off[:, 1:2] * ir, off[:, 2:3] * ir, own[:, 3:4] * ir, valid]
        cols.append([jnp.broadcast_to(q, (8, 128)) for q in c])
    mid = [jnp.where(lane < 64, a, b) for a, b in zip(*cols)]
    sums = []
    for t in range(5):
        ox, oy, oz, q, valid = cols[0] if t < 2 else (mid if t == 2 else cols[1])
        ls = slice(128 * t, 128 * t + 128)
        x = ox + q * dir_ref[0:1, ls]
        y = oy + q * dir_ref[1:2, ls]
        z = oz + q * dir_ref[2:3, ls]
        r2 = x * x + y * y + z * z
        ramp = jnp.clip((1.0 - jnp.sqrt(r2)) * (1.0 / BAND), 0.0, 1.0)
        chi = ramp * ramp * (3.0 - 2.0 * ramp) * valid
        sums.append(jnp.sum(chi, axis=0, keepdims=True))
        cos, sin = [chi, chi * x], [None, chi * y]
        for m in range(2, DEGREE + 1):
            cos.append(cos[m - 1] * x - sin[m - 1] * y)
            sin.append(cos[m - 1] * y + sin[m - 1] * x)
        out = [None] * LM
        for m in range(DEGREE + 1):
            qm = {}
            for l in range(m, DEGREE + 1):
                if l == m + 1:
                    qm[l] = z
                elif l == m + 2:
                    qm[l] = z * z - gam(l, m) * r2
                elif l > m + 2:
                    qm[l] = z * qm[l - 1] - (gam(l, m) * r2) * qm[l - 2]
                for sign, trig in ((1, cos[m]), (-1, sin[m])):
                    if m == 0 and sign < 0:
                        continue
                    out[l * l + l + sign * m] = trig if l == m else trig * qm[l]
        out.append(jnp.zeros((8, 128), F32))
        for p in range(25):
            both = jnp.concatenate([out[2 * p], out[2 * p + 1]], axis=0)
            bh[16 * p : 16 * p + 16, ls] = both.astype(BF)
    return sums


def pair_finish(e, w_ref, t_ref, bh):
    r = jnp.dot(bh[...], w_ref[...], preferred_element_type=F32)
    tt = r[: LM * 8, : 2 * LP] + r[: LM * 8, 2 * LP :]
    a = jnp.swapaxes(tt.reshape(LM, 8, 2 * LP), 0, 1)
    a = jnp.concatenate([a, jnp.zeros((8, LP - LM, 2 * LP), F32)], 1).reshape(8 * LP, 2 * LP)
    hi, lo = halves(a)
    t_ref[e, :, : 2 * LP] = hi
    t_ref[e, :, 2 * LP :] = lo


def uncover(sums):
    low = lax.broadcasted_iota(jnp.int32, (1, 128), 1) < 64
    swap = lambda v: pltpu.roll(v, 64, 1)
    three = []
    for s in sums:
        r2, r3, r4 = swap(s[2]), swap(s[3]), swap(s[4])
        three.append([s[0] + jnp.where(low, r2, r3), s[1] + jnp.where(low, r3, r4), s[2] + r4])
    a, b = three
    b0, b1, b2 = swap(b[0]), swap(b[1]), swap(b[2])
    tiles = [a[0], a[1], jnp.where(low, a[2], b0), jnp.where(low, b0, b1), jnp.where(low, b1, b2)]
    return [jnp.maximum(0.0, 1.0 - t) for t in tiles]


def pair_kernel(
    cnt_ref, before_ref, own_ref, after_ref, nbr_ref, dir_ref, w_ref,
    t_ref, unc_ref, geo, mask, *bhs
):
    spheres, slots = nbr_ref.shape
    reach = slots // 2
    first = (lax.axis_index("sph") * lax.axis_size("fit") + lax.axis_index("fit")) * spheres
    rows = jnp.concatenate([before_ref[...], own_ref[...], after_ref[...]], axis=1)
    wide = jnp.concatenate([rows, jnp.zeros((4, 128 - rows.shape[1]), F32)], axis=1)
    wide = jnp.concatenate([wide, jnp.zeros((124, 128), F32)], axis=0)
    geo[...] = wide.T[: rows.shape[1]]
    row = lax.broadcasted_iota(jnp.int32, (spheres, slots), 0)
    slot = lax.broadcasted_iota(jnp.int32, (spheres, slots), 1)
    rel = nbr_ref[...] - first - row
    many = jnp.zeros((spheres, slots), jnp.int32)
    for i in range(spheres):
        many = jnp.where(row == i, cnt_ref[i], many)
    listed = slot < many
    lane = lax.broadcasted_iota(jnp.int32, (spheres, 128), 1)
    found = jnp.zeros((spheres, 128), F32)
    for c in range(slots):
        gap = c - reach if c < reach else c - reach + 1
        hit = jnp.where(listed & (rel == gap), 1.0, 0.0)
        hit = jnp.max(hit, axis=1, keepdims=True)
        found = jnp.where(lane == c, hit, found)
    mask[...] = found

    def step(b, carry):
        sums = []
        for u in range(QUAD):
            e = b * QUAD + u
            sums.append(pair_build(e, geo, mask, dir_ref, bhs[u]))
            pair_finish(e, w_ref, t_ref, bhs[u])
        tiles = uncover(sums[:2]) + uncover(sums[2:])
        for t, v in enumerate(tiles):
            unc_ref[b, :, 128 * t : 128 * t + 128] = v
        return carry

    lax.fori_loop(0, spheres // QUAD, step, 0)


def pair_call(before, own, after, neighbours, counts):
    spheres, slots = neighbours.shape
    reach = slots // 2
    w, d = pair_weights()
    return pl.pallas_call(
        pair_kernel,
        in_specs=[SMEM] + [VMEM] * 6,
        out_specs=[VMEM] * 2,
        scratch_shapes=[
            pltpu.VMEM((spheres + 2 * reach, 128), F32),
            pltpu.VMEM((spheres, 128), F32),
        ]
        + [pltpu.VMEM((400, 2 * NG), BF)] * QUAD,
        out_shape=[
            jax.ShapeDtypeStruct((spheres, 8 * LP, 4 * LP), BF),
            jax.ShapeDtypeStruct((spheres // QUAD, 1, QN), F32),
        ],
        compiler_params=PARAMS,
        cost_estimate=pl.CostEstimate(
            flops=spheres * 2 * 400 * 640 * 256, bytes_accessed=spheres * 262144, transcendentals=0
        ),
        name="pairs",
    )(counts, before, own, after, neighbours, jnp.asarray(d), jnp.asarray(w))


def rhs_kernel(count, *refs):
    phis, (unc_ref, w_ref, left_ref, right_ref) = refs[:count], refs[count:]
    pairs = 2 * unc_ref.shape[0]
    rows = []
    for b in range(pairs):
        ls = slice(b * PN, (b + 1) * PN)
        total = phis[0][:, ls]
        for p in phis[1:]:
            total = total + p[:, ls]
        rows.append(total * unc_ref[b // 2, :, b % 2 * PN : (b % 2 + 1) * PN])
    hi, lo = halves(jnp.concatenate(rows, 0))
    n = pairs * NDENS
    r = jnp.dot(jnp.concatenate([hi, lo], 0), w_ref[...], preferred_element_type=F32)
    out = r[:n, : 2 * LP] + r[:n, 2 * LP :] + r[n:, : 2 * LP]
    out = out * (-4.0 * math.pi / NG)
    for b in range(pairs):
        ref, at = (left_ref, b) if b < pairs // 2 else (right_ref, b - pairs // 2)
        ref[:, at * 2 * LP : (at + 1) * 2 * LP] = out[b * NDENS : (b + 1) * NDENS]


def rhs_call(phis, unc, w):
    half = unc.shape[0] // 2 * QUAD * LP
    return pl.pallas_call(
        functools.partial(rhs_kernel, len(phis)),
        in_specs=[VMEM] * (len(phis) + 2),
        out_specs=[VMEM] * 2,
        compiler_params=PARAMS,
        out_shape=[jax.ShapeDtypeStruct((NDENS, half), F32)] * 2,
        cost_estimate=pl.CostEstimate(
            flops=6 * NDENS * unc.shape[0] * QN * 256, bytes_accessed=1700000, transcendentals=0
        ),
        name="rhs",
    )(*phis, unc, w)


def gather_field(t_ref, x, xs, e):
    low = lax.broadcasted_iota(jnp.int32, (NDENS, 128), 1) < LP
    parts = []
    for odd in (0, 1):
        i = e + odd
        below, above = (x, xs) if odd == 0 else (xs, x)
        lo_at = e * LP
        up_at = (e + 8) * LP if odd == 0 else (e + 10) * LP
        lhs = jnp.concatenate(
            [below[:, lo_at : lo_at + 8 * LP], above[:, up_at : up_at + 8 * LP]], 0
        )
        r = jnp.dot(lhs, t_ref[i], preferred_element_type=F32)
        n = NDENS
        a = r[0:n, : 2 * LP] + r[n : 2 * n, : 2 * LP] + r[0:n, 2 * LP :]
        b = r[2 * n : 3 * n, : 2 * LP] + r[3 * n :, : 2 * LP] + r[2 * n : 3 * n, 2 * LP :]
        parts.append((a, b))
    (a0, b0), (a1, b1) = parts
    return jnp.where(low, a0, b1) + pltpu.roll(jnp.where(low, a1, b0), LP, 1)


def sweep_kernel(spheres, last, before_ref, left_ref, right_ref, after_ref, t_ref, rl_ref,
                 rr_ref, sc_ref, *rest):
    x, xs = rest[-2:]
    half = left_ref.shape[1]
    at = 0
    for ref in (before_ref, left_ref, right_ref, after_ref):
        wide = ref.shape[1]
        for t in range(wide // 128):
            hi, lo = halves(ref[:, 128 * t : 128 * t + 128] * sc_ref[0:1, :])
            x[0:NDENS, at : at + 128] = hi
            x[NDENS:, at : at + 128] = lo
            at += 128
    v = x[...].astype(F32)
    xs[...] = jnp.concatenate([v[:, LP:], v[:, :LP]], 1).astype(BF)
    rows = []
    for e in range(0, spheres, 2):
        got = gather_field(t_ref, x, xs, e)
        at = e * LP
        ref, at = (rl_ref, at) if at < half else (rr_ref, at - half)
        new = ref[:, at : at + 128] + got
        if last:
            new = new * sc_ref[1:2, :]
            rest[2][e] = new[:, :LM]
            rest[2][e + 1] = pltpu.roll(new, LP, 1)[:, :LM]
            rows.append(new)
        else:
            rest[0 if e * LP < half else 1][:, at : at + 128] = new
    if last:
        unc_ref, y_ref, _, out_ref = rest[:4]
        hi, lo = halves(jnp.concatenate(rows, 0))
        n = len(rows) * NDENS
        r = jnp.dot(jnp.concatenate([hi, lo], 0), y_ref[...], preferred_element_type=F32)
        out = r[:n, :PN] + r[:n, PN:] + r[n:, :PN]
        for b in range(len(rows)):
            weight = unc_ref[b // 2, :, b % 2 * PN : (b % 2 + 1) * PN] * (4.0 * math.pi / NG)
            out_ref[:, b * PN : (b + 1) * PN] = (out[b * NDENS : (b + 1) * NDENS] * weight).astype(BF)


def sweep_call(before, left, right, after, t, rl, rr, scales, last=None):
    spheres = t.shape[0]
    half = left.shape[1]
    if last is None:
        outs = [jax.ShapeDtypeStruct((NDENS, half), F32)] * 2
        more = ()
    else:
        outs = [
            jax.ShapeDtypeStruct((spheres, NDENS, LM), F32),
            jax.ShapeDtypeStruct((NDENS, spheres * NG), BF),
        ]
        more = last
    total = before.shape[1] + 2 * half + after.shape[1]
    return pl.pallas_call(
        functools.partial(sweep_kernel, spheres, last is not None),
        in_specs=[VMEM] * (8 + len(more)),
        out_specs=[VMEM] * 2,
        out_shape=outs,
        scratch_shapes=[pltpu.VMEM((2 * NDENS, total), BF)] * 2,
        compiler_params=PARAMS,
        cost_estimate=pl.CostEstimate(
            flops=spheres * 2 * 64 * 512 * 256, bytes_accessed=spheres * 262144, transcendentals=0
        ),
        name="sweep",
    )(before, left, right, after, t, rl, rr, scales, *more)


def fock_kernel(k, width, charge_ref, tile_ref, *rest):
    total = rest[0][...] if len(rest) == 2 else None
    for p in range(width // PIECE):
        part = lax.dot_general(
            charge_ref[:, p * PIECE : (p + 1) * PIECE],
            tile_ref[:, chunk_piece(k, width, p)],
            (((1,), (1,)), ((), ())),
            preferred_element_type=F32,
        )
        total = part if total is None else total + part
    rest[-1][...] = total


def fock_call(k, charges, tiles, before=None):
    aux = tiles.shape[0]
    width = charges.shape[1]
    more = [] if before is None else [before]
    return pl.pallas_call(
        functools.partial(fock_kernel, k, width),
        in_specs=[VMEM] * (2 + len(more)),
        out_specs=VMEM,
        out_shape=jax.ShapeDtypeStruct((NDENS, aux), F32),
        compiler_params=PARAMS,
        cost_estimate=pl.CostEstimate(
            flops=2 * NDENS * aux * width, bytes_accessed=2 * aux * width, transcendentals=0
        ),
        name="fock",
    )(charges, tiles, *more)


def trade(x, axis, k):
    count = lax.axis_size(axis)
    return lax.ppermute(x, axis, [(i, i ^ k) for i in range(count)])


def reach_out(last, initial):
    axes = ("sph", "fit")
    count = lax.axis_size("sph") * lax.axis_size("fit")
    up = [(i, (i + 1) % count) for i in range(count)]
    down = [((i + 1) % count, i) for i in range(count)]
    return lax.ppermute(last, axes, up), lax.ppermute(initial, axes, down)


def body(tiles, coefs, centres, radii, neighbours, counts):
    spheres, slots = neighbours.shape
    reach = slots // 2
    fits = lax.axis_size("fit")
    sphs = lax.axis_size("sph")
    assert fits & (fits - 1) == 0 and sphs & (sphs - 1) == 0
    assert spheres % (2 * QUAD) == 0 and spheres // 2 == reach == 8
    w, wt = (jnp.asarray(a) for a in even_weights())
    scales = jnp.asarray(lane_scales())
    width = spheres * NG

    own = jnp.concatenate([centres, radii[None, :]], axis=0)
    before, after = reach_out(own[:, spheres - reach :], own[:, :reach])
    *phis, near_tiles = phi_call(coefs, tiles, width)
    phis, before, after = lax.optimization_barrier((phis, before, after))
    got = [trade(phis[k], "fit", k) for k in range(1, fits)]
    t, unc = pair_call(before, own, after, neighbours, counts)
    rl, rr = rhs_call([phis[0], *got], unc, w)
    below, above = reach_out(rr, rl)
    left, right = sweep_call(below, rl, rr, above, t, rl, rr, scales)
    below, above = reach_out(right, left)
    moments, charges = sweep_call(below, left, right, above, t, rl, rr, scales, (unc, wt))
    others = [trade(charges, "fit", k) for k in range(1, fits)]
    fock = fock_call(0, charges, near_tiles)
    for k in range(1, fits):
        fock = fock_call(k, others[k - 1], near_tiles, fock)
    fock = fock + trade(fock, "sph", 1)
    bit = 2
    while bit < sphs:
        ks = [k for k in (bit, 2 * bit, 3 * bit) if k < sphs]
        fock = functools.reduce(jnp.add, [trade(fock, "sph", k) for k in ks], fock)
        bit *= 4
    return moments, fock


def solution(mesh):
    placed = (
        P("fit", "sph"),
        P(None, "fit"),
        P(None, ("sph", "fit")),
        P(("sph", "fit")),
        P(("sph", "fit"), None),
        P(("sph", "fit")),
    )
    return jax.shard_map(
        body,
        mesh=mesh,
        in_specs=placed,
        out_specs=(P(("sph", "fit"), None, None), P(None, "fit")),
        check_vma=False,
    )
```

```python
import functools
import math

import jax
import jax.numpy as jnp
import ml_dtypes
import numpy as np
from jax import lax
from jax.experimental import pallas as pl
from jax.experimental.pallas import tpu as pltpu
from jax.sharding import PartitionSpec as P

DEGREE = 6
LM = 49
NTH = 16
NPHI = 20
NG = 320
NDENS = 16
LP = 64
QUAD = 4
QN = QUAD * NG
PN = 2 * NG
PIECE = 2560
PARAMS = pltpu.CompilerParams(vmem_limit_bytes=16 << 20)
VMEM = pl.BlockSpec(memory_space=pltpu.VMEM)
SMEM = pl.BlockSpec(memory_space=pltpu.SMEM)
BAND = 0.1
REACH = 8
BF = jnp.bfloat16
F32 = jnp.float32


def gam(l, m):
    return (l + m - 1) * (l - 1 - m) / ((2 * l - 1) * (2 * l - 3))


def tables():
    c = -1.0 + (2.0 * np.arange(NTH) + 1.0) / NTH
    f = (np.arange(NPHI) + 0.5) * (2 * np.pi / NPHI)
    z = np.repeat(c, NPHI)
    s = np.sqrt(1 - z * z)
    az = np.tile(f, NTH)
    x, y = s * np.cos(az), s * np.sin(az)
    cos, sin = [np.ones_like(x)], [np.zeros_like(x)]
    for m in range(1, DEGREE + 1):
        cos.append(cos[m - 1] * x - sin[m - 1] * y)
        sin.append(cos[m - 1] * y + sin[m - 1] * x)
    ys, scale, invert = np.zeros((LM, NG)), np.zeros(LM), np.zeros(LM)
    for m in range(DEGREE + 1):
        q, lead = {m: np.ones_like(x)}, {m: 1.0}
        for odd in range(1, 2 * m, 2):
            lead[m] *= odd
        for l in range(m + 1, DEGREE + 1):
            q[l] = z * q[l - 1] - (gam(l, m) * q[l - 2] if l > m + 1 else 0.0)
            lead[l] = lead[l - 1] * (2 * l - 1) / (l - m)
        for l in range(m, DEGREE + 1):
            n = math.sqrt(
                (2 * l + 1) / (4 * math.pi) * math.factorial(l - m) / math.factorial(l + m)
            )
            n *= math.sqrt(2.0) if m else 1.0
            for sign, trig in ((1, cos[m]), (-1, sin[m])):
                if m == 0 and sign < 0:
                    continue
                i = l * l + l + sign * m
                ys[i] = n * lead[l] * q[l] * trig
                scale[i] = n * lead[l] * 4 * math.pi / (2 * l + 1)
                invert[i] = (2 * l + 1) / (4 * math.pi)
    return np.stack([x, y, z]), ys, scale, invert


def split(a):
    a = np.asarray(a, np.float32)
    hi = a.astype(ml_dtypes.bfloat16)
    return hi, (a - hi.astype(np.float32)).astype(ml_dtypes.bfloat16)


def halves(x):
    hi = x.astype(BF)
    return hi, (x - hi.astype(F32)).astype(BF)


def pair_weights():
    dirs, ys, _, _ = tables()
    w = np.zeros((2 * NG, 2 * LP))
    wy = ys.T * (4 * math.pi / NG)
    w[:NG, :LM] = wy
    w[NG:, LP : LP + LM] = wy
    d = np.zeros((8, 2 * NG), np.float32)
    d[:3, :NG] = dirs
    d[:3, NG:] = dirs
    return np.concatenate(split(w), 1), d


def even_weights():
    _, ys, _, _ = tables()
    w = np.zeros((PN, 2 * LP))
    w[:NG, :LM] = ys.T
    w[NG:, LP : LP + LM] = ys.T
    return np.concatenate(split(w), 1), np.concatenate(split(w.T), 1)


def lane_scales():
    _, _, scale, invert = tables()
    rows = np.zeros((8, 2 * LP), np.float32)
    for h in (0, LP):
        rows[0, h : h + LM] = scale * invert
        rows[1, h : h + LM] = invert
    return rows


def chunk_piece(k, width, p):
    at = (lax.axis_index("fit") ^ k) * width + p * PIECE
    return pl.ds(pl.multiple_of(at, 128), PIECE)


def phi_kernel(width, far_coef_ref, far_ref, *rest):
    outs, (tile_ref, coef_ref, sem, coef_sem) = rest[:-4], rest[-4:]
    first = pltpu.make_async_copy(far_coef_ref, coef_ref, coef_sem)
    first.start()
    per = width // PIECE
    todo = [(k, p) for k in [*range(1, len(outs)), 0] for p in range(per)]
    copies = []
    for i, (k, p) in enumerate(todo):
        at = chunk_piece(k, width, p)
        copies.append(pltpu.make_async_copy(far_ref.at[:, at], tile_ref.at[:, at], sem.at[i]))
        copies[-1].start()
    first.wait()
    for (k, p), copy in zip(todo, copies):
        copy.wait()
        outs[k][:, p * PIECE : (p + 1) * PIECE] = jnp.dot(
            coef_ref[...], tile_ref[:, chunk_piece(k, width, p)], preferred_element_type=F32
        )


def phi_call(coefs, tiles, width):
    aux, points = tiles.shape
    count = points // width
    return pl.pallas_call(
        functools.partial(phi_kernel, width),
        in_specs=[pl.BlockSpec(memory_space=pltpu.HBM)] * 2,
        out_specs=[VMEM] * (count + 1),
        out_shape=[jax.ShapeDtypeStruct((NDENS, width), F32)] * count
        + [jax.ShapeDtypeStruct(tiles.shape, tiles.dtype)],
        scratch_shapes=[
            pltpu.VMEM(coefs.shape, coefs.dtype),
            pltpu.SemaphoreType.DMA((points // PIECE,)),
            pltpu.SemaphoreType.DMA,
        ],
        compiler_params=PARAMS,
        cost_estimate=pl.CostEstimate(
            flops=2 * NDENS * aux * points,
            bytes_accessed=(2 * aux + 4 * NDENS) * points,
            transcendentals=0,
        ),
        name="phi",
    )(*(pltpu.with_memory_space_constraint(a, pltpu.HBM) for a in (coefs, tiles)))


def pair_build(e, geo, mask, dir_ref, bh):
    lane = lax.broadcasted_iota(jnp.int32, (8, 128), 1)
    sub = lax.broadcasted_iota(jnp.int32, (8, 128), 0)
    own = jnp.broadcast_to(geo[pl.ds(e + 8, 1), :], (8, 128))
    mrow = jnp.broadcast_to(mask[pl.ds(e, 1), :], (8, 128))
    cols = []
    for g, start in ((0, e), (1, e + 9)):
        near = geo[pl.ds(start, 8), :]
        valid = jnp.sum(jnp.where(lane == sub + 8 * g, mrow, 0.0), axis=1, keepdims=True)
        on = valid > 0.0
        ir = 1.0 / jnp.where(on, near[:, 3:4], 1.0)
        off = jnp.where(on, own - near, 0.0)
        c = [off[:, 0:1] * ir, off[:, 1:2] * ir, off[:, 2:3] * ir, own[:, 3:4] * ir, valid]
        cols.append([jnp.broadcast_to(q, (8, 128)) for q in c])
    mid = [jnp.where(lane < 64, a, b) for a, b in zip(*cols)]
    sums = []
    for t in range(5):
        ox, oy, oz, q, valid = cols[0] if t < 2 else (mid if t == 2 else cols[1])
        ls = slice(128 * t, 128 * t + 128)
        x = ox + q * dir_ref[0:1, ls]
        y = oy + q * dir_ref[1:2, ls]
        z = oz + q * dir_ref[2:3, ls]
        r2 = x * x + y * y + z * z
        ramp = jnp.clip((1.0 - jnp.sqrt(r2)) * (1.0 / BAND), 0.0, 1.0)
        chi = ramp * ramp * (3.0 - 2.0 * ramp) * valid
        sums.append(jnp.sum(chi, axis=0, keepdims=True))
        cos, sin = [chi, chi * x], [None, chi * y]
        for m in range(2, DEGREE + 1):
            cos.append(cos[m - 1] * x - sin[m - 1] * y)
            sin.append(cos[m - 1] * y + sin[m - 1] * x)
        out = [None] * LM
        for m in range(DEGREE + 1):
            qm = {}
            for l in range(m, DEGREE + 1):
                if l == m + 1:
                    qm[l] = z
                elif l == m + 2:
                    qm[l] = z * z - gam(l, m) * r2
                elif l > m + 2:
                    qm[l] = z * qm[l - 1] - (gam(l, m) * r2) * qm[l - 2]
                for sign, trig in ((1, cos[m]), (-1, sin[m])):
                    if m == 0 and sign < 0:
                        continue
                    out[l * l + l + sign * m] = trig if l == m else trig * qm[l]
        out.append(jnp.zeros((8, 128), F32))
        for p in range(25):
            both = jnp.concatenate([out[2 * p], out[2 * p + 1]], axis=0)
            bh[16 * p : 16 * p + 16, ls] = both.astype(BF)
    return sums


def pair_finish(e, w_ref, t_ref, bh):
    r = jnp.dot(bh[...], w_ref[...], preferred_element_type=F32)
    tt = r[: LM * 8, : 2 * LP] + r[: LM * 8, 2 * LP :]
    a = jnp.swapaxes(tt.reshape(LM, 8, 2 * LP), 0, 1)
    a = jnp.concatenate([a, jnp.zeros((8, LP - LM, 2 * LP), F32)], 1).reshape(8 * LP, 2 * LP)
    hi, lo = halves(a)
    t_ref[e, :, : 2 * LP] = hi
    t_ref[e, :, 2 * LP :] = lo


def uncover(sums):
    low = lax.broadcasted_iota(jnp.int32, (1, 128), 1) < 64
    swap = lambda v: pltpu.roll(v, 64, 1)
    three = []
    for s in sums:
        r2, r3, r4 = swap(s[2]), swap(s[3]), swap(s[4])
        three.append([s[0] + jnp.where(low, r2, r3), s[1] + jnp.where(low, r3, r4), s[2] + r4])
    a, b = three
    b0, b1, b2 = swap(b[0]), swap(b[1]), swap(b[2])
    tiles = [a[0], a[1], jnp.where(low, a[2], b0), jnp.where(low, b0, b1), jnp.where(low, b1, b2)]
    return [jnp.maximum(0.0, 1.0 - t) for t in tiles]


def pair_kernel(before_ref, own_ref, after_ref, dir_ref, w_ref, t_ref, unc_ref, geo, mask, *bhs):
    spheres = own_ref.shape[1]
    slots = 2 * REACH
    wide = spheres + 2 * REACH
    rows = jnp.concatenate([before_ref[...], own_ref[...], after_ref[...]], axis=1)
    rows = jnp.concatenate([rows, jnp.zeros((rows.shape[0], 128 - rows.shape[1]), F32)], axis=1)
    rows = jnp.concatenate([rows, jnp.zeros((128 - rows.shape[0], 128), F32)], axis=0)
    geo[...] = rows.T[: geo.shape[0]]
    first = (lax.axis_index("sph") * lax.axis_size("fit") + lax.axis_index("fit")) * spheres
    row = lax.broadcasted_iota(jnp.int32, (wide, slots), 0) + (first - REACH)
    slot = lax.broadcasted_iota(jnp.int32, (wide, slots), 1)
    about = geo[spheres - REACH : 2 * spheres + REACH, :]
    rel = about[:, 4 : 4 + slots] - row.astype(F32)
    listed = slot.astype(F32) < about[:, 4 + slots : 5 + slots]
    lane = lax.broadcasted_iota(jnp.int32, (wide, 128), 1)
    found = jnp.zeros((wide, 128), F32)
    for c in range(slots):
        gap = c - REACH if c < REACH else c - REACH + 1
        hit = jnp.where(listed & (rel == float(gap)), 1.0, 0.0)
        hit = jnp.max(hit, axis=1, keepdims=True)
        found = jnp.where(lane == c, hit, found)
    mask[...] = found

    def step(b, carry):
        sums = []
        for u in range(QUAD):
            e = b * QUAD + u
            sums.append(pair_build(e, geo, mask, dir_ref, bhs[u]))
            pair_finish(e, w_ref, t_ref, bhs[u])
        tiles = uncover(sums[:2]) + uncover(sums[2:])
        for t, v in enumerate(tiles):
            unc_ref[b, :, 128 * t : 128 * t + 128] = v
        return carry

    lax.fori_loop(0, wide // QUAD, step, 0)


def pair_call(before, own, after):
    spheres = own.shape[1]
    wide = spheres + 2 * REACH
    w, d = pair_weights()
    return pl.pallas_call(
        pair_kernel,
        in_specs=[VMEM] * 5,
        out_specs=[VMEM] * 2,
        scratch_shapes=[pltpu.VMEM((3 * spheres, 128), F32), pltpu.VMEM((wide, 128), F32)]
        + [pltpu.VMEM((400, 2 * NG), BF)] * QUAD,
        out_shape=[
            jax.ShapeDtypeStruct((wide, 8 * LP, 4 * LP), BF),
            jax.ShapeDtypeStruct((wide // QUAD, 1, QN), F32),
        ],
        compiler_params=PARAMS,
        cost_estimate=pl.CostEstimate(
            flops=wide * 2 * 400 * 640 * 256, bytes_accessed=wide * 262144, transcendentals=0
        ),
        name="pairs",
    )(before, own, after, jnp.asarray(d), jnp.asarray(w))


def own_uncovered(unc_ref, b):
    b = b + REACH // 2
    return unc_ref[b // 2, :, b % 2 * PN : (b % 2 + 1) * PN]


def rhs_kernel(count, *refs):
    phis, (unc_ref, w_ref, out_ref) = refs[:count], refs[count:]
    pairs = out_ref.shape[1] // (2 * LP)
    rows = []
    for b in range(pairs):
        ls = slice(b * PN, (b + 1) * PN)
        total = phis[0][:, ls]
        for p in phis[1:]:
            total = total + p[:, ls]
        rows.append(total * own_uncovered(unc_ref, b))
    hi, lo = halves(jnp.concatenate(rows, 0))
    n = pairs * NDENS
    r = jnp.dot(jnp.concatenate([hi, lo], 0), w_ref[...], preferred_element_type=F32)
    out = r[:n, : 2 * LP] + r[:n, 2 * LP :] + r[n:, : 2 * LP]
    out = out * (-4.0 * math.pi / NG)
    for b in range(pairs):
        out_ref[:, b * 2 * LP : (b + 1) * 2 * LP] = out[b * NDENS : (b + 1) * NDENS]


def rhs_call(phis, unc, w):
    spheres = phis[0].shape[1] // NG
    return pl.pallas_call(
        functools.partial(rhs_kernel, len(phis)),
        in_specs=[VMEM] * (len(phis) + 2),
        out_specs=VMEM,
        compiler_params=PARAMS,
        out_shape=jax.ShapeDtypeStruct((NDENS, spheres * LP), F32),
        cost_estimate=pl.CostEstimate(
            flops=6 * NDENS * spheres * NG * 256, bytes_accessed=1700000, transcendentals=0
        ),
        name="rhs",
    )(*phis, unc, w)


def gather_field(t_ref, shift, x, xs, e):
    low = lax.broadcasted_iota(jnp.int32, (NDENS, 128), 1) < LP
    parts = []
    for odd in (0, 1):
        below, above = (x, xs) if odd == 0 else (xs, x)
        lo_at = e * LP
        up_at = (e + 8) * LP if odd == 0 else (e + 10) * LP
        lhs = jnp.concatenate(
            [below[:, lo_at : lo_at + 8 * LP], above[:, up_at : up_at + 8 * LP]], 0
        )
        r = jnp.dot(lhs, t_ref[e + odd + shift], preferred_element_type=F32)
        n = NDENS
        a = r[0:n, : 2 * LP] + r[n : 2 * n, : 2 * LP] + r[0:n, 2 * LP :]
        b = r[2 * n : 3 * n, : 2 * LP] + r[3 * n :, : 2 * LP] + r[2 * n : 3 * n, 2 * LP :]
        parts.append((a, b))
    (a0, b0), (a1, b1) = parts
    return jnp.where(low, a0, b1) + pltpu.roll(jnp.where(low, a1, b0), LP, 1)


def put_scaled(x, at, value):
    hi, lo = halves(value)
    x[0:NDENS, at : at + 128] = hi
    x[NDENS:, at : at + 128] = lo


def put_shifted(xs, x):
    v = x[...].astype(F32)
    xs[...] = jnp.concatenate([v[:, LP:], v[:, :LP]], 1).astype(BF)


def sweep_kernel(
    before_ref, own_ref, after_ref, t_ref, sc_ref, unc_ref, y_ref,
    m_ref, out_ref, x, xs, z, zs
):
    own = own_ref.shape[1]
    spheres = own // LP
    right = lambda at: (before_ref, own_ref, after_ref)[at // own][:, at % own : at % own + 128]
    for at in range(0, 3 * own, 128):
        put_scaled(x, at, right(at) * sc_ref[0:1, :])
    put_shifted(xs, x)
    for e in range(0, spheres + 2 * REACH, 2):
        new = right((e + spheres - REACH) * LP) + gather_field(t_ref, 0, x, xs, e)
        put_scaled(z, e * LP, new * sc_ref[0:1, :])
    put_shifted(zs, z)
    rows = []
    for e in range(0, spheres, 2):
        new = own_ref[:, e * LP : e * LP + 128] + gather_field(t_ref, REACH, z, zs, e)
        new = new * sc_ref[1:2, :]
        m_ref[e] = new[:, :LM]
        m_ref[e + 1] = pltpu.roll(new, LP, 1)[:, :LM]
        rows.append(new)
    hi, lo = halves(jnp.concatenate(rows, 0))
    n = len(rows) * NDENS
    r = jnp.dot(jnp.concatenate([hi, lo], 0), y_ref[...], preferred_element_type=F32)
    out = r[:n, :PN] + r[:n, PN:] + r[n:, :PN]
    for b in range(len(rows)):
        weight = own_uncovered(unc_ref, b) * (4.0 * math.pi / NG)
        out_ref[:, b * PN : (b + 1) * PN] = (out[b * NDENS : (b + 1) * NDENS] * weight).astype(BF)


def sweep_call(before, own, after, t, scales, unc, wt):
    lanes = own.shape[1]
    spheres = lanes // LP
    return pl.pallas_call(
        sweep_kernel,
        in_specs=[VMEM] * 7,
        out_specs=[VMEM] * 2,
        out_shape=[
            jax.ShapeDtypeStruct((spheres, NDENS, LM), F32),
            jax.ShapeDtypeStruct((NDENS, spheres * NG), BF),
        ],
        scratch_shapes=[pltpu.VMEM((2 * NDENS, 3 * lanes), BF)] * 2
        + [pltpu.VMEM((2 * NDENS, lanes + 2 * REACH * LP), BF)] * 2,
        compiler_params=PARAMS,
        cost_estimate=pl.CostEstimate(
            flops=3 * spheres * 2 * 64 * 512 * 256,
            bytes_accessed=2 * spheres * 262144,
            transcendentals=0,
        ),
        name="sweeps",
    )(before, own, after, t, scales, unc, wt)


def fock_kernel(k, width, charge_ref, tile_ref, *rest):
    total = rest[0][...] if len(rest) == 2 else None
    for p in range(width // PIECE):
        part = lax.dot_general(
            charge_ref[:, p * PIECE : (p + 1) * PIECE],
            tile_ref[:, chunk_piece(k, width, p)],
            (((1,), (1,)), ((), ())),
            preferred_element_type=F32,
        )
        total = part if total is None else total + part
    rest[-1][...] = total


def fock_call(k, charges, tiles, before=None):
    aux = tiles.shape[0]
    width = charges.shape[1]
    more = [] if before is None else [before]
    return pl.pallas_call(
        functools.partial(fock_kernel, k, width),
        in_specs=[VMEM] * (2 + len(more)),
        out_specs=VMEM,
        out_shape=jax.ShapeDtypeStruct((NDENS, aux), F32),
        compiler_params=PARAMS,
        cost_estimate=pl.CostEstimate(
            flops=2 * NDENS * aux * width, bytes_accessed=2 * aux * width, transcendentals=0
        ),
        name="fock",
    )(charges, tiles, *more)


def trade(x, axis, k):
    count = lax.axis_size(axis)
    return lax.ppermute(x, axis, [(i, i ^ k) for i in range(count)])


def from_beside(x):
    axes = ("sph", "fit")
    count = lax.axis_size("sph") * lax.axis_size("fit")
    up = [(i, (i + 1) % count) for i in range(count)]
    down = [((i + 1) % count, i) for i in range(count)]
    return lax.ppermute(x, axes, up), lax.ppermute(x, axes, down)


def body(tiles, coefs, centres, radii, neighbours, counts):
    spheres, slots = neighbours.shape
    fits = lax.axis_size("fit")
    sphs = lax.axis_size("sph")
    assert fits & (fits - 1) == 0 and sphs & (sphs - 1) == 0
    assert spheres % (2 * QUAD) == 0 and spheres == slots == 2 * REACH
    w, wt = (jnp.asarray(a) for a in even_weights())
    scales = jnp.asarray(lane_scales())

    own = [centres, radii[None, :], neighbours.T.astype(F32), counts[None, :].astype(F32)]
    own = jnp.concatenate(own + [jnp.zeros((3, spheres), F32)], axis=0)
    before, after = from_beside(own)
    *phis, near_tiles = phi_call(coefs, tiles, spheres * NG)
    phis, before, after = lax.optimization_barrier((phis, before, after))
    got = [trade(phis[k], "fit", k) for k in range(1, fits)]
    t, unc = pair_call(before, own, after)
    rhs = rhs_call([phis[0], *got], unc, w)
    below, above = from_beside(rhs)
    moments, charges = sweep_call(below, rhs, above, t, scales, unc, wt)
    others = [trade(charges, "fit", k) for k in range(1, fits)]
    fock = fock_call(0, charges, near_tiles)
    for k in range(1, fits):
        fock = fock_call(k, others[k - 1], near_tiles, fock)
    fock = fock + trade(fock, "sph", 1)
    bit = 2
    while bit < sphs:
        ks = [k for k in (bit, 2 * bit, 3 * bit) if k < sphs]
        fock = functools.reduce(jnp.add, [trade(fock, "sph", k) for k in ks], fock)
        bit *= 4
    return moments, fock


def solution(mesh):
    placed = (
        P("fit", "sph"),
        P(None, "fit"),
        P(None, ("sph", "fit")),
        P(("sph", "fit")),
        P(("sph", "fit"), None),
        P(("sph", "fit")),
    )
    return jax.shard_map(
        body,
        mesh=mesh,
        in_specs=placed,
        out_specs=(P(("sph", "fit"), None, None), P(None, "fit")),
        check_vma=False,
    )
```

```python
import functools
import math

import jax
import jax.numpy as jnp
import ml_dtypes
import numpy as np
from jax import lax
from jax.experimental import pallas as pl
from jax.experimental.pallas import tpu as pltpu
from jax.sharding import PartitionSpec as P

DEGREE = 6
LM = 49
NTH = 16
NPHI = 20
NG = 320
NDENS = 16
LP = 64
QUAD = 4
QN = QUAD * NG
PN = 2 * NG
PIECE = 2560
PARAMS = pltpu.CompilerParams(vmem_limit_bytes=16 << 20)
VMEM = pl.BlockSpec(memory_space=pltpu.VMEM)
SMEM = pl.BlockSpec(memory_space=pltpu.SMEM)
BAND = 0.1
REACH = 8
BF = jnp.bfloat16
F32 = jnp.float32


def gam(l, m):
    return (l + m - 1) * (l - 1 - m) / ((2 * l - 1) * (2 * l - 3))


def tables():
    c = -1.0 + (2.0 * np.arange(NTH) + 1.0) / NTH
    f = (np.arange(NPHI) + 0.5) * (2 * np.pi / NPHI)
    z = np.repeat(c, NPHI)
    s = np.sqrt(1 - z * z)
    az = np.tile(f, NTH)
    x, y = s * np.cos(az), s * np.sin(az)
    cos, sin = [np.ones_like(x)], [np.zeros_like(x)]
    for m in range(1, DEGREE + 1):
        cos.append(cos[m - 1] * x - sin[m - 1] * y)
        sin.append(cos[m - 1] * y + sin[m - 1] * x)
    ys, scale, invert = np.zeros((LM, NG)), np.zeros(LM), np.zeros(LM)
    for m in range(DEGREE + 1):
        q, lead = {m: np.ones_like(x)}, {m: 1.0}
        for odd in range(1, 2 * m, 2):
            lead[m] *= odd
        for l in range(m + 1, DEGREE + 1):
            q[l] = z * q[l - 1] - (gam(l, m) * q[l - 2] if l > m + 1 else 0.0)
            lead[l] = lead[l - 1] * (2 * l - 1) / (l - m)
        for l in range(m, DEGREE + 1):
            n = math.sqrt(
                (2 * l + 1) / (4 * math.pi) * math.factorial(l - m) / math.factorial(l + m)
            )
            n *= math.sqrt(2.0) if m else 1.0
            for sign, trig in ((1, cos[m]), (-1, sin[m])):
                if m == 0 and sign < 0:
                    continue
                i = l * l + l + sign * m
                ys[i] = n * lead[l] * q[l] * trig
                scale[i] = n * lead[l] * 4 * math.pi / (2 * l + 1)
                invert[i] = (2 * l + 1) / (4 * math.pi)
    return np.stack([x, y, z]), ys, scale, invert


def split(a):
    a = np.asarray(a, np.float32)
    hi = a.astype(ml_dtypes.bfloat16)
    return hi, (a - hi.astype(np.float32)).astype(ml_dtypes.bfloat16)


def halves(x):
    hi = x.astype(BF)
    return hi, (x - hi.astype(F32)).astype(BF)


def pair_weights():
    dirs, ys, _, _ = tables()
    w = np.zeros((2 * NG, 2 * LP))
    wy = ys.T * (4 * math.pi / NG)
    w[:NG, :LM] = wy
    w[NG:, LP : LP + LM] = wy
    d = np.zeros((8, 2 * NG), np.float32)
    d[:3, :NG] = dirs
    d[:3, NG:] = dirs
    return np.concatenate(split(w), 1), d


def even_weights():
    _, ys, _, _ = tables()
    w = np.zeros((PN, 2 * LP))
    w[:NG, :LM] = ys.T
    w[NG:, LP : LP + LM] = ys.T
    return np.concatenate(split(w), 1), np.concatenate(split(w.T), 1)


def lane_scales():
    _, _, scale, invert = tables()
    rows = np.zeros((8, 2 * LP), np.float32)
    for h in (0, LP):
        rows[0, h : h + LM] = scale * invert
        rows[1, h : h + LM] = invert
    return rows


def chunk_piece(k, width, p):
    at = (lax.axis_index("fit") ^ k) * width + p * PIECE
    return pl.ds(pl.multiple_of(at, 128), PIECE)


def code(x):
    top = jnp.maximum(jnp.max(jnp.abs(x), axis=1, keepdims=True), 1e-30)
    power = jnp.floor(jnp.log2(top)) - 13.0
    q = jnp.floor(x * jnp.exp2(-power) + 0.5).astype(jnp.int32)
    tail = jnp.broadcast_to(power, (x.shape[0], 128)).astype(jnp.int32)
    return q.astype(jnp.int16), tail.astype(jnp.int16)


def decode(ref, ls):
    width = ref.shape[1] - 128
    power = ref[:, width:].astype(jnp.int32).astype(F32)[:, 0:1]
    return ref[:, ls].astype(jnp.int32).astype(F32) * jnp.exp2(power)


def phi_kernel(width, far_coef_ref, far_ref, *rest):
    outs, (tile_ref, full, coef_ref, sem, coef_sem) = rest[:-5], rest[-5:]
    first = pltpu.make_async_copy(far_coef_ref, coef_ref, coef_sem)
    first.start()
    per = width // PIECE
    todo = [(k, p) for k in [*range(1, len(outs)), 0] for p in range(per)]
    copies = []
    for i, (k, p) in enumerate(todo):
        at = chunk_piece(k, width, p)
        copies.append(pltpu.make_async_copy(far_ref.at[:, at], tile_ref.at[:, at], sem.at[i]))
        copies[-1].start()
    first.wait()
    for (k, p), copy in zip(todo, copies):
        copy.wait()
        out = full if k else outs[0]
        out[:, p * PIECE : (p + 1) * PIECE] = jnp.dot(
            coef_ref[...], tile_ref[:, chunk_piece(k, width, p)], preferred_element_type=F32
        )
        if k and p == per - 1:
            q, tail = code(full[...])
            outs[k][:, :width] = q
            outs[k][:, width:] = tail


def phi_call(coefs, tiles, width):
    aux, points = tiles.shape
    count = points // width
    return pl.pallas_call(
        functools.partial(phi_kernel, width),
        in_specs=[pl.BlockSpec(memory_space=pltpu.HBM)] * 2,
        out_specs=[VMEM] * (count + 1),
        out_shape=[jax.ShapeDtypeStruct((NDENS, width), F32)]
        + [jax.ShapeDtypeStruct((NDENS, width + 128), jnp.int16)] * (count - 1)
        + [jax.ShapeDtypeStruct(tiles.shape, tiles.dtype)],
        scratch_shapes=[
            pltpu.VMEM((NDENS, width), F32),
            pltpu.VMEM(coefs.shape, coefs.dtype),
            pltpu.SemaphoreType.DMA((points // PIECE,)),
            pltpu.SemaphoreType.DMA,
        ],
        compiler_params=PARAMS,
        cost_estimate=pl.CostEstimate(
            flops=2 * NDENS * aux * points,
            bytes_accessed=(2 * aux + 4 * NDENS) * points,
            transcendentals=0,
        ),
        name="phi",
    )(*(pltpu.with_memory_space_constraint(a, pltpu.HBM) for a in (coefs, tiles)))


def pack_kernel(centre_ref, radius_ref, nbr_ref, cnt_ref, out_ref, c, r, n, k, sem):
    copies = [
        pltpu.make_async_copy(a, b, sem.at[i])
        for i, (a, b) in enumerate(zip((centre_ref, radius_ref, nbr_ref, cnt_ref), (c, r, n, k)))
    ]
    for copy in copies:
        copy.start()
    for copy in copies:
        copy.wait()
    spheres, slots = n.shape
    out_ref[...] = jnp.zeros_like(out_ref)
    out_ref[0:3, :] = c[...]
    out_ref[3:4, :] = r[...]
    out_ref[4:5, :] = k[...].astype(F32)
    out_ref[8:, :] = n[...].astype(F32)


def pack_call(centres, radii, neighbours, counts):
    spheres, slots = neighbours.shape
    args = (centres, radii.reshape(1, spheres), neighbours, counts.reshape(1, spheres))
    return pl.pallas_call(
        pack_kernel,
        in_specs=[pl.BlockSpec(memory_space=pltpu.HBM)] * 4,
        out_specs=VMEM,
        out_shape=jax.ShapeDtypeStruct((8 + spheres, spheres), F32),
        scratch_shapes=[pltpu.VMEM(a.shape, a.dtype) for a in args]
        + [pltpu.SemaphoreType.DMA((4,))],
        compiler_params=PARAMS,
        name="pack",
    )(*(pltpu.with_memory_space_constraint(a, pltpu.HBM) for a in args))


def pair_build(e, geo, mask, dir_ref, bh):
    lane = lax.broadcasted_iota(jnp.int32, (8, 128), 1)
    sub = lax.broadcasted_iota(jnp.int32, (8, 128), 0)
    own = jnp.broadcast_to(geo[pl.ds(e + 8, 1), :], (8, 128))
    mrow = jnp.broadcast_to(mask[pl.ds(e, 1), :], (8, 128))
    cols = []
    for g, start in ((0, e), (1, e + 9)):
        near = geo[pl.ds(start, 8), :]
        valid = jnp.sum(jnp.where(lane == sub + 8 * g, mrow, 0.0), axis=1, keepdims=True)
        on = valid > 0.0
        ir = 1.0 / jnp.where(on, near[:, 3:4], 1.0)
        off = jnp.where(on, own - near, 0.0)
        c = [off[:, 0:1] * ir, off[:, 1:2] * ir, off[:, 2:3] * ir, own[:, 3:4] * ir, valid]
        cols.append([jnp.broadcast_to(q, (8, 128)) for q in c])
    mid = [jnp.where(lane < 64, a, b) for a, b in zip(*cols)]
    sums = []
    for t in range(5):
        ox, oy, oz, q, valid = cols[0] if t < 2 else (mid if t == 2 else cols[1])
        ls = slice(128 * t, 128 * t + 128)
        x = ox + q * dir_ref[0:1, ls]
        y = oy + q * dir_ref[1:2, ls]
        z = oz + q * dir_ref[2:3, ls]
        r2 = x * x + y * y + z * z
        ramp = jnp.clip((1.0 - jnp.sqrt(r2)) * (1.0 / BAND), 0.0, 1.0)
        chi = ramp * ramp * (3.0 - 2.0 * ramp) * valid
        sums.append(jnp.sum(chi, axis=0, keepdims=True))
        cos, sin = [chi, chi * x], [None, chi * y]
        for m in range(2, DEGREE + 1):
            cos.append(cos[m - 1] * x - sin[m - 1] * y)
            sin.append(cos[m - 1] * y + sin[m - 1] * x)
        out = [None] * LM
        for m in range(DEGREE + 1):
            qm = {}
            for l in range(m, DEGREE + 1):
                if l == m + 1:
                    qm[l] = z
                elif l == m + 2:
                    qm[l] = z * z - gam(l, m) * r2
                elif l > m + 2:
                    qm[l] = z * qm[l - 1] - (gam(l, m) * r2) * qm[l - 2]
                for sign, trig in ((1, cos[m]), (-1, sin[m])):
                    if m == 0 and sign < 0:
                        continue
                    out[l * l + l + sign * m] = trig if l == m else trig * qm[l]
        out.append(jnp.zeros((8, 128), F32))
        for p in range(25):
            both = jnp.concatenate([out[2 * p], out[2 * p + 1]], axis=0)
            bh[16 * p : 16 * p + 16, ls] = both.astype(BF)
    return sums


def pair_finish(e, w_ref, t_ref, bh):
    r = jnp.dot(bh[...], w_ref[...], preferred_element_type=F32)
    tt = r[: LM * 8, : 2 * LP] + r[: LM * 8, 2 * LP :]
    a = jnp.swapaxes(tt.reshape(LM, 8, 2 * LP), 0, 1)
    a = jnp.concatenate([a, jnp.zeros((8, LP - LM, 2 * LP), F32)], 1).reshape(8 * LP, 2 * LP)
    hi, lo = halves(a)
    t_ref[e, :, : 2 * LP] = hi
    t_ref[e, :, 2 * LP :] = lo


def uncover(sums):
    low = lax.broadcasted_iota(jnp.int32, (1, 128), 1) < 64
    swap = lambda v: pltpu.roll(v, 64, 1)
    three = []
    for s in sums:
        r2, r3, r4 = swap(s[2]), swap(s[3]), swap(s[4])
        three.append([s[0] + jnp.where(low, r2, r3), s[1] + jnp.where(low, r3, r4), s[2] + r4])
    a, b = three
    b0, b1, b2 = swap(b[0]), swap(b[1]), swap(b[2])
    tiles = [a[0], a[1], jnp.where(low, a[2], b0), jnp.where(low, b0, b1), jnp.where(low, b1, b2)]
    return [jnp.maximum(0.0, 1.0 - t) for t in tiles]


def pair_kernel(before_ref, own_ref, after_ref, dir_ref, w_ref, t_ref, unc_ref, geo, mask, *bhs):
    spheres = own_ref.shape[1]
    slots = 2 * REACH
    wide = spheres + 2 * REACH
    packs = (before_ref, own_ref, after_ref)
    rows = jnp.concatenate([p[0:8, :] for p in packs], axis=1)
    rows = jnp.concatenate([rows, jnp.zeros((8, 128 - rows.shape[1]), F32)], axis=1)
    rows = jnp.concatenate([rows, jnp.zeros((120, 128), F32)], axis=0)
    geo[...] = rows.T[: geo.shape[0]]
    first = (lax.axis_index("sph") * lax.axis_size("fit") + lax.axis_index("fit")) * spheres
    row = lax.broadcasted_iota(jnp.int32, (wide, slots), 0) + (first - REACH)
    slot = lax.broadcasted_iota(jnp.int32, (wide, slots), 1)
    lists = [before_ref[8 + spheres - REACH :, :], own_ref[8:, :], after_ref[8 : 8 + REACH, :]]
    rel = jnp.concatenate(lists, axis=0) - row.astype(F32)
    listed = slot.astype(F32) < geo[spheres - REACH : 2 * spheres + REACH, 4:5]
    lane = lax.broadcasted_iota(jnp.int32, (wide, 128), 1)
    found = jnp.zeros((wide, 128), F32)
    for c in range(slots):
        gap = c - REACH if c < REACH else c - REACH + 1
        hit = jnp.where(listed & (rel == float(gap)), 1.0, 0.0)
        hit = jnp.max(hit, axis=1, keepdims=True)
        found = jnp.where(lane == c, hit, found)
    mask[...] = found

    def step(b, carry):
        sums = []
        for u in range(QUAD):
            e = b * QUAD + u
            sums.append(pair_build(e, geo, mask, dir_ref, bhs[u]))
            pair_finish(e, w_ref, t_ref, bhs[u])
        tiles = uncover(sums[:2]) + uncover(sums[2:])
        for t, v in enumerate(tiles):
            unc_ref[b, :, 128 * t : 128 * t + 128] = v
        return carry

    lax.fori_loop(0, wide // QUAD, step, 0, unroll=8)


def pair_call(before, own, after):
    spheres = own.shape[1]
    wide = spheres + 2 * REACH
    w, d = pair_weights()
    return pl.pallas_call(
        pair_kernel,
        in_specs=[VMEM] * 5,
        out_specs=[VMEM] * 2,
        scratch_shapes=[pltpu.VMEM((3 * spheres, 128), F32), pltpu.VMEM((wide, 128), F32)]
        + [pltpu.VMEM((400, 2 * NG), BF)] * QUAD,
        out_shape=[
            jax.ShapeDtypeStruct((wide, 8 * LP, 4 * LP), BF),
            jax.ShapeDtypeStruct((wide // QUAD, 1, QN), F32),
        ],
        compiler_params=PARAMS,
        cost_estimate=pl.CostEstimate(
            flops=wide * 2 * 400 * 640 * 256, bytes_accessed=wide * 262144, transcendentals=0
        ),
        name="pairs",
    )(before, own, after, jnp.asarray(d), jnp.asarray(w))


def own_uncovered(unc_ref, b):
    b = b + REACH // 2
    return unc_ref[b // 2, :, b % 2 * PN : (b % 2 + 1) * PN]


def rhs_kernel(count, *refs):
    phis, (unc_ref, w_ref, out_ref) = refs[:count], refs[count:]
    pairs = out_ref.shape[1] // (2 * LP)
    rows = []
    for b in range(pairs):
        ls = slice(b * PN, (b + 1) * PN)
        total = phis[0][:, ls]
        for p in phis[1:]:
            total = total + decode(p, ls)
        rows.append(total * own_uncovered(unc_ref, b))
    hi, lo = halves(jnp.concatenate(rows, 0))
    n = pairs * NDENS
    r = jnp.dot(jnp.concatenate([hi, lo], 0), w_ref[...], preferred_element_type=F32)
    out = r[:n, : 2 * LP] + r[:n, 2 * LP :] + r[n:, : 2 * LP]
    out = out * (-4.0 * math.pi / NG)
    for b in range(pairs):
        out_ref[:, b * 2 * LP : (b + 1) * 2 * LP] = out[b * NDENS : (b + 1) * NDENS]


def rhs_call(phis, unc, w):
    spheres = phis[0].shape[1] // NG
    return pl.pallas_call(
        functools.partial(rhs_kernel, len(phis)),
        in_specs=[VMEM] * (len(phis) + 2),
        out_specs=VMEM,
        compiler_params=PARAMS,
        out_shape=jax.ShapeDtypeStruct((NDENS, spheres * LP), F32),
        cost_estimate=pl.CostEstimate(
            flops=6 * NDENS * spheres * NG * 256, bytes_accessed=1700000, transcendentals=0
        ),
        name="rhs",
    )(*phis, unc, w)


def gather_field(t_ref, shift, x, xs, e):
    low = lax.broadcasted_iota(jnp.int32, (NDENS, 128), 1) < LP
    parts = []
    for odd in (0, 1):
        below, above = (x, xs) if odd == 0 else (xs, x)
        lo_at = e * LP
        up_at = (e + 8) * LP if odd == 0 else (e + 10) * LP
        lhs = jnp.concatenate(
            [below[:, lo_at : lo_at + 8 * LP], above[:, up_at : up_at + 8 * LP]], 0
        )
        r = jnp.dot(lhs, t_ref[e + odd + shift], preferred_element_type=F32)
        n = NDENS
        a = r[0:n, : 2 * LP] + r[n : 2 * n, : 2 * LP] + r[0:n, 2 * LP :]
        b = r[2 * n : 3 * n, : 2 * LP] + r[3 * n :, : 2 * LP] + r[2 * n : 3 * n, 2 * LP :]
        parts.append((a, b))
    (a0, b0), (a1, b1) = parts
    return jnp.where(low, a0, b1) + pltpu.roll(jnp.where(low, a1, b0), LP, 1)


def put_scaled(x, at, value):
    hi, lo = halves(value)
    x[0:NDENS, at : at + 128] = hi
    x[NDENS:, at : at + 128] = lo


def put_shifted(xs, x):
    v = x[...].astype(F32)
    xs[...] = jnp.concatenate([v[:, LP:], v[:, :LP]], 1).astype(BF)


def sweep_kernel(
    before_ref, own_ref, after_ref, t_ref, sc_ref, unc_ref, m_ref, out_ref, x, xs, z, zs
):
    own = own_ref.shape[1]
    spheres = own // LP
    right = lambda at: (before_ref, own_ref, after_ref)[at // own][:, at % own : at % own + 128]
    for at in range(0, 3 * own, 128):
        put_scaled(x, at, right(at) * sc_ref[0:1, :])
    put_shifted(xs, x)
    for e in range(0, spheres + 2 * REACH, 2):
        new = right((e + spheres - REACH) * LP) + gather_field(t_ref, 0, x, xs, e)
        put_scaled(z, e * LP, new * sc_ref[0:1, :])
    put_shifted(zs, z)
    for e in range(0, spheres, 2):
        new = own_ref[:, e * LP : e * LP + 128] + gather_field(t_ref, REACH, z, zs, e)
        new = new * sc_ref[1:2, :]
        m_ref[e] = new[:, :LM]
        m_ref[e + 1] = pltpu.roll(new, LP, 1)[:, :LM]
        out_ref[:, e * LP : e * LP + 128] = new
    out_ref[:, own:] = jnp.zeros((NDENS, 384), F32)
    pairs = spheres // 2
    for b in range(pairs):
        part = own_uncovered(unc_ref, b)
        out_ref[b : b + 1, own:] = part[:, :384]
        out_ref[pairs + b : pairs + b + 1, own : own + 256] = part[:, 384:]


def sweep_call(before, own, after, t, scales, unc):
    lanes = own.shape[1]
    spheres = lanes // LP
    return pl.pallas_call(
        sweep_kernel,
        in_specs=[VMEM] * 6,
        out_specs=[VMEM] * 2,
        out_shape=[
            jax.ShapeDtypeStruct((spheres, NDENS, LM), F32),
            jax.ShapeDtypeStruct((NDENS, lanes + 384), F32),
        ],
        scratch_shapes=[pltpu.VMEM((2 * NDENS, 3 * lanes), BF)] * 2
        + [pltpu.VMEM((2 * NDENS, lanes + 2 * REACH * LP), BF)] * 2,
        compiler_params=PARAMS,
        cost_estimate=pl.CostEstimate(
            flops=3 * spheres * 2 * 64 * 512 * 256,
            bytes_accessed=2 * spheres * 262144,
            transcendentals=0,
        ),
        name="sweeps",
    )(before, own, after, t, scales, unc)


def fock_kernel(k, pay_ref, y_ref, tile_ref, *rest):
    out_ref, charge = rest[-2:]
    own = pay_ref.shape[1] - 384
    pairs = own // (2 * LP)
    width = pairs * PN
    rows = [pay_ref[:, b * 2 * LP : (b + 1) * 2 * LP] for b in range(pairs)]
    hi, lo = halves(jnp.concatenate(rows, 0))
    n = pairs * NDENS
    r = jnp.dot(jnp.concatenate([hi, lo], 0), y_ref[...], preferred_element_type=F32)
    out = r[:n, :PN] + r[:n, PN:] + r[n:, :PN]
    for b in range(pairs):
        unc = jnp.concatenate(
            [pay_ref[b : b + 1, own:], pay_ref[pairs + b : pairs + b + 1, own : own + 256]], 1
        )
        weight = unc * (4.0 * math.pi / NG)
        charge[:, b * PN : (b + 1) * PN] = (out[b * NDENS : (b + 1) * NDENS] * weight).astype(BF)
    total = rest[0][...] if len(rest) == 3 else None
    for p in range(width // PIECE):
        part = lax.dot_general(
            charge[:, p * PIECE : (p + 1) * PIECE],
            tile_ref[:, chunk_piece(k, width, p)],
            (((1,), (1,)), ((), ())),
            preferred_element_type=F32,
        )
        total = part if total is None else total + part
    out_ref[...] = total


def fock_call(k, pay, wt, tiles, width, before=None):
    aux = tiles.shape[0]
    more = [] if before is None else [before]
    return pl.pallas_call(
        functools.partial(fock_kernel, k),
        in_specs=[VMEM] * (3 + len(more)),
        out_specs=VMEM,
        out_shape=jax.ShapeDtypeStruct((NDENS, aux), F32),
        scratch_shapes=[pltpu.VMEM((NDENS, width), BF)],
        compiler_params=PARAMS,
        cost_estimate=pl.CostEstimate(
            flops=2 * NDENS * aux * width, bytes_accessed=2 * aux * width, transcendentals=0
        ),
        name="fock",
    )(pay, wt, tiles, *more)


def trade(x, axis, k):
    count = lax.axis_size(axis)
    return lax.ppermute(x, axis, [(i, i ^ k) for i in range(count)])


def from_beside(x):
    axes = ("sph", "fit")
    count = lax.axis_size("sph") * lax.axis_size("fit")
    up = [(i, (i + 1) % count) for i in range(count)]
    down = [((i + 1) % count, i) for i in range(count)]
    return lax.ppermute(x, axes, up), lax.ppermute(x, axes, down)


def body(tiles, coefs, centres, radii, neighbours, counts):
    spheres, slots = neighbours.shape
    fits = lax.axis_size("fit")
    sphs = lax.axis_size("sph")
    assert fits & (fits - 1) == 0 and sphs & (sphs - 1) == 0
    assert spheres % (2 * QUAD) == 0 and spheres == slots == 2 * REACH
    w, wt = (jnp.asarray(a) for a in even_weights())
    scales = jnp.asarray(lane_scales())

    width = spheres * NG
    own = pack_call(centres, radii, neighbours, counts)
    before, after = from_beside(own)
    *phis, near_tiles = phi_call(coefs, tiles, width)
    phis, before, after = lax.optimization_barrier((phis, before, after))
    got = [trade(phis[k], "fit", k) for k in range(1, fits)]
    t, unc = pair_call(before, own, after)
    rhs = rhs_call([phis[0], *got], unc, w)
    below, above = from_beside(rhs)
    moments, pay = sweep_call(below, rhs, above, t, scales, unc)
    others = [trade(pay, "fit", k) for k in range(1, fits)]
    fock = fock_call(0, pay, wt, near_tiles, width)
    for k in range(1, fits):
        fock = fock_call(k, others[k - 1], wt, near_tiles, width, fock)
    fock = fock + trade(fock, "sph", 1)
    bit = 2
    while bit < sphs:
        ks = [k for k in (bit, 2 * bit, 3 * bit) if k < sphs]
        fock = functools.reduce(jnp.add, [trade(fock, "sph", k) for k in ks], fock)
        bit *= 4
    return moments, fock


def solution(mesh):
    placed = (
        P("fit", "sph"),
        P(None, "fit"),
        P(None, ("sph", "fit")),
        P(("sph", "fit")),
        P(("sph", "fit"), None),
        P(("sph", "fit")),
    )
    return jax.shard_map(
        body,
        mesh=mesh,
        in_specs=placed,
        out_specs=(P(("sph", "fit"), None, None), P(None, "fit")),
        check_vma=False,
    )
```

```python
import functools
import math

import jax
import jax.numpy as jnp
import ml_dtypes
import numpy as np
from jax import lax
from jax.experimental import pallas as pl
from jax.experimental.pallas import tpu as pltpu
from jax.sharding import PartitionSpec as P

DEGREE = 6
LM = 49
NTH = 16
NPHI = 20
NG = 320
NDENS = 16
LP = 64
QUAD = 4
QN = QUAD * NG
PN = 2 * NG
PIECE = 2560
PARAMS = pltpu.CompilerParams(vmem_limit_bytes=16 << 20)
VMEM = pl.BlockSpec(memory_space=pltpu.VMEM)
SMEM = pl.BlockSpec(memory_space=pltpu.SMEM)
BAND = 0.1
REACH = 8
BF = jnp.bfloat16
F32 = jnp.float32


def gam(l, m):
    return (l + m - 1) * (l - 1 - m) / ((2 * l - 1) * (2 * l - 3))


def tables():
    c = -1.0 + (2.0 * np.arange(NTH) + 1.0) / NTH
    f = (np.arange(NPHI) + 0.5) * (2 * np.pi / NPHI)
    z = np.repeat(c, NPHI)
    s = np.sqrt(1 - z * z)
    az = np.tile(f, NTH)
    x, y = s * np.cos(az), s * np.sin(az)
    cos, sin = [np.ones_like(x)], [np.zeros_like(x)]
    for m in range(1, DEGREE + 1):
        cos.append(cos[m - 1] * x - sin[m - 1] * y)
        sin.append(cos[m - 1] * y + sin[m - 1] * x)
    ys, scale, invert = np.zeros((LM, NG)), np.zeros(LM), np.zeros(LM)
    for m in range(DEGREE + 1):
        q, lead = {m: np.ones_like(x)}, {m: 1.0}
        for odd in range(1, 2 * m, 2):
            lead[m] *= odd
        for l in range(m + 1, DEGREE + 1):
            q[l] = z * q[l - 1] - (gam(l, m) * q[l - 2] if l > m + 1 else 0.0)
            lead[l] = lead[l - 1] * (2 * l - 1) / (l - m)
        for l in range(m, DEGREE + 1):
            n = math.sqrt(
                (2 * l + 1) / (4 * math.pi) * math.factorial(l - m) / math.factorial(l + m)
            )
            n *= math.sqrt(2.0) if m else 1.0
            for sign, trig in ((1, cos[m]), (-1, sin[m])):
                if m == 0 and sign < 0:
                    continue
                i = l * l + l + sign * m
                ys[i] = n * lead[l] * q[l] * trig
                scale[i] = n * lead[l] * 4 * math.pi / (2 * l + 1)
                invert[i] = (2 * l + 1) / (4 * math.pi)
    return np.stack([x, y, z]), ys, scale, invert


def split(a):
    a = np.asarray(a, np.float32)
    hi = a.astype(ml_dtypes.bfloat16)
    return hi, (a - hi.astype(np.float32)).astype(ml_dtypes.bfloat16)


def halves(x):
    hi = x.astype(BF)
    return hi, (x - hi.astype(F32)).astype(BF)


def pair_weights():
    dirs, ys, _, _ = tables()
    w = np.zeros((2 * NG, 2 * LP))
    wy = ys.T * (4 * math.pi / NG)
    w[:NG, :LM] = wy
    w[NG:, LP : LP + LM] = wy
    d = np.zeros((8, 2 * NG), np.float32)
    d[:3, :NG] = dirs
    d[:3, NG:] = dirs
    return np.concatenate(split(w), 1), d


def even_weights():
    _, ys, _, _ = tables()
    w = np.zeros((PN, 2 * LP))
    w[:NG, :LM] = ys.T
    w[NG:, LP : LP + LM] = ys.T
    return np.concatenate(split(w), 1), np.concatenate(split(w.T), 1)


def lane_scales():
    _, _, scale, invert = tables()
    rows = np.zeros((8, 2 * LP), np.float32)
    for h in (0, LP):
        rows[0, h : h + LM] = scale * invert
        rows[1, h : h + LM] = invert
    return rows


def chunk_piece(k, width, p):
    at = (lax.axis_index("fit") ^ k) * width + p * PIECE
    return pl.ds(pl.multiple_of(at, 128), PIECE)


def code(x):
    top = jnp.maximum(jnp.max(jnp.abs(x), axis=1, keepdims=True), 1e-30)
    power = jnp.floor(jnp.log2(top)) - 13.0
    q = jnp.floor(x * jnp.exp2(-power) + 0.5).astype(jnp.int32)
    tail = jnp.broadcast_to(power, (x.shape[0], 128)).astype(jnp.int32)
    return q.astype(jnp.int16), tail.astype(jnp.int16)


def decode(ref, ls):
    width = ref.shape[1] - 128
    power = ref[:, width:].astype(jnp.int32).astype(F32)[:, 0:1]
    return ref[:, ls].astype(jnp.int32).astype(F32) * jnp.exp2(power)


def phi_kernel(width, far_coef_ref, far_ref, *rest):
    outs, (tile_ref, full, coef_ref, sem, coef_sem) = rest[:-5], rest[-5:]
    first = pltpu.make_async_copy(far_coef_ref, coef_ref, coef_sem)
    first.start()
    per = width // PIECE
    todo = [(k, p) for k in [*range(1, len(outs)), 0] for p in range(per)]
    copies = []
    for i, (k, p) in enumerate(todo):
        at = chunk_piece(k, width, p)
        copies.append(pltpu.make_async_copy(far_ref.at[:, at], tile_ref.at[:, at], sem.at[i]))
        copies[-1].start()
    first.wait()
    for (k, p), copy in zip(todo, copies):
        copy.wait()
        out = full if k else outs[0]
        out[:, p * PIECE : (p + 1) * PIECE] = jnp.dot(
            coef_ref[...], tile_ref[:, chunk_piece(k, width, p)], preferred_element_type=F32
        )
        if k and p == per - 1:
            q, tail = code(full[...])
            outs[k][:, :width] = q
            outs[k][:, width:] = tail


def phi_call(coefs, tiles, width):
    aux, points = tiles.shape
    count = points // width
    return pl.pallas_call(
        functools.partial(phi_kernel, width),
        in_specs=[pl.BlockSpec(memory_space=pltpu.HBM)] * 2,
        out_specs=[VMEM] * (count + 1),
        out_shape=[jax.ShapeDtypeStruct((NDENS, width), F32)]
        + [jax.ShapeDtypeStruct((NDENS, width + 128), jnp.int16)] * (count - 1)
        + [jax.ShapeDtypeStruct(tiles.shape, tiles.dtype)],
        scratch_shapes=[
            pltpu.VMEM((NDENS, width), F32),
            pltpu.VMEM(coefs.shape, coefs.dtype),
            pltpu.SemaphoreType.DMA((points // PIECE,)),
            pltpu.SemaphoreType.DMA,
        ],
        compiler_params=PARAMS,
        cost_estimate=pl.CostEstimate(
            flops=2 * NDENS * aux * points,
            bytes_accessed=(2 * aux + 4 * NDENS) * points,
            transcendentals=0,
        ),
        name="phi",
    )(*(pltpu.with_memory_space_constraint(a, pltpu.HBM) for a in (coefs, tiles)))


def pack_kernel(centre_ref, radius_ref, nbr_ref, cnt_ref, out_ref, c, r, n, k, sem):
    copies = [
        pltpu.make_async_copy(a, b, sem.at[i])
        for i, (a, b) in enumerate(zip((centre_ref, radius_ref, nbr_ref, cnt_ref), (c, r, n, k)))
    ]
    for copy in copies:
        copy.start()
    for copy in copies:
        copy.wait()
    spheres, slots = n.shape
    out_ref[...] = jnp.zeros_like(out_ref)
    out_ref[0:3, :] = c[...]
    out_ref[3:4, :] = r[...]
    out_ref[4:5, :] = k[...].astype(F32)
    out_ref[8:, :] = n[...].astype(F32)


def pack_call(centres, radii, neighbours, counts):
    spheres, slots = neighbours.shape
    args = (centres, radii.reshape(1, spheres), neighbours, counts.reshape(1, spheres))
    return pl.pallas_call(
        pack_kernel,
        in_specs=[pl.BlockSpec(memory_space=pltpu.HBM)] * 4,
        out_specs=VMEM,
        out_shape=jax.ShapeDtypeStruct((8 + spheres, spheres), F32),
        scratch_shapes=[pltpu.VMEM(a.shape, a.dtype) for a in args]
        + [pltpu.SemaphoreType.DMA((4,))],
        compiler_params=PARAMS,
        name="pack",
    )(*(pltpu.with_memory_space_constraint(a, pltpu.HBM) for a in args))


def pair_build(e, geo, mask, dir_ref, bh):
    lane = lax.broadcasted_iota(jnp.int32, (8, 128), 1)
    sub = lax.broadcasted_iota(jnp.int32, (8, 128), 0)
    own = jnp.broadcast_to(geo[pl.ds(e + 8, 1), :], (8, 128))
    mrow = jnp.broadcast_to(mask[pl.ds(e, 1), :], (8, 128))
    cols = []
    for g, start in ((0, e), (1, e + 9)):
        near = geo[pl.ds(start, 8), :]
        valid = jnp.sum(jnp.where(lane == sub + 8 * g, mrow, 0.0), axis=1, keepdims=True)
        on = valid > 0.0
        ir = 1.0 / jnp.where(on, near[:, 3:4], 1.0)
        off = jnp.where(on, own - near, 0.0)
        c = [off[:, 0:1] * ir, off[:, 1:2] * ir, off[:, 2:3] * ir, own[:, 3:4] * ir, valid]
        cols.append([jnp.broadcast_to(q, (8, 128)) for q in c])
    mid = [jnp.where(lane < 64, a, b) for a, b in zip(*cols)]
    sums = []
    for t in range(5):
        ox, oy, oz, q, valid = cols[0] if t < 2 else (mid if t == 2 else cols[1])
        ls = slice(128 * t, 128 * t + 128)
        x = ox + q * dir_ref[0:1, ls]
        y = oy + q * dir_ref[1:2, ls]
        z = oz + q * dir_ref[2:3, ls]
        r2 = x * x + y * y + z * z
        ramp = jnp.clip((1.0 - jnp.sqrt(r2)) * (1.0 / BAND), 0.0, 1.0)
        chi = ramp * ramp * (3.0 - 2.0 * ramp) * valid
        sums.append(jnp.sum(chi, axis=0, keepdims=True))
        cos, sin = [chi, chi * x], [None, chi * y]
        for m in range(2, DEGREE + 1):
            cos.append(cos[m - 1] * x - sin[m - 1] * y)
            sin.append(cos[m - 1] * y + sin[m - 1] * x)
        out = [None] * LM
        for m in range(DEGREE + 1):
            qm = {}
            for l in range(m, DEGREE + 1):
                if l == m + 1:
                    qm[l] = z
                elif l == m + 2:
                    qm[l] = z * z - gam(l, m) * r2
                elif l > m + 2:
                    qm[l] = z * qm[l - 1] - (gam(l, m) * r2) * qm[l - 2]
                for sign, trig in ((1, cos[m]), (-1, sin[m])):
                    if m == 0 and sign < 0:
                        continue
                    out[l * l + l + sign * m] = trig if l == m else trig * qm[l]
        out.append(jnp.zeros((8, 128), F32))
        for p in range(25):
            both = jnp.concatenate([out[2 * p], out[2 * p + 1]], axis=0)
            bh[16 * p : 16 * p + 16, ls] = both.astype(BF)
    return sums


def pair_finish(e, w_ref, t_ref, bh):
    r = jnp.dot(bh[...], w_ref[...], preferred_element_type=F32)
    tt = r[: LM * 8, : 2 * LP] + r[: LM * 8, 2 * LP :]
    a = jnp.swapaxes(tt.reshape(LM, 8, 2 * LP), 0, 1)
    a = jnp.concatenate([a, jnp.zeros((8, LP - LM, 2 * LP), F32)], 1).reshape(8 * LP, 2 * LP)
    hi, lo = halves(a)
    t_ref[e, :, : 2 * LP] = hi
    t_ref[e, :, 2 * LP :] = lo


def uncover(sums):
    low = lax.broadcasted_iota(jnp.int32, (1, 128), 1) < 64
    swap = lambda v: pltpu.roll(v, 64, 1)
    three = []
    for s in sums:
        r2, r3, r4 = swap(s[2]), swap(s[3]), swap(s[4])
        three.append([s[0] + jnp.where(low, r2, r3), s[1] + jnp.where(low, r3, r4), s[2] + r4])
    a, b = three
    b0, b1, b2 = swap(b[0]), swap(b[1]), swap(b[2])
    tiles = [a[0], a[1], jnp.where(low, a[2], b0), jnp.where(low, b0, b1), jnp.where(low, b1, b2)]
    return [jnp.maximum(0.0, 1.0 - t) for t in tiles]


def pair_kernel(
    lo, hi, before_ref, own_ref, after_ref, dir_ref, w_ref, t_ref, unc_ref, geo, mask, *bhs
):
    spheres = own_ref.shape[1]
    slots = 2 * REACH
    wide = spheres + 2 * REACH
    packs = (before_ref, own_ref, after_ref)
    rows = jnp.concatenate([p[0:8, :] for p in packs], axis=1)
    rows = jnp.concatenate([rows, jnp.zeros((8, 128 - rows.shape[1]), F32)], axis=1)
    rows = jnp.concatenate([rows, jnp.zeros((120, 128), F32)], axis=0)
    geo[...] = rows.T[: geo.shape[0]]
    first = (lax.axis_index("sph") * lax.axis_size("fit") + lax.axis_index("fit")) * spheres
    row = lax.broadcasted_iota(jnp.int32, (wide, slots), 0) + (first - REACH)
    slot = lax.broadcasted_iota(jnp.int32, (wide, slots), 1)
    lists = [before_ref[8 + spheres - REACH :, :], own_ref[8:, :], after_ref[8 : 8 + REACH, :]]
    rel = jnp.concatenate(lists, axis=0) - row.astype(F32)
    listed = slot.astype(F32) < geo[spheres - REACH : 2 * spheres + REACH, 4:5]
    lane = lax.broadcasted_iota(jnp.int32, (wide, 128), 1)
    found = jnp.zeros((wide, 128), F32)
    for c in range(slots):
        gap = c - REACH if c < REACH else c - REACH + 1
        hit = jnp.where(listed & (rel == float(gap)), 1.0, 0.0)
        hit = jnp.max(hit, axis=1, keepdims=True)
        found = jnp.where(lane == c, hit, found)
    mask[...] = found

    def step(b, carry):
        sums = []
        for u in range(QUAD):
            at = b * QUAD + u
            sums.append(pair_build(at + lo, geo, mask, dir_ref, bhs[u]))
            pair_finish(at, w_ref, t_ref, bhs[u])
        tiles = uncover(sums[:2]) + uncover(sums[2:])
        for t, v in enumerate(tiles):
            unc_ref[b, :, 128 * t : 128 * t + 128] = v
        return carry

    lax.fori_loop(0, (hi - lo) // QUAD, step, 0, unroll=(hi - lo) // QUAD)


def pair_call(before, own, after, lo, hi):
    spheres = own.shape[1]
    wide = spheres + 2 * REACH
    count = hi - lo
    w, d = pair_weights()
    return pl.pallas_call(
        functools.partial(pair_kernel, lo, hi),
        in_specs=[VMEM] * 5,
        out_specs=[VMEM] * 2,
        scratch_shapes=[pltpu.VMEM((3 * spheres, 128), F32), pltpu.VMEM((wide, 128), F32)]
        + [pltpu.VMEM((400, 2 * NG), BF)] * QUAD,
        out_shape=[
            jax.ShapeDtypeStruct((count, 8 * LP, 4 * LP), BF),
            jax.ShapeDtypeStruct((count // QUAD, 1, QN), F32),
        ],
        compiler_params=PARAMS,
        cost_estimate=pl.CostEstimate(
            flops=count * 2 * 400 * 640 * 256, bytes_accessed=count * 262144, transcendentals=0
        ),
        name="pairs",
    )(before, own, after, jnp.asarray(d), jnp.asarray(w))


def own_uncovered(unc_ref, b):
    b = b + REACH // 2
    return unc_ref[b // 2, :, b % 2 * PN : (b % 2 + 1) * PN]


def rhs_kernel(count, *refs):
    phis, (unc_ref, w_ref, out_ref) = refs[:count], refs[count:]
    pairs = out_ref.shape[1] // (2 * LP)
    rows = []
    for b in range(pairs):
        ls = slice(b * PN, (b + 1) * PN)
        total = phis[0][:, ls]
        for p in phis[1:]:
            total = total + decode(p, ls)
        rows.append(total * own_uncovered(unc_ref, b))
    hi, lo = halves(jnp.concatenate(rows, 0))
    n = pairs * NDENS
    r = jnp.dot(jnp.concatenate([hi, lo], 0), w_ref[...], preferred_element_type=F32)
    out = r[:n, : 2 * LP] + r[:n, 2 * LP :] + r[n:, : 2 * LP]
    out = out * (-4.0 * math.pi / NG)
    for b in range(pairs):
        out_ref[:, b * 2 * LP : (b + 1) * 2 * LP] = out[b * NDENS : (b + 1) * NDENS]


def rhs_call(phis, unc, w):
    spheres = phis[0].shape[1] // NG
    return pl.pallas_call(
        functools.partial(rhs_kernel, len(phis)),
        in_specs=[VMEM] * (len(phis) + 2),
        out_specs=VMEM,
        compiler_params=PARAMS,
        out_shape=jax.ShapeDtypeStruct((NDENS, spheres * LP), F32),
        cost_estimate=pl.CostEstimate(
            flops=6 * NDENS * spheres * NG * 256, bytes_accessed=1700000, transcendentals=0
        ),
        name="rhs",
    )(*phis, unc, w)


def gather_field(t_refs, shift, x, xs, e):
    low = lax.broadcasted_iota(jnp.int32, (NDENS, 128), 1) < LP
    parts = []
    for odd in (0, 1):
        below, above = (x, xs) if odd == 0 else (xs, x)
        lo_at = e * LP
        up_at = (e + 8) * LP if odd == 0 else (e + 10) * LP
        lhs = jnp.concatenate(
            [below[:, lo_at : lo_at + 8 * LP], above[:, up_at : up_at + 8 * LP]], 0
        )
        at = e + odd + shift
        most = t_refs[0].shape[0]
        t = t_refs[0][at] if at < most else t_refs[1][at - most]
        r = jnp.dot(lhs, t, preferred_element_type=F32)
        n = NDENS
        a = r[0:n, : 2 * LP] + r[n : 2 * n, : 2 * LP] + r[0:n, 2 * LP :]
        b = r[2 * n : 3 * n, : 2 * LP] + r[3 * n :, : 2 * LP] + r[2 * n : 3 * n, 2 * LP :]
        parts.append((a, b))
    (a0, b0), (a1, b1) = parts
    return jnp.where(low, a0, b1) + pltpu.roll(jnp.where(low, a1, b0), LP, 1)


def put_scaled(x, at, value):
    hi, lo = halves(value)
    x[0:NDENS, at : at + 128] = hi
    x[NDENS:, at : at + 128] = lo


def put_shifted(xs, x):
    v = x[...].astype(F32)
    xs[...] = jnp.concatenate([v[:, LP:], v[:, :LP]], 1).astype(BF)


def sweep_kernel(
    before_ref, own_ref, after_ref, t_ref, rest_ref, sc_ref, unc_ref, m_ref, out_ref,
    x, xs, z, zs
):
    own = own_ref.shape[1]
    spheres = own // LP
    right = lambda at: (before_ref, own_ref, after_ref)[at // own][:, at % own : at % own + 128]
    for at in range(0, 3 * own, 128):
        put_scaled(x, at, right(at) * sc_ref[0:1, :])
    put_shifted(xs, x)
    for e in range(0, spheres + 2 * REACH, 2):
        new = right((e + spheres - REACH) * LP) + gather_field((t_ref, rest_ref), 0, x, xs, e)
        put_scaled(z, e * LP, new * sc_ref[0:1, :])
    put_shifted(zs, z)
    for e in range(0, spheres, 2):
        new = own_ref[:, e * LP : e * LP + 128] + gather_field((t_ref, rest_ref), REACH, z, zs, e)
        new = new * sc_ref[1:2, :]
        m_ref[e] = new[:, :LM]
        m_ref[e + 1] = pltpu.roll(new, LP, 1)[:, :LM]
        out_ref[:, e * LP : e * LP + 128] = new
    out_ref[:, own:] = jnp.zeros((NDENS, 384), F32)
    pairs = spheres // 2
    for b in range(pairs):
        part = own_uncovered(unc_ref, b)
        out_ref[b : b + 1, own:] = part[:, :384]
        out_ref[pairs + b : pairs + b + 1, own : own + 256] = part[:, 384:]


def sweep_call(before, own, after, t, rest, scales, unc):
    lanes = own.shape[1]
    spheres = lanes // LP
    return pl.pallas_call(
        sweep_kernel,
        in_specs=[VMEM] * 7,
        out_specs=[VMEM] * 2,
        out_shape=[
            jax.ShapeDtypeStruct((spheres, NDENS, LM), F32),
            jax.ShapeDtypeStruct((NDENS, lanes + 384), F32),
        ],
        scratch_shapes=[pltpu.VMEM((2 * NDENS, 3 * lanes), BF)] * 2
        + [pltpu.VMEM((2 * NDENS, lanes + 2 * REACH * LP), BF)] * 2,
        compiler_params=PARAMS,
        cost_estimate=pl.CostEstimate(
            flops=3 * spheres * 2 * 64 * 512 * 256,
            bytes_accessed=2 * spheres * 262144,
            transcendentals=0,
        ),
        name="sweeps",
    )(before, own, after, t, rest, scales, unc)


def fock_kernel(k, pay_ref, y_ref, tile_ref, *rest):
    out_ref, charge = rest[-2:]
    own = pay_ref.shape[1] - 384
    pairs = own // (2 * LP)
    width = pairs * PN
    rows = [pay_ref[:, b * 2 * LP : (b + 1) * 2 * LP] for b in range(pairs)]
    hi, lo = halves(jnp.concatenate(rows, 0))
    n = pairs * NDENS
    r = jnp.dot(jnp.concatenate([hi, lo], 0), y_ref[...], preferred_element_type=F32)
    out = r[:n, :PN] + r[:n, PN:] + r[n:, :PN]
    for b in range(pairs):
        unc = jnp.concatenate(
            [pay_ref[b : b + 1, own:], pay_ref[pairs + b : pairs + b + 1, own : own + 256]], 1
        )
        weight = unc * (4.0 * math.pi / NG)
        charge[:, b * PN : (b + 1) * PN] = (out[b * NDENS : (b + 1) * NDENS] * weight).astype(BF)
    total = rest[0][...] if len(rest) == 3 else None
    for p in range(width // PIECE):
        part = lax.dot_general(
            charge[:, p * PIECE : (p + 1) * PIECE],
            tile_ref[:, chunk_piece(k, width, p)],
            (((1,), (1,)), ((), ())),
            preferred_element_type=F32,
        )
        total = part if total is None else total + part
    out_ref[...] = total


def fock_call(k, pay, wt, tiles, width, before=None):
    aux = tiles.shape[0]
    more = [] if before is None else [before]
    return pl.pallas_call(
        functools.partial(fock_kernel, k),
        in_specs=[VMEM] * (3 + len(more)),
        out_specs=VMEM,
        out_shape=jax.ShapeDtypeStruct((NDENS, aux), F32),
        scratch_shapes=[pltpu.VMEM((NDENS, width), BF)],
        compiler_params=PARAMS,
        cost_estimate=pl.CostEstimate(
            flops=2 * NDENS * aux * width, bytes_accessed=2 * aux * width, transcendentals=0
        ),
        name="fock",
    )(pay, wt, tiles, *more)


def trade(x, axis, k):
    count = lax.axis_size(axis)
    return lax.ppermute(x, axis, [(i, i ^ k) for i in range(count)])


def shift(x, axis, k):
    count = lax.axis_size(axis)
    return lax.ppermute(x, axis, [(i, (i + k) % count) for i in range(count)])


def from_beside(x):
    axes = ("sph", "fit")
    count = lax.axis_size("sph") * lax.axis_size("fit")
    up = [(i, (i + 1) % count) for i in range(count)]
    down = [((i + 1) % count, i) for i in range(count)]
    return lax.ppermute(x, axes, up), lax.ppermute(x, axes, down)


def body(tiles, coefs, centres, radii, neighbours, counts):
    spheres, slots = neighbours.shape
    fits = lax.axis_size("fit")
    sphs = lax.axis_size("sph")
    assert fits & (fits - 1) == 0 and sphs & (sphs - 1) == 0
    assert spheres % (2 * QUAD) == 0 and spheres == slots == 2 * REACH
    w, wt = (jnp.asarray(a) for a in even_weights())
    scales = jnp.asarray(lane_scales())

    width = spheres * NG
    own = pack_call(centres, radii, neighbours, counts)
    before, after = from_beside(own)
    *phis, near_tiles = phi_call(coefs, tiles, width)
    phis, before, after = lax.optimization_barrier((phis, before, after))
    got = [trade(phis[k], "fit", k) for k in range(1, fits)]
    wide = spheres + 2 * REACH
    t, unc = pair_call(before, own, after, 0, wide - REACH)
    rhs = rhs_call([phis[0], *got], unc, w)
    below, above = from_beside(rhs)
    late, _ = lax.optimization_barrier((own, rhs))
    rest, _ = pair_call(before, late, after, wide - REACH, wide)
    moments, pay = sweep_call(below, rhs, above, t, rest, scales, unc)
    others = [trade(pay, "fit", k) for k in range(1, fits)]
    fock = fock_call(0, pay, wt, near_tiles, width)
    for k in range(1, fits):
        fock = fock_call(k, others[k - 1], wt, near_tiles, width, fock)
    fock = fock + trade(fock, "sph", 1)
    bit = 2
    while bit < sphs:
        ks = [k for k in (bit, 2 * bit, 3 * bit) if k < sphs]
        if 4 * bit == sphs:
            parts = [shift(fock, "sph", k) for k in ks]
        else:
            parts = [trade(fock, "sph", k) for k in ks]
        fock = functools.reduce(jnp.add, parts, fock)
        bit *= 4
    return moments, fock


def solution(mesh):
    placed = (
        P("fit", "sph"),
        P(None, "fit"),
        P(None, ("sph", "fit")),
        P(("sph", "fit")),
        P(("sph", "fit"), None),
        P(("sph", "fit")),
    )
    return jax.shard_map(
        body,
        mesh=mesh,
        in_specs=placed,
        out_specs=(P(("sph", "fit"), None, None), P(None, "fit")),
        check_vma=False,
    )
```

```python
import functools
import math

import jax
import jax.numpy as jnp
import ml_dtypes
import numpy as np
from jax import lax
from jax.experimental import pallas as pl
from jax.experimental.pallas import tpu as pltpu
from jax.sharding import PartitionSpec as P

DEGREE = 6
LM = 49
NTH = 16
NPHI = 20
NG = 320
NDENS = 16
LP = 64
QUAD = 4
QN = QUAD * NG
PN = 2 * NG
PIECE = 2560
PARAMS = pltpu.CompilerParams(vmem_limit_bytes=16 << 20)
VMEM = pl.BlockSpec(memory_space=pltpu.VMEM)
SMEM = pl.BlockSpec(memory_space=pltpu.SMEM)
BAND = 0.1
REACH = 8
SOONER = 1
BF = jnp.bfloat16
F32 = jnp.float32


def gam(l, m):
    return (l + m - 1) * (l - 1 - m) / ((2 * l - 1) * (2 * l - 3))


def tables():
    c = -1.0 + (2.0 * np.arange(NTH) + 1.0) / NTH
    f = (np.arange(NPHI) + 0.5) * (2 * np.pi / NPHI)
    z = np.repeat(c, NPHI)
    s = np.sqrt(1 - z * z)
    az = np.tile(f, NTH)
    x, y = s * np.cos(az), s * np.sin(az)
    cos, sin = [np.ones_like(x)], [np.zeros_like(x)]
    for m in range(1, DEGREE + 1):
        cos.append(cos[m - 1] * x - sin[m - 1] * y)
        sin.append(cos[m - 1] * y + sin[m - 1] * x)
    ys, scale, invert = np.zeros((LM, NG)), np.zeros(LM), np.zeros(LM)
    for m in range(DEGREE + 1):
        q, lead = {m: np.ones_like(x)}, {m: 1.0}
        for odd in range(1, 2 * m, 2):
            lead[m] *= odd
        for l in range(m + 1, DEGREE + 1):
            q[l] = z * q[l - 1] - (gam(l, m) * q[l - 2] if l > m + 1 else 0.0)
            lead[l] = lead[l - 1] * (2 * l - 1) / (l - m)
        for l in range(m, DEGREE + 1):
            n = math.sqrt(
                (2 * l + 1) / (4 * math.pi) * math.factorial(l - m) / math.factorial(l + m)
            )
            n *= math.sqrt(2.0) if m else 1.0
            for sign, trig in ((1, cos[m]), (-1, sin[m])):
                if m == 0 and sign < 0:
                    continue
                i = l * l + l + sign * m
                ys[i] = n * lead[l] * q[l] * trig
                scale[i] = n * lead[l] * 4 * math.pi / (2 * l + 1)
                invert[i] = (2 * l + 1) / (4 * math.pi)
    return np.stack([x, y, z]), ys, scale, invert


def split(a):
    a = np.asarray(a, np.float32)
    hi = a.astype(ml_dtypes.bfloat16)
    return hi, (a - hi.astype(np.float32)).astype(ml_dtypes.bfloat16)


def halves(x):
    hi = x.astype(BF)
    return hi, (x - hi.astype(F32)).astype(BF)


def pair_weights():
    dirs, ys, _, _ = tables()
    w = np.zeros((2 * NG, 2 * LP))
    wy = ys.T * (4 * math.pi / NG)
    w[:NG, :LM] = wy
    w[NG:, LP : LP + LM] = wy
    d = np.zeros((8, 2 * NG), np.float32)
    d[:3, :NG] = dirs
    d[:3, NG:] = dirs
    return np.concatenate(split(w), 1), d


def even_weights():
    _, ys, _, _ = tables()
    w = np.zeros((PN, 2 * LP))
    w[:NG, :LM] = ys.T
    w[NG:, LP : LP + LM] = ys.T
    hi, lo = split(w.T)
    deep = np.block([[hi, lo], [hi, np.zeros_like(lo)]])
    return np.concatenate(split(w), 1), deep


def lane_scales():
    _, _, scale, invert = tables()
    rows = np.zeros((8, 2 * LP), np.float32)
    for h in (0, LP):
        rows[0, h : h + LM] = scale * invert
        rows[1, h : h + LM] = invert
    return rows


def chunk_piece(k, width, p):
    at = (lax.axis_index("fit") ^ k) * width + p * PIECE
    return pl.ds(pl.multiple_of(at, 128), PIECE)


def code(x):
    top = jnp.maximum(jnp.max(jnp.abs(x), axis=1, keepdims=True), 1e-30)
    power = jnp.floor(jnp.log2(top)) - 13.0
    q = jnp.floor(x * jnp.exp2(-power) + 0.5).astype(jnp.int32)
    tail = jnp.broadcast_to(power, (x.shape[0], 128)).astype(jnp.int32)
    return q.astype(jnp.int16), tail.astype(jnp.int16)


def decode(ref, ls):
    width = ref.shape[1] - 128
    power = ref[:, width:].astype(jnp.int32).astype(F32)[:, 0:1]
    return ref[:, ls].astype(jnp.int32).astype(F32) * jnp.exp2(power)


def fetch(far_ref, tile_ref, sem, k, width):
    copies = []
    for p in range(width // PIECE):
        to = tile_ref.at[:, p * PIECE : (p + 1) * PIECE]
        copies.append(pltpu.make_async_copy(far_ref.at[:, chunk_piece(k, width, p)], to, sem.at[p]))
        copies[-1].start()
    return copies


def potentials(copies, coef_ref, tile_ref, out):
    for p, copy in enumerate(copies):
        copy.wait()
        ls = slice(p * PIECE, (p + 1) * PIECE)
        out[:, ls] = jnp.dot(coef_ref[...], tile_ref[:, ls], preferred_element_type=F32)


def phi_kernel(peers, width, far_coef_ref, far_ref, *rest):
    outs, tiles, (full, coef_ref, sem, coef_sem) = rest[:peers], rest[peers : 2 * peers], rest[-4:]
    first = pltpu.make_async_copy(far_coef_ref, coef_ref, coef_sem)
    first.start()
    copies = [fetch(far_ref, t, sem.at[i], i + 1, width) for i, t in enumerate(tiles)]
    first.wait()
    for i in range(peers):
        potentials(copies[i], coef_ref, tiles[i], full)
        q, tail = code(full[...])
        outs[i][:, :width] = q
        outs[i][:, width:] = tail


def phi_call(coefs, tiles, width):
    aux, points = tiles.shape
    peers = points // width - 1
    return pl.pallas_call(
        functools.partial(phi_kernel, peers, width),
        in_specs=[pl.BlockSpec(memory_space=pltpu.HBM)] * 2,
        out_specs=[VMEM] * (2 * peers),
        out_shape=[jax.ShapeDtypeStruct((NDENS, width + 128), jnp.int16)] * peers
        + [jax.ShapeDtypeStruct((aux, width), tiles.dtype)] * peers,
        scratch_shapes=[
            pltpu.VMEM((NDENS, width), F32),
            pltpu.VMEM(coefs.shape, coefs.dtype),
            pltpu.SemaphoreType.DMA((peers, width // PIECE)),
            pltpu.SemaphoreType.DMA,
        ],
        compiler_params=PARAMS,
        cost_estimate=pl.CostEstimate(
            flops=2 * NDENS * aux * width * peers,
            bytes_accessed=(2 * aux + 4 * NDENS) * width * peers,
            transcendentals=0,
        ),
        name="phi",
    )(*(pltpu.with_memory_space_constraint(a, pltpu.HBM) for a in (coefs, tiles)))


def pack_kernel(centre_ref, radius_ref, nbr_ref, cnt_ref, out_ref, c, r, n, k, sem):
    copies = [
        pltpu.make_async_copy(a, b, sem.at[i])
        for i, (a, b) in enumerate(zip((centre_ref, radius_ref, nbr_ref, cnt_ref), (c, r, n, k)))
    ]
    for copy in copies:
        copy.start()
    for copy in copies:
        copy.wait()
    spheres, slots = n.shape
    out_ref[...] = jnp.zeros_like(out_ref)
    out_ref[0:3, :] = c[...]
    out_ref[3:4, :] = r[...]
    out_ref[4:5, :] = k[...].astype(F32)
    out_ref[8:, :] = n[...].astype(F32)


def pack_call(centres, radii, neighbours, counts):
    spheres, slots = neighbours.shape
    args = (centres, radii.reshape(1, spheres), neighbours, counts.reshape(1, spheres))
    return pl.pallas_call(
        pack_kernel,
        in_specs=[pl.BlockSpec(memory_space=pltpu.HBM)] * 4,
        out_specs=VMEM,
        out_shape=jax.ShapeDtypeStruct((8 + spheres, spheres), F32),
        scratch_shapes=[pltpu.VMEM(a.shape, a.dtype) for a in args]
        + [pltpu.SemaphoreType.DMA((4,))],
        compiler_params=PARAMS,
        name="pack",
    )(*(pltpu.with_memory_space_constraint(a, pltpu.HBM) for a in args))


def pair_build(e, geo, mask, dir_ref, bh):
    lane = lax.broadcasted_iota(jnp.int32, (8, 128), 1)
    sub = lax.broadcasted_iota(jnp.int32, (8, 128), 0)
    own = jnp.broadcast_to(geo[pl.ds(e + 8, 1), :], (8, 128))
    mrow = jnp.broadcast_to(mask[pl.ds(e, 1), :], (8, 128))
    cols = []
    for g, start in ((0, e), (1, e + 9)):
        near = geo[pl.ds(start, 8), :]
        valid = jnp.sum(jnp.where(lane == sub + 8 * g, mrow, 0.0), axis=1, keepdims=True)
        on = valid > 0.0
        ir = 1.0 / jnp.where(on, near[:, 3:4], 1.0)
        off = jnp.where(on, own - near, 0.0)
        c = [off[:, 0:1] * ir, off[:, 1:2] * ir, off[:, 2:3] * ir, own[:, 3:4] * ir, valid]
        cols.append([jnp.broadcast_to(q, (8, 128)) for q in c])
    mid = [jnp.where(lane < 64, a, b) for a, b in zip(*cols)]
    sums = []
    for t in range(5):
        ox, oy, oz, q, valid = cols[0] if t < 2 else (mid if t == 2 else cols[1])
        ls = slice(128 * t, 128 * t + 128)
        x = ox + q * dir_ref[0:1, ls]
        y = oy + q * dir_ref[1:2, ls]
        z = oz + q * dir_ref[2:3, ls]
        r2 = x * x + y * y + z * z
        ramp = jnp.clip((1.0 - jnp.sqrt(r2)) * (1.0 / BAND), 0.0, 1.0)
        chi = ramp * ramp * (3.0 - 2.0 * ramp) * valid
        sums.append(jnp.sum(chi, axis=0, keepdims=True))
        cos, sin = [chi, chi * x], [None, chi * y]
        for m in range(2, DEGREE + 1):
            cos.append(cos[m - 1] * x - sin[m - 1] * y)
            sin.append(cos[m - 1] * y + sin[m - 1] * x)
        out = [None] * LM
        for m in range(DEGREE + 1):
            qm = {}
            for l in range(m, DEGREE + 1):
                if l == m + 1:
                    qm[l] = z
                elif l == m + 2:
                    qm[l] = z * z - gam(l, m) * r2
                elif l > m + 2:
                    qm[l] = z * qm[l - 1] - (gam(l, m) * r2) * qm[l - 2]
                for sign, trig in ((1, cos[m]), (-1, sin[m])):
                    if m == 0 and sign < 0:
                        continue
                    out[l * l + l + sign * m] = trig if l == m else trig * qm[l]
        out.append(jnp.zeros((8, 128), F32))
        for p in range(25):
            both = jnp.concatenate([out[2 * p], out[2 * p + 1]], axis=0)
            bh[16 * p : 16 * p + 16, ls] = both.astype(BF)
    return sums


def pair_finish(e, w_ref, t_ref, bh):
    r = jnp.dot(bh[...], w_ref[...], preferred_element_type=F32)
    tt = r[: LM * 8, : 2 * LP] + r[: LM * 8, 2 * LP :]
    a = jnp.swapaxes(tt.reshape(LM, 8, 2 * LP), 0, 1)
    a = jnp.concatenate([a, jnp.zeros((8, LP - LM, 2 * LP), F32)], 1).reshape(8 * LP, 2 * LP)
    hi, lo = halves(a)
    t_ref[e, :, : 2 * LP] = hi
    t_ref[e, :, 2 * LP :] = lo


def uncover(sums):
    low = lax.broadcasted_iota(jnp.int32, (1, 128), 1) < 64
    swap = lambda v: pltpu.roll(v, 64, 1)
    three = []
    for s in sums:
        r2, r3, r4 = swap(s[2]), swap(s[3]), swap(s[4])
        three.append([s[0] + jnp.where(low, r2, r3), s[1] + jnp.where(low, r3, r4), s[2] + r4])
    a, b = three
    b0, b1, b2 = swap(b[0]), swap(b[1]), swap(b[2])
    tiles = [a[0], a[1], jnp.where(low, a[2], b0), jnp.where(low, b0, b1), jnp.where(low, b1, b2)]
    return [jnp.maximum(0.0, 1.0 - t) for t in tiles]


def pair_kernel(quads, extra, before_ref, own_ref, after_ref, dir_ref, w_ref, *rest):
    if extra:
        coef_ref, far_ref, t_ref, unc_ref, phi_ref, tile_ref, geo, mask, sem, *bhs = rest
        copies = fetch(far_ref, tile_ref, sem, 0, tile_ref.shape[1])
    else:
        t_ref, unc_ref, geo, mask, *bhs = rest
    spheres = own_ref.shape[1]
    slots = 2 * REACH
    wide = spheres + 2 * REACH
    packs = (before_ref, own_ref, after_ref)
    rows = jnp.concatenate([p[0:8, :] for p in packs], axis=1)
    rows = jnp.concatenate([rows, jnp.zeros((8, 128 - rows.shape[1]), F32)], axis=1)
    rows = jnp.concatenate([rows, jnp.zeros((120, 128), F32)], axis=0)
    geo[...] = rows.T[: geo.shape[0]]
    first = (lax.axis_index("sph") * lax.axis_size("fit") + lax.axis_index("fit")) * spheres
    row = lax.broadcasted_iota(jnp.int32, (wide, slots), 0) + (first - REACH)
    slot = lax.broadcasted_iota(jnp.int32, (wide, slots), 1)
    lists = [before_ref[8 + spheres - REACH :, :], own_ref[8:, :], after_ref[8 : 8 + REACH, :]]
    rel = jnp.concatenate(lists, axis=0) - row.astype(F32)
    listed = slot.astype(F32) < geo[spheres - REACH : 2 * spheres + REACH, 4:5]
    lane = lax.broadcasted_iota(jnp.int32, (wide, 128), 1)
    found = jnp.zeros((wide, 128), F32)
    for c in range(slots):
        gap = c - REACH if c < REACH else c - REACH + 1
        hit = jnp.where(listed & (rel == float(gap)), 1.0, 0.0)
        hit = jnp.max(hit, axis=1, keepdims=True)
        found = jnp.where(lane == c, hit, found)
    mask[...] = found

    for b, quad in enumerate(quads):
        sums = []
        for u in range(QUAD):
            sums.append(pair_build(quad * QUAD + u, geo, mask, dir_ref, bhs[u]))
            pair_finish(b * QUAD + u, w_ref, t_ref, bhs[u])
        tiles = uncover(sums[:2]) + uncover(sums[2:])
        for t, v in enumerate(tiles):
            unc_ref[b, :, 128 * t : 128 * t + 128] = v
    if extra:
        potentials(copies, coef_ref, tile_ref, phi_ref)


def pair_call(before, own, after, quads, coefs=None, tiles=None):
    spheres = own.shape[1]
    wide = spheres + 2 * REACH
    count = len(quads)
    width = spheres * NG
    w, d = pair_weights()
    extra = tiles is not None
    in_specs = [VMEM] * 5
    out_shape = [
        jax.ShapeDtypeStruct((count * QUAD, 8 * LP, 4 * LP), BF),
        jax.ShapeDtypeStruct((count, 1, QN), F32),
    ]
    scratch = [pltpu.VMEM((3 * spheres, 128), F32), pltpu.VMEM((wide, 128), F32)]
    more = ()
    if extra:
        in_specs = in_specs + [VMEM, pl.BlockSpec(memory_space=pltpu.HBM)]
        out_shape = out_shape + [
            jax.ShapeDtypeStruct((NDENS, width), F32),
            jax.ShapeDtypeStruct((tiles.shape[0], width), tiles.dtype),
        ]
        scratch = scratch + [pltpu.SemaphoreType.DMA((width // PIECE,))]
        more = (coefs, pltpu.with_memory_space_constraint(tiles, pltpu.HBM))
    return pl.pallas_call(
        functools.partial(pair_kernel, quads, extra),
        in_specs=in_specs,
        out_specs=[VMEM] * len(out_shape),
        scratch_shapes=scratch + [pltpu.VMEM((400, 2 * NG), BF)] * QUAD,
        out_shape=out_shape,
        compiler_params=PARAMS,
        cost_estimate=pl.CostEstimate(
            flops=count * QUAD * 2 * 400 * 640 * 256,
            bytes_accessed=count * QUAD * 262144,
            transcendentals=0,
        ),
        name="pairs",
    )(before, own, after, jnp.asarray(d), jnp.asarray(w), *more)


def own_uncovered(unc_ref, b):
    b = b + SOONER * QUAD // 2
    return unc_ref[b // 2, :, b % 2 * PN : (b % 2 + 1) * PN]


def rhs_kernel(count, *refs):
    phis, (unc_ref, w_ref, out_ref) = refs[:count], refs[count:]
    pairs = out_ref.shape[1] // (2 * LP)
    rows = []
    for b in range(pairs):
        ls = slice(b * PN, (b + 1) * PN)
        total = phis[0][:, ls]
        for p in phis[1:]:
            total = total + decode(p, ls)
        rows.append(total * own_uncovered(unc_ref, b))
    hi, lo = halves(jnp.concatenate(rows, 0))
    n = pairs * NDENS
    r = jnp.dot(jnp.concatenate([hi, lo], 0), w_ref[...], preferred_element_type=F32)
    out = r[:n, : 2 * LP] + r[:n, 2 * LP :] + r[n:, : 2 * LP]
    out = out * (-4.0 * math.pi / NG)
    for b in range(pairs):
        out_ref[:, b * 2 * LP : (b + 1) * 2 * LP] = out[b * NDENS : (b + 1) * NDENS]


def rhs_call(phis, unc, w):
    spheres = phis[0].shape[1] // NG
    return pl.pallas_call(
        functools.partial(rhs_kernel, len(phis)),
        in_specs=[VMEM] * (len(phis) + 2),
        out_specs=VMEM,
        compiler_params=PARAMS,
        out_shape=jax.ShapeDtypeStruct((NDENS, spheres * LP), F32),
        cost_estimate=pl.CostEstimate(
            flops=6 * NDENS * spheres * NG * 256, bytes_accessed=1700000, transcendentals=0
        ),
        name="rhs",
    )(*phis, unc, w)


def gather_field(t_refs, shift, x, xs, e):
    low = lax.broadcasted_iota(jnp.int32, (NDENS, 128), 1) < LP
    parts = []
    for odd in (0, 1):
        below, above = (x, xs) if odd == 0 else (xs, x)
        lo_at = e * LP
        up_at = (e + 8) * LP if odd == 0 else (e + 10) * LP
        lhs = jnp.concatenate(
            [below[:, lo_at : lo_at + 8 * LP], above[:, up_at : up_at + 8 * LP]], 0
        )
        at = e + odd + shift - (REACH - SOONER * QUAD)
        most = t_refs[0].shape[0]
        if 0 <= at < most:
            t = t_refs[0][at]
        else:
            lowest = REACH - SOONER * QUAD
            t = t_refs[1][at - most + lowest if at > 0 else at + lowest]
        r = jnp.dot(lhs, t, preferred_element_type=F32)
        n = NDENS
        a = r[0:n, : 2 * LP] + r[n : 2 * n, : 2 * LP] + r[0:n, 2 * LP :]
        b = r[2 * n : 3 * n, : 2 * LP] + r[3 * n :, : 2 * LP] + r[2 * n : 3 * n, 2 * LP :]
        parts.append((a, b))
    (a0, b0), (a1, b1) = parts
    return jnp.where(low, a0, b1) + pltpu.roll(jnp.where(low, a1, b0), LP, 1)


def put_scaled(x, at, value):
    hi, lo = halves(value)
    x[0:NDENS, at : at + 128] = hi
    x[NDENS:, at : at + 128] = lo


def put_shifted(xs, x):
    v = x[...].astype(F32)
    xs[...] = jnp.concatenate([v[:, LP:], v[:, :LP]], 1).astype(BF)


def sweep_kernel(
    before_ref, own_ref, after_ref, t_ref, rest_ref, sc_ref, unc_ref, m_ref, out_ref,
    x, xs, z, zs
):
    own = own_ref.shape[1]
    spheres = own // LP
    right = lambda at: (before_ref, own_ref, after_ref)[at // own][:, at % own : at % own + 128]
    for at in range(0, 3 * own, 128):
        put_scaled(x, at, right(at) * sc_ref[0:1, :])
    put_shifted(xs, x)
    for e in range(0, spheres + 2 * REACH, 2):
        new = right((e + spheres - REACH) * LP) + gather_field((t_ref, rest_ref), 0, x, xs, e)
        put_scaled(z, e * LP, new * sc_ref[0:1, :])
    put_shifted(zs, z)
    for e in range(0, spheres, 2):
        new = own_ref[:, e * LP : e * LP + 128] + gather_field((t_ref, rest_ref), REACH, z, zs, e)
        new = new * sc_ref[1:2, :]
        m_ref[e] = new[:, :LM]
        m_ref[e + 1] = pltpu.roll(new, LP, 1)[:, :LM]
        out_ref[:, e * LP : e * LP + 128] = new
    out_ref[:, own:] = jnp.zeros((NDENS, 384), F32)
    pairs = spheres // 2
    for b in range(pairs):
        part = own_uncovered(unc_ref, b)
        out_ref[b : b + 1, own:] = part[:, :384]
        out_ref[pairs + b : pairs + b + 1, own : own + 256] = part[:, 384:]


def sweep_call(before, own, after, t, rest, scales, unc):
    lanes = own.shape[1]
    spheres = lanes // LP
    return pl.pallas_call(
        sweep_kernel,
        in_specs=[VMEM] * 7,
        out_specs=[VMEM] * 2,
        out_shape=[
            jax.ShapeDtypeStruct((spheres, NDENS, LM), F32),
            jax.ShapeDtypeStruct((NDENS, lanes + 384), F32),
        ],
        scratch_shapes=[pltpu.VMEM((2 * NDENS, 3 * lanes), BF)] * 2
        + [pltpu.VMEM((2 * NDENS, lanes + 2 * REACH * LP), BF)] * 2,
        compiler_params=PARAMS,
        cost_estimate=pl.CostEstimate(
            flops=3 * spheres * 2 * 64 * 512 * 256,
            bytes_accessed=2 * spheres * 262144,
            transcendentals=0,
        ),
        name="sweeps",
    )(before, own, after, t, rest, scales, unc)


def fock_kernel(pay_ref, y_ref, tile_ref, *rest):
    out_ref, charge = rest[-2:]
    own = pay_ref.shape[1] - 384
    pairs = own // (2 * LP)
    width = pairs * PN
    rows = [pay_ref[:, b * 2 * LP : (b + 1) * 2 * LP] for b in range(pairs)]
    hi, lo = halves(jnp.concatenate(rows, 0))
    r = jnp.dot(jnp.concatenate([hi, lo], 1), y_ref[...], preferred_element_type=F32)
    out = r[:, :PN] + r[:, PN:]
    for b in range(pairs):
        unc = jnp.concatenate(
            [pay_ref[b : b + 1, own:], pay_ref[pairs + b : pairs + b + 1, own : own + 256]], 1
        )
        weight = unc * (4.0 * math.pi / NG)
        charge[:, b * PN : (b + 1) * PN] = (out[b * NDENS : (b + 1) * NDENS] * weight).astype(BF)
    total = rest[0][...] if len(rest) == 3 else None
    for p in range(width // PIECE):
        part = lax.dot_general(
            charge[:, p * PIECE : (p + 1) * PIECE],
            tile_ref[:, p * PIECE : (p + 1) * PIECE],
            (((1,), (1,)), ((), ())),
            preferred_element_type=F32,
        )
        total = part if total is None else total + part
    out_ref[...] = total


def fock_call(pay, wt, tiles, before=None):
    aux, width = tiles.shape
    more = [] if before is None else [before]
    return pl.pallas_call(
        fock_kernel,
        in_specs=[VMEM] * (3 + len(more)),
        out_specs=VMEM,
        out_shape=jax.ShapeDtypeStruct((NDENS, aux), F32),
        scratch_shapes=[pltpu.VMEM((NDENS, width), BF)],
        compiler_params=PARAMS,
        cost_estimate=pl.CostEstimate(
            flops=2 * NDENS * aux * width, bytes_accessed=2 * aux * width, transcendentals=0
        ),
        name="fock",
    )(pay, wt, tiles, *more)


def trade(x, axis, k):
    count = lax.axis_size(axis)
    return lax.ppermute(x, axis, [(i, i ^ k) for i in range(count)])


def shift(x, axis, k):
    count = lax.axis_size(axis)
    return lax.ppermute(x, axis, [(i, (i + k) % count) for i in range(count)])


def from_beside(x):
    axes = ("sph", "fit")
    count = lax.axis_size("sph") * lax.axis_size("fit")
    up = [(i, (i + 1) % count) for i in range(count)]
    down = [((i + 1) % count, i) for i in range(count)]
    return lax.ppermute(x, axes, up), lax.ppermute(x, axes, down)


def body(tiles, coefs, centres, radii, neighbours, counts):
    spheres, slots = neighbours.shape
    fits = lax.axis_size("fit")
    sphs = lax.axis_size("sph")
    assert fits & (fits - 1) == 0 and sphs & (sphs - 1) == 0
    assert spheres % (2 * QUAD) == 0 and spheres == slots == 2 * REACH
    w, wt = (jnp.asarray(a) for a in even_weights())
    scales = jnp.asarray(lane_scales())

    width = spheres * NG
    own = pack_call(centres, radii, neighbours, counts)
    before, after = from_beside(own)
    sent = phi_call(coefs, tiles, width)
    sent, near_tiles = sent[: fits - 1], sent[fits - 1 :]
    sent, before, after = lax.optimization_barrier((sent, before, after))
    got = [trade(sent[k - 1], "fit", k) for k in range(1, fits)]
    below_own, last_own = REACH // QUAD, (REACH + spheres) // QUAD
    soon = range(below_own - SOONER, last_own)
    later = [*range(below_own - SOONER), *range(last_own, last_own + below_own)]
    t, unc, mine, tile = pair_call(before, own, after, list(soon), coefs, tiles)
    rhs = rhs_call([mine, *got], unc, w)
    below, above = from_beside(rhs)
    late, _ = lax.optimization_barrier((own, rhs))
    rest, _ = pair_call(before, late, after, later)
    moments, pay = sweep_call(below, rhs, above, t, rest, scales, unc)
    others = [trade(pay, "fit", k) for k in range(1, fits)]
    fock = fock_call(pay, wt, tile)
    for other, near in zip(others, near_tiles):
        fock = fock_call(other, wt, near, fock)
    fock = fock + trade(fock, "sph", 1)
    bit = 2
    while bit < sphs:
        ks = [k for k in (bit, 2 * bit, 3 * bit) if k < sphs]
        if 4 * bit == sphs:
            parts = [shift(fock, "sph", k) for k in ks]
        else:
            parts = [trade(fock, "sph", k) for k in ks]
        fock = functools.reduce(jnp.add, parts, fock)
        bit *= 4
    return moments, fock


def solution(mesh):
    placed = (
        P("fit", "sph"),
        P(None, "fit"),
        P(None, ("sph", "fit")),
        P(("sph", "fit")),
        P(("sph", "fit"), None),
        P(("sph", "fit")),
    )
    return jax.shard_map(
        body,
        mesh=mesh,
        in_specs=placed,
        out_specs=(P(("sph", "fit"), None, None), P(None, "fit")),
        check_vma=False,
    )
```

```python
import functools
import math

import jax
import jax.numpy as jnp
import ml_dtypes
import numpy as np
from jax import lax
from jax.experimental import pallas as pl
from jax.experimental.pallas import tpu as pltpu
from jax.sharding import PartitionSpec as P

DEGREE = 6
LM = 49
NTH = 16
NPHI = 20
NG = 320
NDENS = 16
LP = 64
QUAD = 4
QN = QUAD * NG
PN = 2 * NG
PIECE = 2560
PARAMS = pltpu.CompilerParams(vmem_limit_bytes=16 << 20)
VMEM = pl.BlockSpec(memory_space=pltpu.VMEM)
SMEM = pl.BlockSpec(memory_space=pltpu.SMEM)
BAND = 0.1
REACH = 8
SOONER = 1
BF = jnp.bfloat16
F32 = jnp.float32


def gam(l, m):
    return (l + m - 1) * (l - 1 - m) / ((2 * l - 1) * (2 * l - 3))


def tables():
    c = -1.0 + (2.0 * np.arange(NTH) + 1.0) / NTH
    f = (np.arange(NPHI) + 0.5) * (2 * np.pi / NPHI)
    z = np.repeat(c, NPHI)
    s = np.sqrt(1 - z * z)
    az = np.tile(f, NTH)
    x, y = s * np.cos(az), s * np.sin(az)
    cos, sin = [np.ones_like(x)], [np.zeros_like(x)]
    for m in range(1, DEGREE + 1):
        cos.append(cos[m - 1] * x - sin[m - 1] * y)
        sin.append(cos[m - 1] * y + sin[m - 1] * x)
    ys, scale, invert = np.zeros((LM, NG)), np.zeros(LM), np.zeros(LM)
    for m in range(DEGREE + 1):
        q, lead = {m: np.ones_like(x)}, {m: 1.0}
        for odd in range(1, 2 * m, 2):
            lead[m] *= odd
        for l in range(m + 1, DEGREE + 1):
            q[l] = z * q[l - 1] - (gam(l, m) * q[l - 2] if l > m + 1 else 0.0)
            lead[l] = lead[l - 1] * (2 * l - 1) / (l - m)
        for l in range(m, DEGREE + 1):
            n = math.sqrt(
                (2 * l + 1) / (4 * math.pi) * math.factorial(l - m) / math.factorial(l + m)
            )
            n *= math.sqrt(2.0) if m else 1.0
            for sign, trig in ((1, cos[m]), (-1, sin[m])):
                if m == 0 and sign < 0:
                    continue
                i = l * l + l + sign * m
                ys[i] = n * lead[l] * q[l] * trig
                scale[i] = n * lead[l] * 4 * math.pi / (2 * l + 1)
                invert[i] = (2 * l + 1) / (4 * math.pi)
    return np.stack([x, y, z]), ys, scale, invert


def split(a):
    a = np.asarray(a, np.float32)
    hi = a.astype(ml_dtypes.bfloat16)
    return hi, (a - hi.astype(np.float32)).astype(ml_dtypes.bfloat16)


def halves(x):
    hi = x.astype(BF)
    return hi, (x - hi.astype(F32)).astype(BF)


def pair_weights():
    dirs, ys, _, _ = tables()
    w = np.zeros((2 * NG, 2 * LP))
    wy = ys.T * (4 * math.pi / NG)
    w[:NG, :LM] = wy
    w[NG:, LP : LP + LM] = wy
    d = np.zeros((8, 2 * NG), np.float32)
    d[:3, :NG] = dirs
    d[:3, NG:] = dirs
    return np.concatenate(split(w), 1), d


def even_weights():
    _, ys, _, _ = tables()
    w = np.zeros((PN, 2 * LP))
    w[:NG, :LM] = ys.T
    w[NG:, LP : LP + LM] = ys.T
    hi, lo = split(w.T)
    deep = np.block([[hi, lo], [hi, np.zeros_like(lo)]])
    return np.concatenate(split(w), 1), deep


def lane_scales():
    _, _, scale, invert = tables()
    rows = np.zeros((8, 2 * LP), np.float32)
    for h in (0, LP):
        rows[0, h : h + LM] = scale * invert
        rows[1, h : h + LM] = invert
    return rows


def chunk_piece(k, width, p):
    at = (lax.axis_index("fit") ^ k) * width + p * PIECE
    return pl.ds(pl.multiple_of(at, 128), PIECE)


def code(x):
    top = jnp.maximum(jnp.max(jnp.abs(x), axis=1, keepdims=True), 1e-30)
    power = jnp.floor(jnp.log2(top)) - 13.0
    q = jnp.floor(x * jnp.exp2(-power) + 0.5).astype(jnp.int32)
    tail = jnp.broadcast_to(power, (x.shape[0], 128)).astype(jnp.int32)
    return q.astype(jnp.int16), tail.astype(jnp.int16)


def decode(ref, ls):
    width = ref.shape[1] - 128
    power = ref[:, width:].astype(jnp.int32).astype(F32)[:, 0:1]
    return ref[:, ls].astype(jnp.int32).astype(F32) * jnp.exp2(power)


def phi_kernel(width, far_coef_ref, far_ref, *rest):
    outs, (tile_ref, full, coef_ref, sem, coef_sem) = rest[:-5], rest[-5:]
    first = pltpu.make_async_copy(far_coef_ref, coef_ref, coef_sem)
    first.start()
    per = width // PIECE
    todo = [(k, p) for k in [*range(1, len(outs)), 0] for p in range(per)]
    copies = []
    for i, (k, p) in enumerate(todo):
        at = chunk_piece(k, width, p)
        copies.append(pltpu.make_async_copy(far_ref.at[:, at], tile_ref.at[:, at], sem.at[i]))
        copies[-1].start()
    first.wait()
    for (k, p), copy in zip(todo, copies):
        copy.wait()
        out = full if k else outs[0]
        out[:, p * PIECE : (p + 1) * PIECE] = jnp.dot(
            coef_ref[...], tile_ref[:, chunk_piece(k, width, p)], preferred_element_type=F32
        )
        if k and p == per - 1:
            q, tail = code(full[...])
            outs[k][:, :width] = q
            outs[k][:, width:] = tail


def phi_call(coefs, tiles, width):
    aux, points = tiles.shape
    count = points // width
    return pl.pallas_call(
        functools.partial(phi_kernel, width),
        in_specs=[pl.BlockSpec(memory_space=pltpu.HBM)] * 2,
        out_specs=[VMEM] * (count + 1),
        out_shape=[jax.ShapeDtypeStruct((NDENS, width), F32)]
        + [jax.ShapeDtypeStruct((NDENS, width + 128), jnp.int16)] * (count - 1)
        + [jax.ShapeDtypeStruct(tiles.shape, tiles.dtype)],
        scratch_shapes=[
            pltpu.VMEM((NDENS, width), F32),
            pltpu.VMEM(coefs.shape, coefs.dtype),
            pltpu.SemaphoreType.DMA((points // PIECE,)),
            pltpu.SemaphoreType.DMA,
        ],
        compiler_params=PARAMS,
        cost_estimate=pl.CostEstimate(
            flops=2 * NDENS * aux * points,
            bytes_accessed=(2 * aux + 4 * NDENS) * points,
            transcendentals=0,
        ),
        name="phi",
    )(*(pltpu.with_memory_space_constraint(a, pltpu.HBM) for a in (coefs, tiles)))


def pack_kernel(centre_ref, radius_ref, nbr_ref, cnt_ref, out_ref, c, r, n, k, sem):
    copies = [
        pltpu.make_async_copy(a, b, sem.at[i])
        for i, (a, b) in enumerate(zip((centre_ref, radius_ref, nbr_ref, cnt_ref), (c, r, n, k)))
    ]
    for copy in copies:
        copy.start()
    for copy in copies:
        copy.wait()
    spheres, slots = n.shape
    out_ref[...] = jnp.zeros_like(out_ref)
    out_ref[0:3, :] = c[...]
    out_ref[3:4, :] = r[...]
    out_ref[4:5, :] = k[...].astype(F32)
    out_ref[8:, :] = n[...].astype(F32)


def pack_call(centres, radii, neighbours, counts):
    spheres, slots = neighbours.shape
    args = (centres, radii.reshape(1, spheres), neighbours, counts.reshape(1, spheres))
    return pl.pallas_call(
        pack_kernel,
        in_specs=[pl.BlockSpec(memory_space=pltpu.HBM)] * 4,
        out_specs=VMEM,
        out_shape=jax.ShapeDtypeStruct((8 + spheres, spheres), F32),
        scratch_shapes=[pltpu.VMEM(a.shape, a.dtype) for a in args]
        + [pltpu.SemaphoreType.DMA((4,))],
        compiler_params=PARAMS,
        name="pack",
    )(*(pltpu.with_memory_space_constraint(a, pltpu.HBM) for a in args))


def pair_build(e, geo, mask, dir_ref, bh):
    lane = lax.broadcasted_iota(jnp.int32, (8, 128), 1)
    sub = lax.broadcasted_iota(jnp.int32, (8, 128), 0)
    own = jnp.broadcast_to(geo[pl.ds(e + 8, 1), :], (8, 128))
    mrow = jnp.broadcast_to(mask[pl.ds(e, 1), :], (8, 128))
    cols = []
    for g, start in ((0, e), (1, e + 9)):
        near = geo[pl.ds(start, 8), :]
        valid = jnp.sum(jnp.where(lane == sub + 8 * g, mrow, 0.0), axis=1, keepdims=True)
        on = valid > 0.0
        ir = 1.0 / jnp.where(on, near[:, 3:4], 1.0)
        off = jnp.where(on, own - near, 0.0)
        c = [off[:, 0:1] * ir, off[:, 1:2] * ir, off[:, 2:3] * ir, own[:, 3:4] * ir, valid]
        cols.append([jnp.broadcast_to(q, (8, 128)) for q in c])
    mid = [jnp.where(lane < 64, a, b) for a, b in zip(*cols)]
    sums = []
    for t in range(5):
        ox, oy, oz, q, valid = cols[0] if t < 2 else (mid if t == 2 else cols[1])
        ls = slice(128 * t, 128 * t + 128)
        x = ox + q * dir_ref[0:1, ls]
        y = oy + q * dir_ref[1:2, ls]
        z = oz + q * dir_ref[2:3, ls]
        r2 = x * x + y * y + z * z
        ramp = jnp.clip((1.0 - jnp.sqrt(r2)) * (1.0 / BAND), 0.0, 1.0)
        chi = ramp * ramp * (3.0 - 2.0 * ramp) * valid
        sums.append(jnp.sum(chi, axis=0, keepdims=True))
        cos, sin = [chi, chi * x], [None, chi * y]
        for m in range(2, DEGREE + 1):
            cos.append(cos[m - 1] * x - sin[m - 1] * y)
            sin.append(cos[m - 1] * y + sin[m - 1] * x)
        out = [None] * LM
        for m in range(DEGREE + 1):
            qm = {}
            for l in range(m, DEGREE + 1):
                if l == m + 1:
                    qm[l] = z
                elif l == m + 2:
                    qm[l] = z * z - gam(l, m) * r2
                elif l > m + 2:
                    qm[l] = z * qm[l - 1] - (gam(l, m) * r2) * qm[l - 2]
                for sign, trig in ((1, cos[m]), (-1, sin[m])):
                    if m == 0 and sign < 0:
                        continue
                    out[l * l + l + sign * m] = trig if l == m else trig * qm[l]
        out.append(jnp.zeros((8, 128), F32))
        for p in range(25):
            both = jnp.concatenate([out[2 * p], out[2 * p + 1]], axis=0)
            bh[16 * p : 16 * p + 16, ls] = both.astype(BF)
    return sums


def pair_finish(e, w_ref, t_ref, bh):
    r = jnp.dot(bh[...], w_ref[...], preferred_element_type=F32)
    tt = r[: LM * 8, : 2 * LP] + r[: LM * 8, 2 * LP :]
    a = jnp.swapaxes(tt.reshape(LM, 8, 2 * LP), 0, 1)
    a = jnp.concatenate([a, jnp.zeros((8, LP - LM, 2 * LP), F32)], 1).reshape(8 * LP, 2 * LP)
    hi, lo = halves(a)
    t_ref[e, :, : 2 * LP] = hi
    t_ref[e, :, 2 * LP :] = lo


def uncover(sums):
    low = lax.broadcasted_iota(jnp.int32, (1, 128), 1) < 64
    swap = lambda v: pltpu.roll(v, 64, 1)
    three = []
    for s in sums:
        r2, r3, r4 = swap(s[2]), swap(s[3]), swap(s[4])
        three.append([s[0] + jnp.where(low, r2, r3), s[1] + jnp.where(low, r3, r4), s[2] + r4])
    a, b = three
    b0, b1, b2 = swap(b[0]), swap(b[1]), swap(b[2])
    tiles = [a[0], a[1], jnp.where(low, a[2], b0), jnp.where(low, b0, b1), jnp.where(low, b1, b2)]
    return [jnp.maximum(0.0, 1.0 - t) for t in tiles]


def pair_setup(before_ref, own_ref, after_ref, geo, mask):
    spheres = own_ref.shape[1]
    slots = 2 * REACH
    wide = spheres + 2 * REACH
    packs = (before_ref, own_ref, after_ref)
    rows = jnp.concatenate([p[0:8, :] for p in packs], axis=1)
    rows = jnp.concatenate([rows, jnp.zeros((8, 128 - rows.shape[1]), F32)], axis=1)
    rows = jnp.concatenate([rows, jnp.zeros((120, 128), F32)], axis=0)
    geo[...] = rows.T[: geo.shape[0]]
    first = (lax.axis_index("sph") * lax.axis_size("fit") + lax.axis_index("fit")) * spheres
    row = lax.broadcasted_iota(jnp.int32, (wide, slots), 0) + (first - REACH)
    slot = lax.broadcasted_iota(jnp.int32, (wide, slots), 1)
    lists = [before_ref[8 + spheres - REACH :, :], own_ref[8:, :], after_ref[8 : 8 + REACH, :]]
    rel = jnp.concatenate(lists, axis=0) - row.astype(F32)
    listed = slot.astype(F32) < geo[spheres - REACH : 2 * spheres + REACH, 4:5]
    lane = lax.broadcasted_iota(jnp.int32, (wide, 128), 1)
    found = jnp.zeros((wide, 128), F32)
    for c in range(slots):
        gap = c - REACH if c < REACH else c - REACH + 1
        hit = jnp.where(listed & (rel == float(gap)), 1.0, 0.0)
        hit = jnp.max(hit, axis=1, keepdims=True)
        found = jnp.where(lane == c, hit, found)
    mask[...] = found


def pair_work(quads, geo, mask, dir_ref, w_ref, t_ref, unc_ref, bhs):
    for b, quad in enumerate(quads):
        sums = []
        for u in range(QUAD):
            sums.append(pair_build(quad * QUAD + u, geo, mask, dir_ref, bhs[u]))
            pair_finish(b * QUAD + u, w_ref, t_ref, bhs[u])
        if unc_ref is not None:
            tiles = uncover(sums[:2]) + uncover(sums[2:])
            for t, v in enumerate(tiles):
                unc_ref[b, :, 128 * t : 128 * t + 128] = v


def first_pair_kernel(
    quads, before_ref, own_ref, after_ref, dir_ref, w_ref, t_ref, unc_ref, geo, mask, *bhs
):
    pair_setup(before_ref, own_ref, after_ref, geo, mask)
    pair_work(quads, geo, mask, dir_ref, w_ref, t_ref, unc_ref, bhs)


def next_pair_kernel(quads, geo, mask, dir_ref, w_ref, t_ref, *bhs):
    pair_work(quads, geo, mask, dir_ref, w_ref, t_ref, None, bhs)


def pair_call(quads, consts, packs=None, known=None):
    count = len(quads)
    out_shape = [jax.ShapeDtypeStruct((count * QUAD, 8 * LP, 4 * LP), BF)]
    if known is None:
        kernel, args = first_pair_kernel, packs
        spheres = packs[1].shape[1]
        out_shape += [
            jax.ShapeDtypeStruct((count, 1, QN), F32),
            jax.ShapeDtypeStruct((3 * spheres, 128), F32),
            jax.ShapeDtypeStruct((spheres + 2 * REACH, 128), F32),
        ]
    else:
        kernel, args = next_pair_kernel, known
    return pl.pallas_call(
        functools.partial(kernel, quads),
        in_specs=[VMEM] * (len(args) + 2),
        out_specs=[VMEM] * len(out_shape),
        scratch_shapes=[pltpu.VMEM((400, 2 * NG), BF)] * QUAD,
        out_shape=out_shape,
        compiler_params=PARAMS,
        cost_estimate=pl.CostEstimate(
            flops=count * QUAD * 2 * 400 * 640 * 256,
            bytes_accessed=count * QUAD * 262144,
            transcendentals=0,
        ),
        name="pairs",
    )(*args, *consts)


def own_uncovered(unc_ref, b):
    b = b + SOONER * QUAD // 2
    return unc_ref[b // 2, :, b % 2 * PN : (b % 2 + 1) * PN]


def rhs_kernel(count, *refs):
    phis, (unc_ref, w_ref, out_ref) = refs[:count], refs[count:]
    pairs = out_ref.shape[1] // (2 * LP)
    rows = []
    for b in range(pairs):
        ls = slice(b * PN, (b + 1) * PN)
        total = phis[0][:, ls]
        for p in phis[1:]:
            total = total + decode(p, ls)
        rows.append(total * own_uncovered(unc_ref, b))
    hi, lo = halves(jnp.concatenate(rows, 0))
    n = pairs * NDENS
    r = jnp.dot(jnp.concatenate([hi, lo], 0), w_ref[...], preferred_element_type=F32)
    out = r[:n, : 2 * LP] + r[:n, 2 * LP :] + r[n:, : 2 * LP]
    out = out * (-4.0 * math.pi / NG)
    for b in range(pairs):
        out_ref[:, b * 2 * LP : (b + 1) * 2 * LP] = out[b * NDENS : (b + 1) * NDENS]


def rhs_call(phis, unc, w):
    spheres = phis[0].shape[1] // NG
    return pl.pallas_call(
        functools.partial(rhs_kernel, len(phis)),
        in_specs=[VMEM] * (len(phis) + 2),
        out_specs=VMEM,
        compiler_params=PARAMS,
        out_shape=jax.ShapeDtypeStruct((NDENS, spheres * LP), F32),
        cost_estimate=pl.CostEstimate(
            flops=6 * NDENS * spheres * NG * 256, bytes_accessed=1700000, transcendentals=0
        ),
        name="rhs",
    )(*phis, unc, w)


def gather_field(t_refs, shift, x, xs, e):
    low = lax.broadcasted_iota(jnp.int32, (NDENS, 128), 1) < LP
    parts = []
    for odd in (0, 1):
        below, above = (x, xs) if odd == 0 else (xs, x)
        lo_at = e * LP
        up_at = (e + 8) * LP if odd == 0 else (e + 10) * LP
        lhs = jnp.concatenate(
            [below[:, lo_at : lo_at + 8 * LP], above[:, up_at : up_at + 8 * LP]], 0
        )
        lowest, most = REACH - SOONER * QUAD, t_refs[0].shape[0]
        at = e + odd + shift - lowest
        if 0 <= at < most:
            t = t_refs[0][at]
        else:
            t = t_refs[1][at + lowest - (most if at > 0 else 0)]
        r = jnp.dot(lhs, t, preferred_element_type=F32)
        n = NDENS
        a = r[0:n, : 2 * LP] + r[n : 2 * n, : 2 * LP] + r[0:n, 2 * LP :]
        b = r[2 * n : 3 * n, : 2 * LP] + r[3 * n :, : 2 * LP] + r[2 * n : 3 * n, 2 * LP :]
        parts.append((a, b))
    (a0, b0), (a1, b1) = parts
    return jnp.where(low, a0, b1) + pltpu.roll(jnp.where(low, a1, b0), LP, 1)


def put_scaled(x, at, value):
    hi, lo = halves(value)
    x[0:NDENS, at : at + 128] = hi
    x[NDENS:, at : at + 128] = lo


def put_shifted(xs, x):
    v = x[...].astype(F32)
    xs[...] = jnp.concatenate([v[:, LP:], v[:, :LP]], 1).astype(BF)


def sweep_kernel(
    before_ref, own_ref, after_ref, t_ref, rest_ref, sc_ref, unc_ref, m_ref, out_ref,
    x, xs, z, zs
):
    own = own_ref.shape[1]
    spheres = own // LP
    right = lambda at: (before_ref, own_ref, after_ref)[at // own][:, at % own : at % own + 128]
    for at in range(0, 3 * own, 128):
        put_scaled(x, at, right(at) * sc_ref[0:1, :])
    put_shifted(xs, x)
    for e in range(0, spheres + 2 * REACH, 2):
        new = right((e + spheres - REACH) * LP) + gather_field((t_ref, rest_ref), 0, x, xs, e)
        put_scaled(z, e * LP, new * sc_ref[0:1, :])
    put_shifted(zs, z)
    for e in range(0, spheres, 2):
        new = own_ref[:, e * LP : e * LP + 128] + gather_field((t_ref, rest_ref), REACH, z, zs, e)
        new = new * sc_ref[1:2, :]
        m_ref[e] = new[:, :LM]
        m_ref[e + 1] = pltpu.roll(new, LP, 1)[:, :LM]
        out_ref[:, e * LP : e * LP + 128] = new
    out_ref[:, own:] = jnp.zeros((NDENS, 384), F32)
    pairs = spheres // 2
    for b in range(pairs):
        part = own_uncovered(unc_ref, b)
        out_ref[b : b + 1, own:] = part[:, :384]
        out_ref[pairs + b : pairs + b + 1, own : own + 256] = part[:, 384:]


def sweep_call(before, own, after, t, rest, scales, unc):
    lanes = own.shape[1]
    spheres = lanes // LP
    return pl.pallas_call(
        sweep_kernel,
        in_specs=[VMEM] * 7,
        out_specs=[VMEM] * 2,
        out_shape=[
            jax.ShapeDtypeStruct((spheres, NDENS, LM), F32),
            jax.ShapeDtypeStruct((NDENS, lanes + 384), F32),
        ],
        scratch_shapes=[pltpu.VMEM((2 * NDENS, 3 * lanes), BF)] * 2
        + [pltpu.VMEM((2 * NDENS, lanes + 2 * REACH * LP), BF)] * 2,
        compiler_params=PARAMS,
        cost_estimate=pl.CostEstimate(
            flops=3 * spheres * 2 * 64 * 512 * 256,
            bytes_accessed=2 * spheres * 262144,
            transcendentals=0,
        ),
        name="sweeps",
    )(before, own, after, t, rest, scales, unc)


def fock_kernel(k, pay_ref, y_ref, tile_ref, *rest):
    out_ref, charge = rest[-2:]
    own = pay_ref.shape[1] - 384
    pairs = own // (2 * LP)
    width = pairs * PN
    rows = [pay_ref[:, b * 2 * LP : (b + 1) * 2 * LP] for b in range(pairs)]
    hi, lo = halves(jnp.concatenate(rows, 0))
    r = jnp.dot(jnp.concatenate([hi, lo], 1), y_ref[...], preferred_element_type=F32)
    out = r[:, :PN] + r[:, PN:]
    for b in range(pairs):
        unc = jnp.concatenate(
            [pay_ref[b : b + 1, own:], pay_ref[pairs + b : pairs + b + 1, own : own + 256]], 1
        )
        weight = unc * (4.0 * math.pi / NG)
        charge[:, b * PN : (b + 1) * PN] = (out[b * NDENS : (b + 1) * NDENS] * weight).astype(BF)
    total = rest[0][...] if len(rest) == 3 else None
    for p in range(width // PIECE):
        part = lax.dot_general(
            charge[:, p * PIECE : (p + 1) * PIECE],
            tile_ref[:, chunk_piece(k, width, p)],
            (((1,), (1,)), ((), ())),
            preferred_element_type=F32,
        )
        total = part if total is None else total + part
    out_ref[...] = total


def fock_call(k, pay, wt, tiles, width, before=None):
    aux = tiles.shape[0]
    more = [] if before is None else [before]
    return pl.pallas_call(
        functools.partial(fock_kernel, k),
        in_specs=[VMEM] * (3 + len(more)),
        out_specs=VMEM,
        out_shape=jax.ShapeDtypeStruct((NDENS, aux), F32),
        scratch_shapes=[pltpu.VMEM((NDENS, width), BF)],
        compiler_params=PARAMS,
        cost_estimate=pl.CostEstimate(
            flops=2 * NDENS * aux * width, bytes_accessed=2 * aux * width, transcendentals=0
        ),
        name="fock",
    )(pay, wt, tiles, *more)


def trade(x, axis, k):
    count = lax.axis_size(axis)
    return lax.ppermute(x, axis, [(i, i ^ k) for i in range(count)])


def shift(x, axis, k):
    count = lax.axis_size(axis)
    return lax.ppermute(x, axis, [(i, (i + k) % count) for i in range(count)])


def from_beside(x):
    axes = ("sph", "fit")
    count = lax.axis_size("sph") * lax.axis_size("fit")
    up = [(i, (i + 1) % count) for i in range(count)]
    down = [((i + 1) % count, i) for i in range(count)]
    return lax.ppermute(x, axes, up), lax.ppermute(x, axes, down)


def body(tiles, coefs, centres, radii, neighbours, counts):
    spheres, slots = neighbours.shape
    fits = lax.axis_size("fit")
    sphs = lax.axis_size("sph")
    assert fits & (fits - 1) == 0 and sphs & (sphs - 1) == 0
    assert spheres % (2 * QUAD) == 0 and spheres == slots == 2 * REACH
    w, wt = (jnp.asarray(a) for a in even_weights())
    scales = jnp.asarray(lane_scales())

    width = spheres * NG
    own = pack_call(centres, radii, neighbours, counts)
    before, after = from_beside(own)
    *phis, near_tiles = phi_call(coefs, tiles, width)
    phis, before, after = lax.optimization_barrier((phis, before, after))
    got = [trade(phis[k], "fit", k) for k in range(1, fits)]
    below_own, last_own = REACH // QUAD, (REACH + spheres) // QUAD
    soon = [*range(below_own - SOONER, last_own)]
    later = [*range(below_own - SOONER), *range(last_own, last_own + below_own)]
    pw, dirs = pair_weights()
    consts = (jnp.asarray(dirs), jnp.asarray(pw))
    t, unc, geo, mask = pair_call(soon, consts, packs=(before, own, after))
    rhs = rhs_call([phis[0], *got], unc, w)
    below, above = from_beside(rhs)
    mask, _ = lax.optimization_barrier((mask, rhs))
    (rest,) = pair_call(later, consts, known=(geo, mask))
    moments, pay = sweep_call(below, rhs, above, t, rest, scales, unc)
    others = [trade(pay, "fit", k) for k in range(1, fits)]
    fock = fock_call(0, pay, wt, near_tiles, width)
    for k in range(1, fits):
        fock = fock_call(k, others[k - 1], wt, near_tiles, width, fock)
    fock = fock + trade(fock, "sph", 1)
    bit = 2
    while bit < sphs:
        ks = [k for k in (bit, 2 * bit, 3 * bit) if k < sphs]
        if 4 * bit == sphs:
            parts = [shift(fock, "sph", k) for k in ks]
        else:
            parts = [trade(fock, "sph", k) for k in ks]
        fock = functools.reduce(jnp.add, parts, fock)
        bit *= 4
    return moments, fock


def solution(mesh):
    placed = (
        P("fit", "sph"),
        P(None, "fit"),
        P(None, ("sph", "fit")),
        P(("sph", "fit")),
        P(("sph", "fit"), None),
        P(("sph", "fit")),
    )
    return jax.shard_map(
        body,
        mesh=mesh,
        in_specs=placed,
        out_specs=(P(("sph", "fit"), None, None), P(None, "fit")),
        check_vma=False,
    )
```

```python
import functools
import math

import jax
import jax.numpy as jnp
import ml_dtypes
import numpy as np
from jax import lax
from jax.experimental import pallas as pl
from jax.experimental.pallas import tpu as pltpu
from jax.sharding import PartitionSpec as P

DEGREE = 6
LM = 49
NTH = 16
NPHI = 20
NG = 320
NDENS = 16
LP = 64
QUAD = 4
QN = QUAD * NG
PN = 2 * NG
PIECE = 2560
PARAMS = pltpu.CompilerParams(vmem_limit_bytes=16 << 20)
VMEM = pl.BlockSpec(memory_space=pltpu.VMEM)
SMEM = pl.BlockSpec(memory_space=pltpu.SMEM)
BAND = 0.1
REACH = 8
SOONER = 1
BF = jnp.bfloat16
F32 = jnp.float32


def gam(l, m):
    return (l + m - 1) * (l - 1 - m) / ((2 * l - 1) * (2 * l - 3))


def tables():
    c = -1.0 + (2.0 * np.arange(NTH) + 1.0) / NTH
    f = (np.arange(NPHI) + 0.5) * (2 * np.pi / NPHI)
    z = np.repeat(c, NPHI)
    s = np.sqrt(1 - z * z)
    az = np.tile(f, NTH)
    x, y = s * np.cos(az), s * np.sin(az)
    cos, sin = [np.ones_like(x)], [np.zeros_like(x)]
    for m in range(1, DEGREE + 1):
        cos.append(cos[m - 1] * x - sin[m - 1] * y)
        sin.append(cos[m - 1] * y + sin[m - 1] * x)
    ys, scale, invert = np.zeros((LM, NG)), np.zeros(LM), np.zeros(LM)
    for m in range(DEGREE + 1):
        q, lead = {m: np.ones_like(x)}, {m: 1.0}
        for odd in range(1, 2 * m, 2):
            lead[m] *= odd
        for l in range(m + 1, DEGREE + 1):
            q[l] = z * q[l - 1] - (gam(l, m) * q[l - 2] if l > m + 1 else 0.0)
            lead[l] = lead[l - 1] * (2 * l - 1) / (l - m)
        for l in range(m, DEGREE + 1):
            n = math.sqrt(
                (2 * l + 1) / (4 * math.pi) * math.factorial(l - m) / math.factorial(l + m)
            )
            n *= math.sqrt(2.0) if m else 1.0
            for sign, trig in ((1, cos[m]), (-1, sin[m])):
                if m == 0 and sign < 0:
                    continue
                i = l * l + l + sign * m
                ys[i] = n * lead[l] * q[l] * trig
                scale[i] = n * lead[l] * 4 * math.pi / (2 * l + 1)
                invert[i] = (2 * l + 1) / (4 * math.pi)
    return np.stack([x, y, z]), ys, scale, invert


def split(a):
    a = np.asarray(a, np.float32)
    hi = a.astype(ml_dtypes.bfloat16)
    return hi, (a - hi.astype(np.float32)).astype(ml_dtypes.bfloat16)


def halves(x):
    hi = x.astype(BF)
    return hi, (x - hi.astype(F32)).astype(BF)


def pair_weights():
    dirs, ys, _, _ = tables()
    w = np.zeros((2 * NG, 2 * LP))
    wy = ys.T * (4 * math.pi / NG)
    w[:NG, :LM] = wy
    w[NG:, LP : LP + LM] = wy
    d = np.zeros((8, 2 * NG), np.float32)
    d[:3, :NG] = dirs
    d[:3, NG:] = dirs
    return np.concatenate(split(w), 1), d


def even_weights():
    _, ys, _, _ = tables()
    w = np.zeros((PN, 2 * LP))
    w[:NG, :LM] = ys.T
    w[NG:, LP : LP + LM] = ys.T
    hi, lo = split(w.T)
    deep = np.block([[hi, lo], [hi, np.zeros_like(lo)]])
    return np.concatenate(split(w), 1), deep


def lane_scales():
    _, _, scale, invert = tables()
    rows = np.zeros((8, 2 * LP), np.float32)
    for h in (0, LP):
        rows[0, h : h + LM] = scale * invert
        rows[1, h : h + LM] = invert
    return rows


def chunk_piece(k, width, p):
    at = (lax.axis_index("fit") ^ k) * width + p * PIECE
    return pl.ds(pl.multiple_of(at, 128), PIECE)


def code(x):
    top = jnp.maximum(jnp.max(jnp.abs(x), axis=1, keepdims=True), 1e-30)
    power = jnp.floor(jnp.log2(top)) - 13.0
    q = jnp.floor(x * jnp.exp2(-power) + 0.5).astype(jnp.int32)
    tail = jnp.broadcast_to(power, (x.shape[0], 128)).astype(jnp.int32)
    return q.astype(jnp.int16), tail.astype(jnp.int16)


def decode(ref, ls):
    width = ref.shape[1] - 128
    power = ref[:, width:].astype(jnp.int32).astype(F32)[:, 0:1]
    return ref[:, ls].astype(jnp.int32).astype(F32) * jnp.exp2(power)


def phi_kernel(width, far_coef_ref, far_ref, *rest):
    outs, (tile_ref, full, coef_ref, sem, coef_sem) = rest[:-5], rest[-5:]
    first = pltpu.make_async_copy(far_coef_ref, coef_ref, coef_sem)
    first.start()
    per = width // PIECE
    todo = [(k, p) for k in [*range(1, len(outs)), 0] for p in range(per)]
    copies = []
    for i, (k, p) in enumerate(todo):
        at = chunk_piece(k, width, p)
        copies.append(pltpu.make_async_copy(far_ref.at[:, at], tile_ref.at[:, at], sem.at[i]))
        copies[-1].start()
    first.wait()
    for (k, p), copy in zip(todo, copies):
        copy.wait()
        out = full if k else outs[0]
        out[:, p * PIECE : (p + 1) * PIECE] = jnp.dot(
            coef_ref[...], tile_ref[:, chunk_piece(k, width, p)], preferred_element_type=F32
        )
        if k and p == per - 1:
            q, tail = code(full[...])
            outs[k][:, :width] = q
            outs[k][:, width:] = tail


def phi_call(coefs, tiles, width):
    aux, points = tiles.shape
    count = points // width
    return pl.pallas_call(
        functools.partial(phi_kernel, width),
        in_specs=[pl.BlockSpec(memory_space=pltpu.HBM)] * 2,
        out_specs=[VMEM] * (count + 1),
        out_shape=[jax.ShapeDtypeStruct((NDENS, width), F32)]
        + [jax.ShapeDtypeStruct((NDENS, width + 128), jnp.int16)] * (count - 1)
        + [jax.ShapeDtypeStruct(tiles.shape, tiles.dtype)],
        scratch_shapes=[
            pltpu.VMEM((NDENS, width), F32),
            pltpu.VMEM(coefs.shape, coefs.dtype),
            pltpu.SemaphoreType.DMA((points // PIECE,)),
            pltpu.SemaphoreType.DMA,
        ],
        compiler_params=PARAMS,
        cost_estimate=pl.CostEstimate(
            flops=2 * NDENS * aux * points,
            bytes_accessed=(2 * aux + 4 * NDENS) * points,
            transcendentals=0,
        ),
        name="phi",
    )(*(pltpu.with_memory_space_constraint(a, pltpu.HBM) for a in (coefs, tiles)))


def pack_kernel(centre_ref, radius_ref, nbr_ref, cnt_ref, out_ref, c, r, n, k, sem):
    copies = [
        pltpu.make_async_copy(a, b, sem.at[i])
        for i, (a, b) in enumerate(zip((centre_ref, radius_ref, nbr_ref, cnt_ref), (c, r, n, k)))
    ]
    for copy in copies:
        copy.start()
    for copy in copies:
        copy.wait()
    spheres, slots = n.shape
    out_ref[...] = jnp.zeros_like(out_ref)
    out_ref[0:3, :] = c[...]
    out_ref[3:4, :] = r[...]
    out_ref[4:5, :] = k[...].astype(F32)
    out_ref[8:, :] = n[...].astype(F32)


def pack_call(centres, radii, neighbours, counts):
    spheres, slots = neighbours.shape
    args = (centres, radii.reshape(1, spheres), neighbours, counts.reshape(1, spheres))
    return pl.pallas_call(
        pack_kernel,
        in_specs=[pl.BlockSpec(memory_space=pltpu.HBM)] * 4,
        out_specs=VMEM,
        out_shape=jax.ShapeDtypeStruct((8 + spheres, spheres), F32),
        scratch_shapes=[pltpu.VMEM(a.shape, a.dtype) for a in args]
        + [pltpu.SemaphoreType.DMA((4,))],
        compiler_params=PARAMS,
        name="pack",
    )(*(pltpu.with_memory_space_constraint(a, pltpu.HBM) for a in args))


def pair_build(e, geo, mask, dir_ref, bh):
    lane = lax.broadcasted_iota(jnp.int32, (8, 128), 1)
    sub = lax.broadcasted_iota(jnp.int32, (8, 128), 0)
    own = jnp.broadcast_to(geo[pl.ds(e + 8, 1), :], (8, 128))
    mrow = jnp.broadcast_to(mask[pl.ds(e, 1), :], (8, 128))
    cols = []
    for g, start in ((0, e), (1, e + 9)):
        near = geo[pl.ds(start, 8), :]
        valid = jnp.sum(jnp.where(lane == sub + 8 * g, mrow, 0.0), axis=1, keepdims=True)
        on = valid > 0.0
        ir = 1.0 / jnp.where(on, near[:, 3:4], 1.0)
        off = jnp.where(on, own - near, 0.0)
        c = [off[:, 0:1] * ir, off[:, 1:2] * ir, off[:, 2:3] * ir, own[:, 3:4] * ir, valid]
        cols.append([jnp.broadcast_to(q, (8, 128)) for q in c])
    mid = [jnp.where(lane < 64, a, b) for a, b in zip(*cols)]
    sums = []
    for t in range(5):
        ox, oy, oz, q, valid = cols[0] if t < 2 else (mid if t == 2 else cols[1])
        ls = slice(128 * t, 128 * t + 128)
        x = ox + q * dir_ref[0:1, ls]
        y = oy + q * dir_ref[1:2, ls]
        z = oz + q * dir_ref[2:3, ls]
        r2 = x * x + y * y + z * z
        ramp = jnp.clip((1.0 - jnp.sqrt(r2)) * (1.0 / BAND), 0.0, 1.0)
        chi = ramp * ramp * (3.0 - 2.0 * ramp) * valid
        sums.append(jnp.sum(chi, axis=0, keepdims=True))
        cos, sin = [chi, chi * x], [None, chi * y]
        for m in range(2, DEGREE + 1):
            cos.append(cos[m - 1] * x - sin[m - 1] * y)
            sin.append(cos[m - 1] * y + sin[m - 1] * x)
        out = [None] * LM
        for m in range(DEGREE + 1):
            qm = {}
            for l in range(m, DEGREE + 1):
                if l == m + 1:
                    qm[l] = z
                elif l == m + 2:
                    qm[l] = z * z - gam(l, m) * r2
                elif l > m + 2:
                    qm[l] = z * qm[l - 1] - (gam(l, m) * r2) * qm[l - 2]
                for sign, trig in ((1, cos[m]), (-1, sin[m])):
                    if m == 0 and sign < 0:
                        continue
                    out[l * l + l + sign * m] = trig if l == m else trig * qm[l]
        out.append(jnp.zeros((8, 128), F32))
        for p in range(25):
            both = jnp.concatenate([out[2 * p], out[2 * p + 1]], axis=0)
            bh[16 * p : 16 * p + 16, ls] = both.astype(BF)
    return sums


def pair_finish(e, w_ref, t_ref, bh):
    r = jnp.dot(bh[...], w_ref[...], preferred_element_type=F32)
    tt = r[: LM * 8, : 2 * LP] + r[: LM * 8, 2 * LP :]
    a = jnp.swapaxes(tt.reshape(LM, 8, 2 * LP), 0, 1)
    a = jnp.concatenate([a, jnp.zeros((8, LP - LM, 2 * LP), F32)], 1).reshape(8 * LP, 2 * LP)
    hi, lo = halves(a)
    t_ref[e, :, : 2 * LP] = hi
    t_ref[e, :, 2 * LP :] = lo


def uncover(sums):
    low = lax.broadcasted_iota(jnp.int32, (1, 128), 1) < 64
    swap = lambda v: pltpu.roll(v, 64, 1)
    three = []
    for s in sums:
        r2, r3, r4 = swap(s[2]), swap(s[3]), swap(s[4])
        three.append([s[0] + jnp.where(low, r2, r3), s[1] + jnp.where(low, r3, r4), s[2] + r4])
    a, b = three
    b0, b1, b2 = swap(b[0]), swap(b[1]), swap(b[2])
    tiles = [a[0], a[1], jnp.where(low, a[2], b0), jnp.where(low, b0, b1), jnp.where(low, b1, b2)]
    return [jnp.maximum(0.0, 1.0 - t) for t in tiles]


def pair_setup(before_ref, own_ref, after_ref, geo, mask):
    spheres = own_ref.shape[1]
    slots = 2 * REACH
    wide = spheres + 2 * REACH
    packs = (before_ref, own_ref, after_ref)
    rows = jnp.concatenate([p[0:8, :] for p in packs], axis=1)
    rows = jnp.concatenate([rows, jnp.zeros((8, 128 - rows.shape[1]), F32)], axis=1)
    rows = jnp.concatenate([rows, jnp.zeros((120, 128), F32)], axis=0)
    geo[...] = rows.T[: geo.shape[0]]
    first = (lax.axis_index("sph") * lax.axis_size("fit") + lax.axis_index("fit")) * spheres
    row = lax.broadcasted_iota(jnp.int32, (wide, slots), 0) + (first - REACH)
    slot = lax.broadcasted_iota(jnp.int32, (wide, slots), 1)
    lists = [before_ref[8 + spheres - REACH :, :], own_ref[8:, :], after_ref[8 : 8 + REACH, :]]
    rel = jnp.concatenate(lists, axis=0) - row.astype(F32)
    listed = slot.astype(F32) < geo[spheres - REACH : 2 * spheres + REACH, 4:5]
    lane = lax.broadcasted_iota(jnp.int32, (wide, 128), 1)
    found = jnp.zeros((wide, 128), F32)
    for c in range(slots):
        gap = c - REACH if c < REACH else c - REACH + 1
        hit = jnp.where(listed & (rel == float(gap)), 1.0, 0.0)
        hit = jnp.max(hit, axis=1, keepdims=True)
        found = jnp.where(lane == c, hit, found)
    mask[...] = found


def pair_work(quads, geo, mask, dir_ref, w_ref, t_ref, unc_ref, bhs):
    for b, quad in enumerate(quads):
        sums = []
        for u in range(QUAD):
            sums.append(pair_build(quad * QUAD + u, geo, mask, dir_ref, bhs[u]))
            pair_finish(b * QUAD + u, w_ref, t_ref, bhs[u])
        if unc_ref is not None:
            tiles = uncover(sums[:2]) + uncover(sums[2:])
            for t, v in enumerate(tiles):
                unc_ref[b, :, 128 * t : 128 * t + 128] = v


def first_pair_kernel(
    quads, before_ref, own_ref, after_ref, dir_ref, w_ref, t_ref, unc_ref, geo, mask, *bhs
):
    pair_setup(before_ref, own_ref, after_ref, geo, mask)
    pair_work(quads, geo, mask, dir_ref, w_ref, t_ref, unc_ref, bhs)


def next_pair_kernel(quads, geo, mask, dir_ref, w_ref, t_ref, *bhs):
    pair_work(quads, geo, mask, dir_ref, w_ref, t_ref, None, bhs)


def pair_call(quads, consts, packs=None, known=None):
    count = len(quads)
    out_shape = [jax.ShapeDtypeStruct((count * QUAD, 8 * LP, 4 * LP), BF)]
    if known is None:
        kernel, args = first_pair_kernel, packs
        spheres = packs[1].shape[1]
        out_shape += [
            jax.ShapeDtypeStruct((count, 1, QN), F32),
            jax.ShapeDtypeStruct((3 * spheres, 128), F32),
            jax.ShapeDtypeStruct((spheres + 2 * REACH, 128), F32),
        ]
    else:
        kernel, args = next_pair_kernel, known
    return pl.pallas_call(
        functools.partial(kernel, quads),
        in_specs=[VMEM] * (len(args) + 2),
        out_specs=[VMEM] * len(out_shape),
        scratch_shapes=[pltpu.VMEM((400, 2 * NG), BF)] * QUAD,
        out_shape=out_shape,
        compiler_params=PARAMS,
        cost_estimate=pl.CostEstimate(
            flops=count * QUAD * 2 * 400 * 640 * 256,
            bytes_accessed=count * QUAD * 262144,
            transcendentals=0,
        ),
        name="pairs",
    )(*args, *consts)


def own_uncovered(unc_ref, b):
    b = b + SOONER * QUAD // 2
    return unc_ref[b // 2, :, b % 2 * PN : (b % 2 + 1) * PN]


def rhs_kernel(count, *refs):
    phis, (unc_ref, w_ref, out_ref) = refs[:count], refs[count:]
    pairs = out_ref.shape[1] // (2 * LP)
    rows = []
    for b in range(pairs):
        ls = slice(b * PN, (b + 1) * PN)
        total = phis[0][:, ls]
        for p in phis[1:]:
            total = total + decode(p, ls)
        rows.append(total * own_uncovered(unc_ref, b))
    hi, lo = halves(jnp.concatenate(rows, 0))
    n = pairs * NDENS
    r = jnp.dot(jnp.concatenate([hi, lo], 0), w_ref[...], preferred_element_type=F32)
    out = r[:n, : 2 * LP] + r[:n, 2 * LP :] + r[n:, : 2 * LP]
    out = out * (-4.0 * math.pi / NG)
    for b in range(pairs):
        out_ref[:, b * 2 * LP : (b + 1) * 2 * LP] = out[b * NDENS : (b + 1) * NDENS]


def rhs_call(phis, unc, w):
    spheres = phis[0].shape[1] // NG
    return pl.pallas_call(
        functools.partial(rhs_kernel, len(phis)),
        in_specs=[VMEM] * (len(phis) + 2),
        out_specs=VMEM,
        compiler_params=PARAMS,
        out_shape=jax.ShapeDtypeStruct((NDENS, spheres * LP), F32),
        cost_estimate=pl.CostEstimate(
            flops=6 * NDENS * spheres * NG * 256, bytes_accessed=1700000, transcendentals=0
        ),
        name="rhs",
    )(*phis, unc, w)


def gather_field(t_refs, shift, x, xs, e):
    low = lax.broadcasted_iota(jnp.int32, (NDENS, 128), 1) < LP
    parts = []
    for odd in (0, 1):
        below, above = (x, xs) if odd == 0 else (xs, x)
        lo_at = e * LP
        up_at = (e + 8) * LP if odd == 0 else (e + 10) * LP
        lhs = jnp.concatenate(
            [below[:, lo_at : lo_at + 8 * LP], above[:, up_at : up_at + 8 * LP]], 0
        )
        lowest, most = REACH - SOONER * QUAD, t_refs[0].shape[0]
        at = e + odd + shift - lowest
        if 0 <= at < most:
            t = t_refs[0][at]
        else:
            t = t_refs[1][at + lowest - (most if at > 0 else 0)]
        r = jnp.dot(lhs, t, preferred_element_type=F32)
        n = NDENS
        a = r[0:n, : 2 * LP] + r[n : 2 * n, : 2 * LP] + r[0:n, 2 * LP :]
        b = r[2 * n : 3 * n, : 2 * LP] + r[3 * n :, : 2 * LP] + r[2 * n : 3 * n, 2 * LP :]
        parts.append((a, b))
    (a0, b0), (a1, b1) = parts
    return jnp.where(low, a0, b1) + pltpu.roll(jnp.where(low, a1, b0), LP, 1)


def put_scaled(x, at, value):
    hi, lo = halves(value)
    x[0:NDENS, at : at + 128] = hi
    x[NDENS:, at : at + 128] = lo


def put_shifted(xs, x):
    v = x[...].astype(F32)
    xs[...] = jnp.concatenate([v[:, LP:], v[:, :LP]], 1).astype(BF)


def sweep_kernel(
    before_ref, own_ref, after_ref, t_ref, rest_ref, sc_ref, unc_ref, out_ref, x, xs, z, zs
):
    own = own_ref.shape[1]
    spheres = own // LP
    right = lambda at: (before_ref, own_ref, after_ref)[at // own][:, at % own : at % own + 128]
    for at in range(0, 3 * own, 128):
        put_scaled(x, at, right(at) * sc_ref[0:1, :])
    put_shifted(xs, x)
    for e in range(0, spheres + 2 * REACH, 2):
        new = right((e + spheres - REACH) * LP) + gather_field((t_ref, rest_ref), 0, x, xs, e)
        put_scaled(z, e * LP, new * sc_ref[0:1, :])
    put_shifted(zs, z)
    for e in range(0, spheres, 2):
        new = own_ref[:, e * LP : e * LP + 128] + gather_field((t_ref, rest_ref), REACH, z, zs, e)
        new = new * sc_ref[1:2, :]
        out_ref[:, e * LP : e * LP + 128] = new
    out_ref[:, own:] = jnp.zeros((NDENS, 384), F32)
    pairs = spheres // 2
    for b in range(pairs):
        part = own_uncovered(unc_ref, b)
        out_ref[b : b + 1, own:] = part[:, :384]
        out_ref[pairs + b : pairs + b + 1, own : own + 256] = part[:, 384:]


def sweep_call(before, own, after, t, rest, scales, unc):
    lanes = own.shape[1]
    spheres = lanes // LP
    return pl.pallas_call(
        sweep_kernel,
        in_specs=[VMEM] * 7,
        out_specs=VMEM,
        out_shape=jax.ShapeDtypeStruct((NDENS, lanes + 384), F32),
        scratch_shapes=[pltpu.VMEM((2 * NDENS, 3 * lanes), BF)] * 2
        + [pltpu.VMEM((2 * NDENS, lanes + 2 * REACH * LP), BF)] * 2,
        compiler_params=PARAMS,
        cost_estimate=pl.CostEstimate(
            flops=3 * spheres * 2 * 64 * 512 * 256,
            bytes_accessed=2 * spheres * 262144,
            transcendentals=0,
        ),
        name="sweeps",
    )(before, own, after, t, rest, scales, unc)


def moment_kernel(pay_ref, m_ref):
    for e in range(0, m_ref.shape[0], 2):
        both = pay_ref[:, e * LP : e * LP + 128]
        m_ref[e] = both[:, :LM]
        m_ref[e + 1] = pltpu.roll(both, LP, 1)[:, :LM]


def moment_call(pay, spheres):
    return pl.pallas_call(
        moment_kernel,
        in_specs=[VMEM],
        out_specs=VMEM,
        out_shape=jax.ShapeDtypeStruct((spheres, NDENS, LM), F32),
        compiler_params=PARAMS,
        cost_estimate=pl.CostEstimate(flops=0, bytes_accessed=200000, transcendentals=0),
        name="moments",
    )(pay)


def fock_kernel(k, pay_ref, y_ref, tile_ref, *rest):
    out_ref, charge = rest[-2:]
    own = pay_ref.shape[1] - 384
    pairs = own // (2 * LP)
    width = pairs * PN
    rows = [pay_ref[:, b * 2 * LP : (b + 1) * 2 * LP] for b in range(pairs)]
    hi, lo = halves(jnp.concatenate(rows, 0))
    r = jnp.dot(jnp.concatenate([hi, lo], 1), y_ref[...], preferred_element_type=F32)
    out = r[:, :PN] + r[:, PN:]
    for b in range(pairs):
        unc = jnp.concatenate(
            [pay_ref[b : b + 1, own:], pay_ref[pairs + b : pairs + b + 1, own : own + 256]], 1
        )
        weight = unc * (4.0 * math.pi / NG)
        charge[:, b * PN : (b + 1) * PN] = (out[b * NDENS : (b + 1) * NDENS] * weight).astype(BF)
    total = rest[0][...] if len(rest) == 3 else None
    for p in range(width // PIECE):
        part = lax.dot_general(
            charge[:, p * PIECE : (p + 1) * PIECE],
            tile_ref[:, chunk_piece(k, width, p)],
            (((1,), (1,)), ((), ())),
            preferred_element_type=F32,
        )
        total = part if total is None else total + part
    out_ref[...] = total


def fock_call(k, pay, wt, tiles, width, before=None):
    aux = tiles.shape[0]
    more = [] if before is None else [before]
    return pl.pallas_call(
        functools.partial(fock_kernel, k),
        in_specs=[VMEM] * (3 + len(more)),
        out_specs=VMEM,
        out_shape=jax.ShapeDtypeStruct((NDENS, aux), F32),
        scratch_shapes=[pltpu.VMEM((NDENS, width), BF)],
        compiler_params=PARAMS,
        cost_estimate=pl.CostEstimate(
            flops=2 * NDENS * aux * width, bytes_accessed=2 * aux * width, transcendentals=0
        ),
        name="fock",
    )(pay, wt, tiles, *more)


def trade(x, axis, k):
    count = lax.axis_size(axis)
    return lax.ppermute(x, axis, [(i, i ^ k) for i in range(count)])


def shift(x, axis, k):
    count = lax.axis_size(axis)
    return lax.ppermute(x, axis, [(i, (i + k) % count) for i in range(count)])


def from_beside(x):
    axes = ("sph", "fit")
    count = lax.axis_size("sph") * lax.axis_size("fit")
    up = [(i, (i + 1) % count) for i in range(count)]
    down = [((i + 1) % count, i) for i in range(count)]
    return lax.ppermute(x, axes, up), lax.ppermute(x, axes, down)


def body(tiles, coefs, centres, radii, neighbours, counts):
    spheres, slots = neighbours.shape
    fits = lax.axis_size("fit")
    sphs = lax.axis_size("sph")
    assert fits & (fits - 1) == 0 and sphs & (sphs - 1) == 0
    assert spheres % (2 * QUAD) == 0 and spheres == slots == 2 * REACH
    w, wt = (jnp.asarray(a) for a in even_weights())
    scales = jnp.asarray(lane_scales())

    width = spheres * NG
    own = pack_call(centres, radii, neighbours, counts)
    before, after = from_beside(own)
    *phis, near_tiles = phi_call(coefs, tiles, width)
    phis, before, after = lax.optimization_barrier((phis, before, after))
    got = [trade(phis[k], "fit", k) for k in range(1, fits)]
    below_own, last_own = REACH // QUAD, (REACH + spheres) // QUAD
    soon = [*range(below_own - SOONER, last_own)]
    later = [*range(below_own - SOONER), *range(last_own, last_own + below_own)]
    pw, dirs = pair_weights()
    consts = (jnp.asarray(dirs), jnp.asarray(pw))
    t, unc, geo, mask = pair_call(soon, consts, packs=(before, own, after))
    rhs = rhs_call([phis[0], *got], unc, w)
    below, above = from_beside(rhs)
    mask, _ = lax.optimization_barrier((mask, rhs))
    (rest,) = pair_call(later, consts, known=(geo, mask))
    pay = sweep_call(below, rhs, above, t, rest, scales, unc)
    others = [trade(pay, "fit", k) for k in range(1, fits)]
    fock = fock_call(0, pay, wt, near_tiles, width)
    for k in range(1, fits):
        fock = fock_call(k, others[k - 1], wt, near_tiles, width, fock)
    fock = fock + trade(fock, "sph", 1)
    held, _ = lax.optimization_barrier((pay, fock))
    moments = moment_call(held, spheres)
    bit = 2
    while bit < sphs:
        ks = [k for k in (bit, 2 * bit, 3 * bit) if k < sphs]
        if 4 * bit == sphs:
            parts = [shift(fock, "sph", k) for k in ks]
        else:
            parts = [trade(fock, "sph", k) for k in ks]
        fock = functools.reduce(jnp.add, parts, fock)
        bit *= 4
    return moments, fock


def solution(mesh):
    placed = (
        P("fit", "sph"),
        P(None, "fit"),
        P(None, ("sph", "fit")),
        P(("sph", "fit")),
        P(("sph", "fit"), None),
        P(("sph", "fit")),
    )
    return jax.shard_map(
        body,
        mesh=mesh,
        in_specs=placed,
        out_specs=(P(("sph", "fit"), None, None), P(None, "fit")),
        check_vma=False,
    )
```

```python
import functools
import math

import jax
import jax.numpy as jnp
import ml_dtypes
import numpy as np
from jax import lax
from jax.experimental import pallas as pl
from jax.experimental.pallas import tpu as pltpu
from jax.sharding import PartitionSpec as P

DEGREE = 6
LM = 49
NTH = 16
NPHI = 20
NG = 320
NDENS = 16
LP = 64
QUAD = 4
QN = QUAD * NG
PN = 2 * NG
PIECE = 2560
PARAMS = pltpu.CompilerParams(vmem_limit_bytes=16 << 20)
VMEM = pl.BlockSpec(memory_space=pltpu.VMEM)
SMEM = pl.BlockSpec(memory_space=pltpu.SMEM)
BAND = 0.1
REACH = 8
SOONER = 1
BF = jnp.bfloat16
F32 = jnp.float32


def gam(l, m):
    return (l + m - 1) * (l - 1 - m) / ((2 * l - 1) * (2 * l - 3))


def tables():
    c = -1.0 + (2.0 * np.arange(NTH) + 1.0) / NTH
    f = (np.arange(NPHI) + 0.5) * (2 * np.pi / NPHI)
    z = np.repeat(c, NPHI)
    s = np.sqrt(1 - z * z)
    az = np.tile(f, NTH)
    x, y = s * np.cos(az), s * np.sin(az)
    cos, sin = [np.ones_like(x)], [np.zeros_like(x)]
    for m in range(1, DEGREE + 1):
        cos.append(cos[m - 1] * x - sin[m - 1] * y)
        sin.append(cos[m - 1] * y + sin[m - 1] * x)
    ys, scale, invert = np.zeros((LM, NG)), np.zeros(LM), np.zeros(LM)
    for m in range(DEGREE + 1):
        q, lead = {m: np.ones_like(x)}, {m: 1.0}
        for odd in range(1, 2 * m, 2):
            lead[m] *= odd
        for l in range(m + 1, DEGREE + 1):
            q[l] = z * q[l - 1] - (gam(l, m) * q[l - 2] if l > m + 1 else 0.0)
            lead[l] = lead[l - 1] * (2 * l - 1) / (l - m)
        for l in range(m, DEGREE + 1):
            n = math.sqrt(
                (2 * l + 1) / (4 * math.pi) * math.factorial(l - m) / math.factorial(l + m)
            )
            n *= math.sqrt(2.0) if m else 1.0
            for sign, trig in ((1, cos[m]), (-1, sin[m])):
                if m == 0 and sign < 0:
                    continue
                i = l * l + l + sign * m
                ys[i] = n * lead[l] * q[l] * trig
                scale[i] = n * lead[l] * 4 * math.pi / (2 * l + 1)
                invert[i] = (2 * l + 1) / (4 * math.pi)
    return np.stack([x, y, z]), ys, scale, invert


def split(a):
    a = np.asarray(a, np.float32)
    hi = a.astype(ml_dtypes.bfloat16)
    return hi, (a - hi.astype(np.float32)).astype(ml_dtypes.bfloat16)


def halves(x):
    hi = x.astype(BF)
    return hi, (x - hi.astype(F32)).astype(BF)


def pair_weights():
    dirs, ys, _, _ = tables()
    w = np.zeros((2 * NG, 2 * LP))
    wy = ys.T * (4 * math.pi / NG)
    w[:NG, :LM] = wy
    w[NG:, LP : LP + LM] = wy
    d = np.zeros((8, 2 * NG), np.float32)
    d[:3, :NG] = dirs
    d[:3, NG:] = dirs
    return np.concatenate(split(w), 1), d


def even_weights():
    _, ys, _, _ = tables()
    w = np.zeros((PN, 2 * LP))
    w[:NG, :LM] = ys.T
    w[NG:, LP : LP + LM] = ys.T
    hi, lo = split(w.T)
    deep = np.block([[hi, lo], [hi, np.zeros_like(lo)]])
    return np.concatenate(split(w), 1), deep


def lane_scales():
    _, _, scale, invert = tables()
    rows = np.zeros((8, 2 * LP), np.float32)
    for h in (0, LP):
        rows[0, h : h + LM] = scale * invert
        rows[1, h : h + LM] = invert
    return rows


def chunk_piece(k, width, p):
    at = (lax.axis_index("fit") ^ k) * width + p * PIECE
    return pl.ds(pl.multiple_of(at, 128), PIECE)


def code(x):
    top = jnp.maximum(jnp.max(jnp.abs(x), axis=1, keepdims=True), 1e-30)
    power = jnp.floor(jnp.log2(top)) - 13.0
    q = jnp.floor(x * jnp.exp2(-power) + 0.5).astype(jnp.int32)
    tail = jnp.broadcast_to(power, (x.shape[0], 128)).astype(jnp.int32)
    return q.astype(jnp.int16), tail.astype(jnp.int16)


def decode(ref, ls):
    width = ref.shape[1] - 128
    power = ref[:, width:].astype(jnp.int32).astype(F32)[:, 0:1]
    return ref[:, ls].astype(jnp.int32).astype(F32) * jnp.exp2(power)


def pack(c, r, n, k, out_ref):
    out_ref[...] = jnp.zeros_like(out_ref)
    out_ref[0:3, :] = c[...]
    out_ref[3:4, :] = r[...]
    out_ref[4:5, :] = k[...].astype(F32)
    out_ref[8:, :] = n[...].astype(F32)


def phi_kernel(width, far_coef_ref, far_ref, *rest):
    geometry, outs = rest[:4], rest[4:-11]
    tile_ref, pack_ref, full, coef_ref, sem, coef_sem, *held = rest[-11:]
    small = [
        pltpu.make_async_copy(a, b, held[4].at[i]) for i, (a, b) in enumerate(zip(geometry, held))
    ]
    for copy in small:
        copy.start()
    first = pltpu.make_async_copy(far_coef_ref, coef_ref, coef_sem)
    first.start()
    per = width // PIECE
    todo = [(k, p) for k in [*range(1, len(outs)), 0] for p in range(per)]
    copies = []
    for i, (k, p) in enumerate(todo):
        at = chunk_piece(k, width, p)
        copies.append(pltpu.make_async_copy(far_ref.at[:, at], tile_ref.at[:, at], sem.at[i]))
        copies[-1].start()
    for copy in small:
        copy.wait()
    pack(*held[:4], pack_ref)
    first.wait()
    for (k, p), copy in zip(todo, copies):
        copy.wait()
        out = full if k else outs[0]
        out[:, p * PIECE : (p + 1) * PIECE] = jnp.dot(
            coef_ref[...], tile_ref[:, chunk_piece(k, width, p)], preferred_element_type=F32
        )
        if k and p == per - 1:
            q, tail = code(full[...])
            outs[k][:, :width] = q
            outs[k][:, width:] = tail


def phi_call(coefs, tiles, geometry, width):
    aux, points = tiles.shape
    count = points // width
    spheres = geometry[0].shape[1]
    return pl.pallas_call(
        functools.partial(phi_kernel, width),
        in_specs=[pl.BlockSpec(memory_space=pltpu.HBM)] * 6,
        out_specs=[VMEM] * (count + 2),
        out_shape=[jax.ShapeDtypeStruct((NDENS, width), F32)]
        + [jax.ShapeDtypeStruct((NDENS, width + 128), jnp.int16)] * (count - 1)
        + [
            jax.ShapeDtypeStruct(tiles.shape, tiles.dtype),
            jax.ShapeDtypeStruct((8 + spheres, spheres), F32),
        ],
        scratch_shapes=[
            pltpu.VMEM((NDENS, width), F32),
            pltpu.VMEM(coefs.shape, coefs.dtype),
            pltpu.SemaphoreType.DMA((points // PIECE,)),
            pltpu.SemaphoreType.DMA,
        ]
        + [pltpu.VMEM(a.shape, a.dtype) for a in geometry]
        + [pltpu.SemaphoreType.DMA((4,))],
        compiler_params=PARAMS,
        cost_estimate=pl.CostEstimate(
            flops=2 * NDENS * aux * points,
            bytes_accessed=(2 * aux + 4 * NDENS) * points,
            transcendentals=0,
        ),
        name="phi",
    )(*(pltpu.with_memory_space_constraint(a, pltpu.HBM) for a in (coefs, tiles, *geometry)))


def pair_build(e, geo, mask, dir_ref, bh):
    lane = lax.broadcasted_iota(jnp.int32, (8, 128), 1)
    sub = lax.broadcasted_iota(jnp.int32, (8, 128), 0)
    own = jnp.broadcast_to(geo[pl.ds(e + 8, 1), :], (8, 128))
    mrow = jnp.broadcast_to(mask[pl.ds(e, 1), :], (8, 128))
    cols = []
    for g, start in ((0, e), (1, e + 9)):
        near = geo[pl.ds(start, 8), :]
        valid = jnp.sum(jnp.where(lane == sub + 8 * g, mrow, 0.0), axis=1, keepdims=True)
        on = valid > 0.0
        ir = 1.0 / jnp.where(on, near[:, 3:4], 1.0)
        off = jnp.where(on, own - near, 0.0)
        c = [off[:, 0:1] * ir, off[:, 1:2] * ir, off[:, 2:3] * ir, own[:, 3:4] * ir, valid]
        cols.append([jnp.broadcast_to(q, (8, 128)) for q in c])
    mid = [jnp.where(lane < 64, a, b) for a, b in zip(*cols)]
    sums = []
    for t in range(5):
        ox, oy, oz, q, valid = cols[0] if t < 2 else (mid if t == 2 else cols[1])
        ls = slice(128 * t, 128 * t + 128)
        x = ox + q * dir_ref[0:1, ls]
        y = oy + q * dir_ref[1:2, ls]
        z = oz + q * dir_ref[2:3, ls]
        r2 = x * x + y * y + z * z
        ramp = jnp.clip((1.0 - jnp.sqrt(r2)) * (1.0 / BAND), 0.0, 1.0)
        chi = ramp * ramp * (3.0 - 2.0 * ramp) * valid
        sums.append(jnp.sum(chi, axis=0, keepdims=True))
        cos, sin = [chi, chi * x], [None, chi * y]
        for m in range(2, DEGREE + 1):
            cos.append(cos[m - 1] * x - sin[m - 1] * y)
            sin.append(cos[m - 1] * y + sin[m - 1] * x)
        out = [None] * LM
        for m in range(DEGREE + 1):
            qm = {}
            for l in range(m, DEGREE + 1):
                if l == m + 1:
                    qm[l] = z
                elif l == m + 2:
                    qm[l] = z * z - gam(l, m) * r2
                elif l > m + 2:
                    qm[l] = z * qm[l - 1] - (gam(l, m) * r2) * qm[l - 2]
                for sign, trig in ((1, cos[m]), (-1, sin[m])):
                    if m == 0 and sign < 0:
                        continue
                    out[l * l + l + sign * m] = trig if l == m else trig * qm[l]
        out.append(jnp.zeros((8, 128), F32))
        for p in range(25):
            both = jnp.concatenate([out[2 * p], out[2 * p + 1]], axis=0)
            bh[16 * p : 16 * p + 16, ls] = both.astype(BF)
    return sums


def pair_finish(e, w_ref, t_ref, bh):
    r = jnp.dot(bh[...], w_ref[...], preferred_element_type=F32)
    tt = r[: LM * 8, : 2 * LP] + r[: LM * 8, 2 * LP :]
    a = jnp.swapaxes(tt.reshape(LM, 8, 2 * LP), 0, 1)
    a = jnp.concatenate([a, jnp.zeros((8, LP - LM, 2 * LP), F32)], 1).reshape(8 * LP, 2 * LP)
    hi, lo = halves(a)
    t_ref[e, :, : 2 * LP] = hi
    t_ref[e, :, 2 * LP :] = lo


def uncover(sums):
    low = lax.broadcasted_iota(jnp.int32, (1, 128), 1) < 64
    swap = lambda v: pltpu.roll(v, 64, 1)
    three = []
    for s in sums:
        r2, r3, r4 = swap(s[2]), swap(s[3]), swap(s[4])
        three.append([s[0] + jnp.where(low, r2, r3), s[1] + jnp.where(low, r3, r4), s[2] + r4])
    a, b = three
    b0, b1, b2 = swap(b[0]), swap(b[1]), swap(b[2])
    tiles = [a[0], a[1], jnp.where(low, a[2], b0), jnp.where(low, b0, b1), jnp.where(low, b1, b2)]
    return [jnp.maximum(0.0, 1.0 - t) for t in tiles]


def pair_setup(before_ref, own_ref, after_ref, geo, mask):
    spheres = own_ref.shape[1]
    slots = 2 * REACH
    wide = spheres + 2 * REACH
    packs = (before_ref, own_ref, after_ref)
    rows = jnp.concatenate([p[0:8, :] for p in packs], axis=1)
    rows = jnp.concatenate([rows, jnp.zeros((8, 128 - rows.shape[1]), F32)], axis=1)
    rows = jnp.concatenate([rows, jnp.zeros((120, 128), F32)], axis=0)
    geo[...] = rows.T[: geo.shape[0]]
    first = (lax.axis_index("sph") * lax.axis_size("fit") + lax.axis_index("fit")) * spheres
    row = lax.broadcasted_iota(jnp.int32, (wide, slots), 0) + (first - REACH)
    slot = lax.broadcasted_iota(jnp.int32, (wide, slots), 1)
    lists = [before_ref[8 + spheres - REACH :, :], own_ref[8:, :], after_ref[8 : 8 + REACH, :]]
    rel = jnp.concatenate(lists, axis=0) - row.astype(F32)
    listed = slot.astype(F32) < geo[spheres - REACH : 2 * spheres + REACH, 4:5]
    lane = lax.broadcasted_iota(jnp.int32, (wide, 128), 1)
    found = jnp.zeros((wide, 128), F32)
    for c in range(slots):
        gap = c - REACH if c < REACH else c - REACH + 1
        hit = jnp.where(listed & (rel == float(gap)), 1.0, 0.0)
        hit = jnp.max(hit, axis=1, keepdims=True)
        found = jnp.where(lane == c, hit, found)
    mask[...] = found


def pair_work(quads, geo, mask, dir_ref, w_ref, t_ref, unc_ref, bhs):
    for b, quad in enumerate(quads):
        sums = []
        for u in range(QUAD):
            sums.append(pair_build(quad * QUAD + u, geo, mask, dir_ref, bhs[u]))
            pair_finish(b * QUAD + u, w_ref, t_ref, bhs[u])
        if unc_ref is not None:
            tiles = uncover(sums[:2]) + uncover(sums[2:])
            for t, v in enumerate(tiles):
                unc_ref[b, :, 128 * t : 128 * t + 128] = v


def first_pair_kernel(
    quads, before_ref, own_ref, after_ref, dir_ref, w_ref, t_ref, unc_ref, geo, mask, *bhs
):
    pair_setup(before_ref, own_ref, after_ref, geo, mask)
    pair_work(quads, geo, mask, dir_ref, w_ref, t_ref, unc_ref, bhs)


def next_pair_kernel(quads, geo, mask, dir_ref, w_ref, t_ref, *bhs):
    pair_work(quads, geo, mask, dir_ref, w_ref, t_ref, None, bhs)


def pair_call(quads, consts, packs=None, known=None):
    count = len(quads)
    out_shape = [jax.ShapeDtypeStruct((count * QUAD, 8 * LP, 4 * LP), BF)]
    if known is None:
        kernel, args = first_pair_kernel, packs
        spheres = packs[1].shape[1]
        out_shape += [
            jax.ShapeDtypeStruct((count, 1, QN), F32),
            jax.ShapeDtypeStruct((3 * spheres, 128), F32),
            jax.ShapeDtypeStruct((spheres + 2 * REACH, 128), F32),
        ]
    else:
        kernel, args = next_pair_kernel, known
    return pl.pallas_call(
        functools.partial(kernel, quads),
        in_specs=[VMEM] * (len(args) + 2),
        out_specs=[VMEM] * len(out_shape),
        scratch_shapes=[pltpu.VMEM((400, 2 * NG), BF)] * QUAD,
        out_shape=out_shape,
        compiler_params=PARAMS,
        cost_estimate=pl.CostEstimate(
            flops=count * QUAD * 2 * 400 * 640 * 256,
            bytes_accessed=count * QUAD * 262144,
            transcendentals=0,
        ),
        name="pairs",
    )(*args, *consts)


def own_uncovered(unc_ref, b):
    b = b + SOONER * QUAD // 2
    return unc_ref[b // 2, :, b % 2 * PN : (b % 2 + 1) * PN]


def rhs_kernel(count, *refs):
    phis, (unc_ref, w_ref, out_ref) = refs[:count], refs[count:]
    pairs = out_ref.shape[1] // (2 * LP)
    rows = []
    for b in range(pairs):
        ls = slice(b * PN, (b + 1) * PN)
        total = phis[0][:, ls]
        for p in phis[1:]:
            total = total + decode(p, ls)
        rows.append(total * own_uncovered(unc_ref, b))
    hi, lo = halves(jnp.concatenate(rows, 0))
    n = pairs * NDENS
    r = jnp.dot(jnp.concatenate([hi, lo], 0), w_ref[...], preferred_element_type=F32)
    out = r[:n, : 2 * LP] + r[:n, 2 * LP :] + r[n:, : 2 * LP]
    out = out * (-4.0 * math.pi / NG)
    for b in range(pairs):
        out_ref[:, b * 2 * LP : (b + 1) * 2 * LP] = out[b * NDENS : (b + 1) * NDENS]


def rhs_call(phis, unc, w):
    spheres = phis[0].shape[1] // NG
    return pl.pallas_call(
        functools.partial(rhs_kernel, len(phis)),
        in_specs=[VMEM] * (len(phis) + 2),
        out_specs=VMEM,
        compiler_params=PARAMS,
        out_shape=jax.ShapeDtypeStruct((NDENS, spheres * LP), F32),
        cost_estimate=pl.CostEstimate(
            flops=6 * NDENS * spheres * NG * 256, bytes_accessed=1700000, transcendentals=0
        ),
        name="rhs",
    )(*phis, unc, w)


def gather_field(t_refs, shift, x, xs, e):
    low = lax.broadcasted_iota(jnp.int32, (NDENS, 128), 1) < LP
    parts = []
    for odd in (0, 1):
        below, above = (x, xs) if odd == 0 else (xs, x)
        lo_at = e * LP
        up_at = (e + 8) * LP if odd == 0 else (e + 10) * LP
        lhs = jnp.concatenate(
            [below[:, lo_at : lo_at + 8 * LP], above[:, up_at : up_at + 8 * LP]], 0
        )
        lowest, most = REACH - SOONER * QUAD, t_refs[0].shape[0]
        at = e + odd + shift - lowest
        if 0 <= at < most:
            t = t_refs[0][at]
        else:
            t = t_refs[1][at + lowest - (most if at > 0 else 0)]
        r = jnp.dot(lhs, t, preferred_element_type=F32)
        n = NDENS
        a = r[0:n, : 2 * LP] + r[n : 2 * n, : 2 * LP] + r[0:n, 2 * LP :]
        b = r[2 * n : 3 * n, : 2 * LP] + r[3 * n :, : 2 * LP] + r[2 * n : 3 * n, 2 * LP :]
        parts.append((a, b))
    (a0, b0), (a1, b1) = parts
    return jnp.where(low, a0, b1) + pltpu.roll(jnp.where(low, a1, b0), LP, 1)


def put_scaled(x, at, value):
    hi, lo = halves(value)
    x[0:NDENS, at : at + 128] = hi
    x[NDENS:, at : at + 128] = lo


def put_shifted(xs, x):
    v = x[...].astype(F32)
    xs[...] = jnp.concatenate([v[:, LP:], v[:, :LP]], 1).astype(BF)


def sweep_kernel(
    before_ref, own_ref, after_ref, t_ref, rest_ref, sc_ref, unc_ref, out_ref, x, xs, z, zs
):
    own = own_ref.shape[1]
    spheres = own // LP
    right = lambda at: (before_ref, own_ref, after_ref)[at // own][:, at % own : at % own + 128]
    for at in range(0, 3 * own, 128):
        put_scaled(x, at, right(at) * sc_ref[0:1, :])
    put_shifted(xs, x)
    for e in range(0, spheres + 2 * REACH, 2):
        new = right((e + spheres - REACH) * LP) + gather_field((t_ref, rest_ref), 0, x, xs, e)
        put_scaled(z, e * LP, new * sc_ref[0:1, :])
    put_shifted(zs, z)
    for e in range(0, spheres, 2):
        new = own_ref[:, e * LP : e * LP + 128] + gather_field((t_ref, rest_ref), REACH, z, zs, e)
        new = new * sc_ref[1:2, :]
        out_ref[:, e * LP : e * LP + 128] = new
    out_ref[:, own:] = jnp.zeros((NDENS, 384), F32)
    pairs = spheres // 2
    for b in range(pairs):
        part = own_uncovered(unc_ref, b)
        out_ref[b : b + 1, own:] = part[:, :384]
        out_ref[pairs + b : pairs + b + 1, own : own + 256] = part[:, 384:]


def sweep_call(before, own, after, t, rest, scales, unc):
    lanes = own.shape[1]
    spheres = lanes // LP
    return pl.pallas_call(
        sweep_kernel,
        in_specs=[VMEM] * 7,
        out_specs=VMEM,
        out_shape=jax.ShapeDtypeStruct((NDENS, lanes + 384), F32),
        scratch_shapes=[pltpu.VMEM((2 * NDENS, 3 * lanes), BF)] * 2
        + [pltpu.VMEM((2 * NDENS, lanes + 2 * REACH * LP), BF)] * 2,
        compiler_params=PARAMS,
        cost_estimate=pl.CostEstimate(
            flops=3 * spheres * 2 * 64 * 512 * 256,
            bytes_accessed=2 * spheres * 262144,
            transcendentals=0,
        ),
        name="sweeps",
    )(before, own, after, t, rest, scales, unc)


def moment_kernel(pay_ref, m_ref):
    for e in range(0, m_ref.shape[0], 2):
        both = pay_ref[:, e * LP : e * LP + 128]
        m_ref[e] = both[:, :LM]
        m_ref[e + 1] = pltpu.roll(both, LP, 1)[:, :LM]


def moment_call(pay, spheres):
    return pl.pallas_call(
        moment_kernel,
        in_specs=[VMEM],
        out_specs=VMEM,
        out_shape=jax.ShapeDtypeStruct((spheres, NDENS, LM), F32),
        compiler_params=PARAMS,
        cost_estimate=pl.CostEstimate(flops=0, bytes_accessed=200000, transcendentals=0),
        name="moments",
    )(pay)


def fock_kernel(k, pay_ref, y_ref, tile_ref, *rest):
    out_ref, charge = rest[-2:]
    own = pay_ref.shape[1] - 384
    pairs = own // (2 * LP)
    width = pairs * PN
    rows = [pay_ref[:, b * 2 * LP : (b + 1) * 2 * LP] for b in range(pairs)]
    hi, lo = halves(jnp.concatenate(rows, 0))
    r = jnp.dot(jnp.concatenate([hi, lo], 1), y_ref[...], preferred_element_type=F32)
    out = r[:, :PN] + r[:, PN:]
    for b in range(pairs):
        unc = jnp.concatenate(
            [pay_ref[b : b + 1, own:], pay_ref[pairs + b : pairs + b + 1, own : own + 256]], 1
        )
        weight = unc * (4.0 * math.pi / NG)
        charge[:, b * PN : (b + 1) * PN] = (out[b * NDENS : (b + 1) * NDENS] * weight).astype(BF)
    total = rest[0][...] if len(rest) == 3 else None
    for p in range(width // PIECE):
        part = lax.dot_general(
            charge[:, p * PIECE : (p + 1) * PIECE],
            tile_ref[:, chunk_piece(k, width, p)],
            (((1,), (1,)), ((), ())),
            preferred_element_type=F32,
        )
        total = part if total is None else total + part
    out_ref[...] = total


def fock_call(k, pay, wt, tiles, width, before=None):
    aux = tiles.shape[0]
    more = [] if before is None else [before]
    return pl.pallas_call(
        functools.partial(fock_kernel, k),
        in_specs=[VMEM] * (3 + len(more)),
        out_specs=VMEM,
        out_shape=jax.ShapeDtypeStruct((NDENS, aux), F32),
        scratch_shapes=[pltpu.VMEM((NDENS, width), BF)],
        compiler_params=PARAMS,
        cost_estimate=pl.CostEstimate(
            flops=2 * NDENS * aux * width, bytes_accessed=2 * aux * width, transcendentals=0
        ),
        name="fock",
    )(pay, wt, tiles, *more)


def trade(x, axis, k):
    count = lax.axis_size(axis)
    return lax.ppermute(x, axis, [(i, i ^ k) for i in range(count)])


def shift(x, axis, k):
    count = lax.axis_size(axis)
    return lax.ppermute(x, axis, [(i, (i + k) % count) for i in range(count)])


def from_beside(x):
    axes = ("sph", "fit")
    count = lax.axis_size("sph") * lax.axis_size("fit")
    up = [(i, (i + 1) % count) for i in range(count)]
    down = [((i + 1) % count, i) for i in range(count)]
    return lax.ppermute(x, axes, up), lax.ppermute(x, axes, down)


def body(tiles, coefs, centres, radii, neighbours, counts):
    spheres, slots = neighbours.shape
    fits = lax.axis_size("fit")
    sphs = lax.axis_size("sph")
    assert fits & (fits - 1) == 0 and sphs & (sphs - 1) == 0
    assert spheres % (2 * QUAD) == 0 and spheres == slots == 2 * REACH
    w, wt = (jnp.asarray(a) for a in even_weights())
    scales = jnp.asarray(lane_scales())

    width = spheres * NG
    geometry = (centres, radii.reshape(1, spheres), neighbours, counts.reshape(1, spheres))
    *phis, near_tiles, own = phi_call(coefs, tiles, geometry, width)
    before, after = from_beside(own)
    got = [trade(phis[k], "fit", k) for k in range(1, fits)]
    below_own, last_own = REACH // QUAD, (REACH + spheres) // QUAD
    soon = [*range(below_own - SOONER, last_own)]
    later = [*range(below_own - SOONER), *range(last_own, last_own + below_own)]
    pw, dirs = pair_weights()
    consts = (jnp.asarray(dirs), jnp.asarray(pw))
    t, unc, geo, mask = pair_call(soon, consts, packs=(before, own, after))
    rhs = rhs_call([phis[0], *got], unc, w)
    below, above = from_beside(rhs)
    mask, _ = lax.optimization_barrier((mask, rhs))
    (rest,) = pair_call(later, consts, known=(geo, mask))
    pay = sweep_call(below, rhs, above, t, rest, scales, unc)
    others = [trade(pay, "fit", k) for k in range(1, fits)]
    fock = fock_call(0, pay, wt, near_tiles, width)
    for k in range(1, fits):
        fock = fock_call(k, others[k - 1], wt, near_tiles, width, fock)
    fock = fock + trade(fock, "sph", 1)
    held, _ = lax.optimization_barrier((pay, fock))
    moments = moment_call(held, spheres)
    bit = 2
    while bit < sphs:
        ks = [k for k in (bit, 2 * bit, 3 * bit) if k < sphs]
        if 4 * bit == sphs:
            parts = [shift(fock, "sph", k) for k in ks]
        else:
            parts = [trade(fock, "sph", k) for k in ks]
        fock = functools.reduce(jnp.add, parts, fock)
        bit *= 4
    return moments, fock


def solution(mesh):
    placed = (
        P("fit", "sph"),
        P(None, "fit"),
        P(None, ("sph", "fit")),
        P(("sph", "fit")),
        P(("sph", "fit"), None),
        P(("sph", "fit")),
    )
    return jax.shard_map(
        body,
        mesh=mesh,
        in_specs=placed,
        out_specs=(P(("sph", "fit"), None, None), P(None, "fit")),
        check_vma=False,
    )
```
